256 devices in a mesh: ctx: 32 (over z, x_hi, core), head: 8 (over y, x_lo).
Axes of the slice: x: 4 (x_hi: 2, x_lo: 2; x = x_hi * 2 + x_lo), y: 4, z: 8, core: 2. Of those that a mesh axis runs over, the one named last changes fastest.
Arguments:
- queries: bfloat16 [8192, 8192], P('ctx', 'head'), may hold values from -10 to 10
- key_rows: bfloat16 [8192, 1024], P('ctx', 'head'), may hold values from -4.5 to 4.5
- values: bfloat16 [8192, 1024], P('ctx', 'head'), may hold values from -24 to 24
- lengths: int32 [17], replicated, may hold values from 1 to 4352, as said below
- block_plan: int32 [1024], P('ctx'), may hold values from 0 to 1023, as said below
- inverse: int32 [1024], replicated, may hold values from 0 to 1023, as said below
- mask_lo: int32 [1024], replicated, may hold values from 0 to 1023, as said below
- out_weight: bfloat16 [8192, 4096], P('head'), may hold values from -0.375 to 0.375
Outputs:
- mixed_out: bfloat16 [8192, 4096], P('ctx', 'head')
The draws below stay inside these ranges and needn't reach their ends.
Inputs may be any that keep to these rules, and one draw needn't show every extreme that they name: One document has exactly 4352 tokens, every other is shorter; the lengths sum to 8192. A permutation of the 1024 blocks; slot block_plan[b] lies on index block_plan[b] // 32 of ctx; every index receives exactly 32 blocks, and at most 2 blocks of one index go to any one index, which is reached in every draw. inverse[block_plan[b]] == b. mask_lo[b] lies between the block holding the first token of the document of block b's first token and b, both included.
All inputs are finite; a program needn't handle non-finite values.
Results may differ from the reference program's by a relative error of at most 0.02.
Values may be sent and summed in bfloat16 or wider, within the bound.
A program may use at most 64 MiB of HBM per device.

```python
import jax
import jax.numpy as jnp
from jax import lax

HQ = 64
KVH = 8
HD = 128
D = 4096
BLK = 8
NDOC = 17
TOKENS = 8192
BPD = 32
NBLK = 1024
WIN = 128
CAP = 2
MOST = 4352
N_CTX = 32
N_HEAD = 8


def document_lengths(key):
    base_key = jax.random.fold_in(key, 7)
    length_key, order_key = jax.random.split(base_key)
    pair_count = (NDOC - 1) // 2
    half_pair = (TOKENS - MOST) // (2 * pair_count)
    first_half = jax.random.randint(length_key, (pair_count,), 1, 2 * half_pair, dtype=jnp.int32)
    longest = jnp.full((1,), MOST, jnp.int32)
    all_lengths = jnp.concatenate([longest, first_half, 2 * half_pair - first_half])
    order_perm = jax.random.permutation(order_key, NDOC)
    return all_lengths[order_perm].astype(jnp.int32)


def plan_tables(key):
    base_key = jax.random.fold_in(key, 11)
    shift_key, source_key, target_key = jax.random.split(base_key, 3)
    device_count = N_CTX
    per_device = BPD
    lowest = per_device // device_count
    leftover = per_device % device_count
    loads = [lowest + (1 if index < leftover else 0) for index in range(device_count)]
    if max(loads) < CAP:
        loads[0] = loads[0] + 1
        loads[leftover - 1 if leftover > 0 else device_count - 1] = loads[leftover - 1 if leftover > 0 else device_count - 1] - 1
    load_ranks = []
    for index in range(device_count):
        load_ranks = load_ranks + [index] * loads[index]
    rank_table = jnp.array(load_ranks, dtype=jnp.int32)
    shift_ids = jnp.arange(device_count, dtype=jnp.int32)
    drawn_order = jax.random.permutation(shift_key, device_count).astype(jnp.int32)
    priority = jnp.where(shift_ids == device_count // 2, -3, jnp.where(shift_ids == 1, -2, jnp.where(shift_ids == device_count - 1, -1, drawn_order)))
    shift_order = jnp.argsort(priority, stable=True).astype(jnp.int32)
    shift_list = shift_order[rank_table]
    source_perms = jax.vmap(lambda sub_key: jax.random.permutation(sub_key, per_device))(jax.random.split(source_key, device_count)).astype(jnp.int32)
    shifts = shift_list[source_perms]
    source_ids = jnp.arange(device_count, dtype=jnp.int32)[:, None]
    targets = ((source_ids + shifts) % device_count).reshape(-1)
    flat_ids = jnp.arange(device_count * per_device, dtype=jnp.int32)
    same_target = targets[None, :] == targets[:, None]
    earlier = flat_ids[None, :] < flat_ids[:, None]
    arrival = jnp.sum((same_target & earlier).astype(jnp.int32), axis=1)
    slot_perms = jax.vmap(lambda sub_key: jax.random.permutation(sub_key, per_device))(jax.random.split(target_key, device_count)).astype(jnp.int32)
    slots = slot_perms[targets, arrival]
    block_plan = (targets * per_device + slots).astype(jnp.int32)
    inverse = jnp.zeros((device_count * per_device,), jnp.int32).at[block_plan].set(flat_ids)
    return (block_plan, inverse)


def draw_queries(key, part):
    shape_full = (TOKENS, HQ * HD)
    base_draw = jnp.clip(jax.random.normal(jax.random.fold_in(key, 3), shape_full, jnp.float32), -4.5, 4.5)
    return base_draw.astype(jnp.bfloat16)


def draw_key_rows(key, part):
    shape_full = (TOKENS, KVH * HD)
    base_draw = jnp.clip(jax.random.normal(jax.random.fold_in(key, 4), shape_full, jnp.float32), -4.5, 4.5)
    return base_draw.astype(jnp.bfloat16)


def draw_lengths(key, part):
    return document_lengths(key)


def draw_block_plan(key, part):
    return plan_tables(key)[0]


def draw_inverse(key, part):
    return plan_tables(key)[1]


def draw_mask_lo(key, part):
    all_lengths = document_lengths(key)
    doc_ends = jnp.cumsum(all_lengths).astype(jnp.int32)
    doc_starts = doc_ends - all_lengths
    block_ids = jnp.arange(NBLK, dtype=jnp.int32)
    first_rows = block_ids * BLK
    doc_ids = jnp.sum((first_rows[:, None] >= doc_ends[None, :]).astype(jnp.int32), axis=1)
    windows = jax.random.randint(jax.random.fold_in(key, 13), (NDOC,), max(1, WIN // 2), WIN + 1, dtype=jnp.int32)
    windows = jnp.where(all_lengths == MOST, NBLK, windows)
    start_block = jnp.take(doc_starts, doc_ids) // BLK
    return jnp.maximum(start_block, block_ids - jnp.take(windows, doc_ids)).astype(jnp.int32)


def strengthened(values, key, source, target, parts, factor):
    def block_of(dim):
        return (jnp.arange(values.shape[dim]) // (values.shape[dim] // parts)).reshape((-1,) + (1,) * (values.ndim - 1 - dim))

    one_side = jax.random.permutation(key, parts)[block_of(target)]
    other_side = (block_of(target) + parts // 2) % parts
    return jnp.where((block_of(source) == one_side) | (block_of(source) == other_side), factor * values, values)


def level_of(stream_key, dims, shards, least, top_value):
    factor_of = 1.0
    for axis_at, blocks in shards:
        draws = jax.random.uniform(jax.random.fold_in(jax.random.fold_in(stream_key, 6), axis_at), (blocks,), jnp.float32, least / len(shards), top_value / len(shards))
        factor_of = factor_of * jnp.repeat(jnp.exp(draws), dims[axis_at] // blocks).reshape((-1,) + (1,) * (len(dims) - 1 - axis_at))
    return factor_of


def normal_values(rng, dims, width, reach, cuts=(), held_as=jnp.bfloat16):
    values = width * jax.random.normal(rng, dims, jnp.float32)
    if cuts:
        values = values * level_of(rng, dims, cuts, -0.22, 0.18)
    return jnp.clip(values, -reach, reach).astype(held_as)


def bell_draw_with(own_key, shape, width, reach, pieces, heavy, kind=jnp.bfloat16):
    drawn = width * jax.random.normal(own_key, shape, jnp.float32)
    if pieces:
        drawn = drawn * level_of(own_key, shape, pieces, -0.22, 0.18)
    return jnp.clip(strengthened(drawn, jax.random.fold_in(own_key, 3), *heavy), -reach, reach).astype(kind)


def setup_inputs(seed: int = 0) -> dict:
    seeds = jax.random.split(jax.random.key(seed), 9)
    queries = draw_queries(jax.random.fold_in(seeds[8], 71), 0)
    key_rows = draw_key_rows(jax.random.fold_in(seeds[8], 71), 0)
    values = normal_values(seeds[2], (TOKENS, KVH * HD), 4.0, 24.0, ((0, 32), (1, 8)))
    lengths = draw_lengths(jax.random.fold_in(seeds[8], 71), 0)
    block_plan = draw_block_plan(jax.random.fold_in(seeds[8], 71), 0)
    inverse = draw_inverse(jax.random.fold_in(seeds[8], 71), 0)
    mask_lo = draw_mask_lo(jax.random.fold_in(seeds[8], 71), 0)
    out_weight = bell_draw_with(seeds[7], (HQ * HD, D), (HQ * HD // 16) ** -0.5, 0.375, ((0, 8),), (0, 1, 8, 2.0))
    return dict(queries=queries, key_rows=key_rows, values=values, lengths=lengths, block_plan=block_plan, inverse=inverse, mask_lo=mask_lo, out_weight=out_weight)


def document_of(positions, lengths):
    doc_ends = jnp.cumsum(lengths).astype(jnp.int32)
    return jnp.sum((positions[:, None] >= doc_ends[None, :]).astype(jnp.int32), axis=1)


def reference(queries, key_rows, values, lengths, block_plan, inverse, mask_lo, out_weight):
    query_width = HQ * HD
    group_size = HQ // KVH

    def place(source_rows):
        blocked = source_rows.reshape(NBLK, BLK, source_rows.shape[1])
        return jnp.zeros_like(blocked).at[block_plan].set(blocked).reshape(source_rows.shape)

    held_queries = place(queries)
    held_keys = place(key_rows)
    held_values = place(values)
    offsets = jnp.arange(BLK, dtype=jnp.int32)
    held_pos = (inverse[:, None].astype(jnp.int32) * BLK + offsets[None, :]).reshape(TOKENS)
    held_doc = document_of(held_pos, lengths)
    held_lo = jnp.repeat(mask_lo[inverse].astype(jnp.int32), BLK)
    key_block = held_pos // BLK
    query_block = 512 if TOKENS % 512 == 0 else TOKENS
    block_total = TOKENS // query_block
    score_scale = HD ** -0.5
    zero_index = jnp.zeros((), jnp.int32)

    def one_item(item_index):
        group_index = (item_index // block_total).astype(jnp.int32)
        block_index = (item_index % block_total).astype(jnp.int32)
        first_row = (block_index * query_block).astype(jnp.int32)
        query_col = (group_index * (group_size * HD)).astype(jnp.int32)
        kv_col = (group_index * HD).astype(jnp.int32)
        query_part = lax.dynamic_slice(held_queries, (first_row, query_col), (query_block, group_size * HD))
        query_part = query_part.astype(jnp.float32).reshape(query_block, group_size, HD)
        key_part = lax.dynamic_slice(held_keys, (zero_index, kv_col), (TOKENS, HD)).astype(jnp.float32)
        value_part = lax.dynamic_slice(held_values, (zero_index, kv_col), (TOKENS, HD)).astype(jnp.float32)
        query_pos = lax.dynamic_slice_in_dim(held_pos, first_row, query_block)
        query_doc = lax.dynamic_slice_in_dim(held_doc, first_row, query_block)
        query_lo = lax.dynamic_slice_in_dim(held_lo, first_row, query_block)
        allowed = (query_doc[:, None] == held_doc[None, :]) & (held_pos[None, :] <= query_pos[:, None]) & (key_block[None, :] >= query_lo[:, None])
        scores = jnp.einsum("tgd,sd->tgs", query_part, key_part) * score_scale
        scores = jnp.where(allowed[:, None, :], scores, -jnp.inf)
        row_max = jnp.max(scores, axis=-1, keepdims=True)
        weights = jnp.where(allowed[:, None, :], jnp.exp(scores - row_max), 0.0)
        denominators = jnp.sum(weights, axis=-1)
        rounded = lax.optimization_barrier(weights.astype(jnp.bfloat16)).astype(jnp.float32)
        result = jnp.einsum("tgs,sd->tgd", rounded, value_part) / denominators[..., None]
        return result.astype(jnp.bfloat16)

    results = lax.map(one_item, jnp.arange(KVH * block_total, dtype=jnp.int32))
    results = results.reshape(KVH, block_total, query_block, group_size, HD)
    held_att = results.transpose(1, 2, 0, 3, 4).reshape(TOKENS, query_width)
    held_blocks = held_att.reshape(NBLK, BLK, query_width)
    attended = jnp.zeros_like(held_blocks).at[inverse].set(held_blocks).reshape(TOKENS, query_width)
    feature_group = query_width // N_HEAD
    summed = jnp.zeros((TOKENS, D), jnp.float32)
    for group_part in range(N_HEAD):
        lower = group_part * feature_group
        partial_value = jnp.dot(attended[:, lower:lower + feature_group], out_weight[lower:lower + feature_group], preferred_element_type=jnp.float32)
        partial_value = lax.optimization_barrier(partial_value.astype(jnp.bfloat16)).astype(jnp.float32)
        summed = summed + partial_value
    return summed.astype(jnp.bfloat16)
```

```python
import functools

import jax
import jax.numpy as jnp
from jax import lax
from jax.experimental import pallas as pl
from jax.experimental.pallas import tpu as pltpu
from jax.sharding import PartitionSpec as P

HD = 128
BLK = 8
TQ = 256
TK = 512
NEG_FILL = -1e30


def attn_kernel(tiles_ref, q_ref, kv_ref, qpos_ref, lo_ref, o_ref, m_sc, l_sc, acc_sc):
    n_q = q_ref.shape[0] // TQ
    scale = HD ** (-0.5)

    def q_body(qi, carry):
        r0 = pl.multiple_of(qi * TQ, TQ)
        q = q_ref[pl.ds(r0, TQ), :]
        qpos = qpos_ref[pl.ds(r0, TQ), :]
        lo = lo_ref[pl.ds(r0, TQ), :]
        m_sc[...] = jnp.full(m_sc.shape, NEG_FILL, jnp.float32)
        l_sc[...] = jnp.zeros(l_sc.shape, jnp.float32)
        acc_sc[...] = jnp.zeros(acc_sc.shape, jnp.float32)

        def k_body(kj, c):
            c0 = pl.multiple_of(kj * TK, TK)
            k = kv_ref[pl.ds(c0, TK), pl.ds(0, HD)]
            v = kv_ref[pl.ds(c0, TK), pl.ds(HD, HD)]
            s = lax.dot_general(
                q, k, (((1,), (1,)), ((), ())), preferred_element_type=jnp.float32
            ) * scale
            kpos = c0 + lax.broadcasted_iota(jnp.int32, (TQ, TK), 1)
            ok = (kpos >= lo) & (kpos <= qpos)
            s = jnp.where(ok, s, NEG_FILL)
            m_prev = m_sc[...]
            m_new = jnp.maximum(m_prev, jnp.max(s, axis=1, keepdims=True))
            p = jnp.where(ok, jnp.exp(s - m_new), 0.0)
            fade = jnp.exp(m_prev - m_new)
            l_sc[...] = l_sc[...] * fade + jnp.sum(p, axis=1, keepdims=True)
            acc_sc[...] = acc_sc[...] * fade + jnp.dot(
                p.astype(jnp.bfloat16), v, preferred_element_type=jnp.float32
            )
            m_sc[...] = m_new
            return c

        lax.fori_loop(tiles_ref[qi, 0], tiles_ref[qi, 1], k_body, 0)
        o_ref[pl.ds(r0, TQ), :] = (acc_sc[...] / l_sc[...]).astype(o_ref.dtype)
        return carry

    lax.fori_loop(0, n_q, q_body, 0)


def attend(q_rows, kv_all, qpos_rows, lo_rows, tiles):
    rows = q_rows.shape[0]
    vmem = pltpu.MemorySpace.VMEM if hasattr(pltpu, "MemorySpace") else pltpu.VMEM
    return pl.pallas_call(
        attn_kernel,
        out_shape=jax.ShapeDtypeStruct((rows, HD), jnp.bfloat16),
        in_specs=[
            pl.BlockSpec(memory_space=pltpu.SMEM),
            pl.BlockSpec(memory_space=vmem),
            pl.BlockSpec(memory_space=vmem),
            pl.BlockSpec(memory_space=vmem),
            pl.BlockSpec(memory_space=vmem),
        ],
        out_specs=pl.BlockSpec(memory_space=vmem),
        scratch_shapes=[
            pltpu.VMEM((TQ, 1), jnp.float32),
            pltpu.VMEM((TQ, 1), jnp.float32),
            pltpu.VMEM((TQ, HD), jnp.float32),
        ],
    )(tiles, q_rows, kv_all, qpos_rows, lo_rows)


def on_device(queries, key_rows, values, lengths, block_plan, inverse, mask_lo, out_weight):
    row_count, query_width = queries.shape
    group_size = query_width // HD
    here = lax.axis_index("ctx")
    first = here * row_count
    pos = first + jnp.arange(row_count, dtype=jnp.int32)
    doc_ends = jnp.cumsum(lengths).astype(jnp.int32)
    doc_start = jnp.max(jnp.where(doc_ends[None, :] <= pos[:, None], doc_ends[None, :], 0), axis=1)
    block_lo = lax.dynamic_slice_in_dim(mask_lo, here * (row_count // BLK), row_count // BLK)
    lo_tok = jnp.maximum(jnp.repeat(block_lo, BLK) * BLK, doc_start)
    qpos_rows = jnp.repeat(pos, group_size)[:, None]
    lo_rows = jnp.repeat(lo_tok, group_size)[:, None]
    tok_per_tile = TQ // group_size
    tile_lo = jnp.min(lo_tok.reshape(-1, tok_per_tile), axis=1)
    tile_hi = pos.reshape(-1, tok_per_tile)[:, -1]
    tiles = jnp.stack([tile_lo // TK, tile_hi // TK + 1], axis=1).astype(jnp.int32)

    kv_local = jnp.concatenate([key_rows, values], axis=1)
    kv_all = lax.all_gather(kv_local, "ctx", axis=0, tiled=True)
    q_rows = queries.reshape(row_count * group_size, HD)
    att = attend(q_rows, kv_all, qpos_rows, lo_rows, tiles).reshape(row_count, query_width)

    partial_value = jnp.dot(att, out_weight, preferred_element_type=jnp.float32).astype(jnp.bfloat16)
    summed = lax.psum_scatter(partial_value, "head", scatter_dimension=1, tiled=True)
    return summed.astype(jnp.float32).astype(jnp.bfloat16)


def solution(mesh):
    in_specs = (
        P("ctx", "head"),
        P("ctx", "head"),
        P("ctx", "head"),
        P(),
        P("ctx"),
        P(),
        P(),
        P("head", None),
    )
    out_specs = P("ctx", "head")
    return jax.shard_map(
        on_device, mesh=mesh, in_specs=in_specs, out_specs=out_specs, check_vma=False
    )
```

```python
import functools

import jax
import jax.numpy as jnp
from jax import lax
from jax.experimental import pallas as pl
from jax.experimental.pallas import tpu as pltpu
from jax.sharding import PartitionSpec as P

HD = 128
BLK = 8
TQ = 256
TK = 512
NEG_FILL = -1e30
LONGEST = 4352


def attn_kernel(tiles_ref, q_ref, kv_ref, qpos_ref, lo_ref, o_ref, m_sc, l_sc, acc_sc):
    n_q = q_ref.shape[0] // TQ
    scale = HD ** (-0.5)

    def q_body(qi, carry):
        r0 = pl.multiple_of(qi * TQ, TQ)
        q = q_ref[pl.ds(r0, TQ), :]
        qpos = qpos_ref[pl.ds(r0, TQ), :]
        lo = lo_ref[pl.ds(r0, TQ), :]
        m_sc[...] = jnp.full(m_sc.shape, NEG_FILL, jnp.float32)
        l_sc[...] = jnp.zeros(l_sc.shape, jnp.float32)
        acc_sc[...] = jnp.zeros(acc_sc.shape, jnp.float32)

        def k_body(kj, c):
            c0 = pl.multiple_of(kj * TK, TK)
            k = kv_ref[pl.ds(c0, TK), pl.ds(0, HD)]
            v = kv_ref[pl.ds(c0, TK), pl.ds(HD, HD)]
            s = lax.dot_general(
                q, k, (((1,), (1,)), ((), ())), preferred_element_type=jnp.float32
            ) * scale
            kpos = c0 + lax.broadcasted_iota(jnp.int32, (TQ, TK), 1)
            ok = (kpos >= lo) & (kpos <= qpos)
            s = jnp.where(ok, s, NEG_FILL)
            m_prev = m_sc[...]
            m_new = jnp.maximum(m_prev, jnp.max(s, axis=1, keepdims=True))
            p = jnp.where(ok, jnp.exp(s - m_new), 0.0)
            fade = jnp.exp(m_prev - m_new)
            l_sc[...] = l_sc[...] * fade + jnp.sum(p, axis=1, keepdims=True)
            acc_sc[...] = acc_sc[...] * fade + jnp.dot(
                p.astype(jnp.bfloat16), v, preferred_element_type=jnp.float32
            )
            m_sc[...] = m_new
            return c

        lax.fori_loop(tiles_ref[qi, 0], tiles_ref[qi, 1], k_body, 0)
        o_ref[pl.ds(r0, TQ), :] = (acc_sc[...] / l_sc[...]).astype(o_ref.dtype)
        return carry

    lax.fori_loop(0, n_q, q_body, 0)


def attend(q_rows, kv_all, qpos_rows, lo_rows, tiles):
    rows = q_rows.shape[0]
    vmem = pltpu.MemorySpace.VMEM if hasattr(pltpu, "MemorySpace") else pltpu.VMEM
    return pl.pallas_call(
        attn_kernel,
        out_shape=jax.ShapeDtypeStruct((rows, HD), jnp.bfloat16),
        in_specs=[
            pl.BlockSpec(memory_space=pltpu.SMEM),
            pl.BlockSpec(memory_space=vmem),
            pl.BlockSpec(memory_space=vmem),
            pl.BlockSpec(memory_space=vmem),
            pl.BlockSpec(memory_space=vmem),
        ],
        out_specs=pl.BlockSpec(memory_space=vmem),
        scratch_shapes=[
            pltpu.VMEM((TQ, 1), jnp.float32),
            pltpu.VMEM((TQ, 1), jnp.float32),
            pltpu.VMEM((TQ, HD), jnp.float32),
        ],
    )(tiles, q_rows, kv_all, qpos_rows, lo_rows)


def on_device(queries, key_rows, values, lengths, block_plan, inverse, mask_lo, out_weight):
    row_count, query_width = queries.shape
    group_size = query_width // HD
    here = lax.axis_index("ctx")
    first = here * row_count
    pos = first + jnp.arange(row_count, dtype=jnp.int32)
    doc_ends = jnp.cumsum(lengths).astype(jnp.int32)
    doc_start = jnp.max(jnp.where(doc_ends[None, :] <= pos[:, None], doc_ends[None, :], 0), axis=1)
    block_lo = lax.dynamic_slice_in_dim(mask_lo, here * (row_count // BLK), row_count // BLK)
    lo_tok = jnp.maximum(jnp.repeat(block_lo, BLK) * BLK, doc_start)
    qpos_rows = jnp.repeat(pos, group_size)[:, None]
    lo_rows = jnp.repeat(lo_tok, group_size)[:, None]
    tok_per_tile = TQ // group_size
    tile_lo = jnp.min(lo_tok.reshape(-1, tok_per_tile), axis=1)
    tile_hi = pos.reshape(-1, tok_per_tile)[:, -1]

    kv_local = jnp.concatenate([key_rows, values], axis=1)
    n_ctx = lax.axis_size("ctx")
    reach = min(n_ctx - 1, -(-(LONGEST - 1) // row_count))
    pieces = []
    for shift in range(reach, 0, -1):
        perm = [(i, i + shift) for i in range(n_ctx - shift)]
        pieces.append(lax.ppermute(kv_local, "ctx", perm))
    pieces.append(kv_local)
    kv_win = jnp.concatenate(pieces, axis=0)
    base = first - reach * row_count
    span = kv_win.shape[0]
    tiles = jnp.stack(
        [(tile_lo - base) // TK, jnp.minimum((tile_hi - base) // TK + 1, span // TK)], axis=1
    ).astype(jnp.int32)
    q_rows = queries.reshape(row_count * group_size, HD)
    att = attend(q_rows, kv_win, qpos_rows - base, lo_rows - base, tiles).reshape(row_count, query_width)

    partial_value = jnp.dot(att, out_weight, preferred_element_type=jnp.float32).astype(jnp.bfloat16)
    n_head = lax.axis_size("head")
    cols = partial_value.shape[1] // n_head
    parts = partial_value.reshape(row_count, n_head, cols).transpose(1, 0, 2)
    got = lax.all_to_all(parts, "head", split_axis=0, concat_axis=0, tiled=True)
    return jnp.sum(got.astype(jnp.float32), axis=0).astype(jnp.bfloat16)


def solution(mesh):
    in_specs = (
        P("ctx", "head"),
        P("ctx", "head"),
        P("ctx", "head"),
        P(),
        P("ctx"),
        P(),
        P(),
        P("head", None),
    )
    out_specs = P("ctx", "head")
    return jax.shard_map(
        on_device, mesh=mesh, in_specs=in_specs, out_specs=out_specs, check_vma=False
    )
```

```python
import functools

import jax
import jax.numpy as jnp
from jax import lax
from jax.experimental import pallas as pl
from jax.experimental.pallas import tpu as pltpu
from jax.sharding import PartitionSpec as P

HD = 128
BLK = 8
TQ = 256
TK = 512
NEG_FILL = -1e30


def attn_kernel(tiles_ref, q_ref, kv_ref, qpos_ref, lo_ref, o_ref, m_sc, l_sc, acc_sc):
    n_q = q_ref.shape[0] // TQ
    scale = HD ** (-0.5)

    def q_body(qi, carry):
        r0 = pl.multiple_of(qi * TQ, TQ)
        q = q_ref[pl.ds(r0, TQ), :]
        qpos = qpos_ref[pl.ds(r0, TQ), :]
        lo = lo_ref[pl.ds(r0, TQ), :]
        m_sc[...] = jnp.full(m_sc.shape, NEG_FILL, jnp.float32)
        l_sc[...] = jnp.zeros(l_sc.shape, jnp.float32)
        acc_sc[...] = jnp.zeros(acc_sc.shape, jnp.float32)

        def k_step(kj, masked):
            c0 = pl.multiple_of(kj * TK, TK)
            k = kv_ref[pl.ds(c0, TK), pl.ds(0, HD)]
            v = kv_ref[pl.ds(c0, TK), pl.ds(HD, HD)]
            s = lax.dot_general(
                q, k, (((1,), (1,)), ((), ())), preferred_element_type=jnp.float32
            ) * scale
            if masked:
                kpos = c0 + lax.broadcasted_iota(jnp.int32, (TQ, TK), 1)
                ok = (kpos >= lo) & (kpos <= qpos)
                s = jnp.where(ok, s, NEG_FILL)
            m_prev = m_sc[...]
            m_new = jnp.maximum(m_prev, jnp.max(s, axis=1, keepdims=True))
            p = jnp.exp(s - m_new)
            if masked:
                p = jnp.where(ok, p, 0.0)
            fade = jnp.exp(m_prev - m_new)
            l_sc[...] = l_sc[...] * fade + jnp.sum(p, axis=1, keepdims=True)
            acc_sc[...] = acc_sc[...] * fade + jnp.dot(
                p.astype(jnp.bfloat16), v, preferred_element_type=jnp.float32
            )
            m_sc[...] = m_new

        def masked_body(kj, c):
            k_step(kj, True)
            return c

        def open_body(kj, c):
            k_step(kj, False)
            return c

        lax.fori_loop(tiles_ref[qi, 0], tiles_ref[qi, 1], masked_body, 0)
        lax.fori_loop(tiles_ref[qi, 1], tiles_ref[qi, 2], open_body, 0)
        lax.fori_loop(tiles_ref[qi, 2], tiles_ref[qi, 3], masked_body, 0)
        o_ref[pl.ds(r0, TQ), :] = (acc_sc[...] / l_sc[...]).astype(o_ref.dtype)
        return carry

    lax.fori_loop(0, n_q, q_body, 0)


def attend(q_rows, kv_all, qpos_rows, lo_rows, tiles):
    rows = q_rows.shape[0]
    vmem = pltpu.MemorySpace.VMEM if hasattr(pltpu, "MemorySpace") else pltpu.VMEM
    return pl.pallas_call(
        attn_kernel,
        out_shape=jax.ShapeDtypeStruct((rows, HD), jnp.bfloat16),
        in_specs=[
            pl.BlockSpec(memory_space=pltpu.SMEM),
            pl.BlockSpec(memory_space=vmem),
            pl.BlockSpec(memory_space=vmem),
            pl.BlockSpec(memory_space=vmem),
            pl.BlockSpec(memory_space=vmem),
        ],
        out_specs=pl.BlockSpec(memory_space=vmem),
        scratch_shapes=[
            pltpu.VMEM((TQ, 1), jnp.float32),
            pltpu.VMEM((TQ, 1), jnp.float32),
            pltpu.VMEM((TQ, HD), jnp.float32),
        ],
    )(tiles, q_rows, kv_all, qpos_rows, lo_rows)


def on_device(queries, key_rows, values, lengths, block_plan, inverse, mask_lo, out_weight):
    row_count, query_width = queries.shape
    group_size = query_width // HD
    here = lax.axis_index("ctx")
    first = here * row_count
    pos = first + jnp.arange(row_count, dtype=jnp.int32)
    doc_ends = jnp.cumsum(lengths).astype(jnp.int32)
    doc_start = jnp.max(jnp.where(doc_ends[None, :] <= pos[:, None], doc_ends[None, :], 0), axis=1)
    block_lo = lax.dynamic_slice_in_dim(mask_lo, here * (row_count // BLK), row_count // BLK)
    lo_tok = jnp.maximum(jnp.repeat(block_lo, BLK) * BLK, doc_start)
    qpos_rows = jnp.repeat(pos, group_size)[:, None]
    lo_rows = jnp.repeat(lo_tok, group_size)[:, None]
    tok_per_tile = TQ // group_size
    tile_lo = jnp.min(lo_tok.reshape(-1, tok_per_tile), axis=1)
    tile_hi = pos.reshape(-1, tok_per_tile)[:, -1]
    tile_lo_max = jnp.max(lo_tok.reshape(-1, tok_per_tile), axis=1)
    tile_hi_min = pos.reshape(-1, tok_per_tile)[:, 0]

    kv_local = jnp.concatenate([key_rows, values], axis=1)
    kv_all = lax.all_gather(kv_local, "ctx", axis=0, tiled=True)
    t0 = tile_lo // TK
    t3 = tile_hi // TK + 1
    t1 = jnp.clip((tile_lo_max + TK - 1) // TK, t0, t3)
    t2 = jnp.clip((tile_hi_min + 1) // TK, t1, t3)
    tiles = jnp.stack([t0, t1, t2, t3], axis=1).astype(jnp.int32)
    q_rows = queries.reshape(row_count * group_size, HD)
    att = attend(q_rows, kv_all, qpos_rows, lo_rows, tiles).reshape(row_count, query_width)

    partial_value = jnp.dot(att, out_weight, preferred_element_type=jnp.float32).astype(jnp.bfloat16)
    n_head = lax.axis_size("head")
    cols = partial_value.shape[1] // n_head
    parts = partial_value.reshape(row_count, n_head, cols).transpose(1, 0, 2)
    got = lax.all_to_all(parts, "head", split_axis=0, concat_axis=0, tiled=True)
    return jnp.sum(got.astype(jnp.float32), axis=0).astype(jnp.bfloat16)


def solution(mesh):
    in_specs = (
        P("ctx", "head"),
        P("ctx", "head"),
        P("ctx", "head"),
        P(),
        P("ctx"),
        P(),
        P(),
        P("head", None),
    )
    out_specs = P("ctx", "head")
    return jax.shard_map(
        on_device, mesh=mesh, in_specs=in_specs, out_specs=out_specs, check_vma=False
    )
```

```python
import functools

import jax
import jax.numpy as jnp
from jax import lax
from jax.experimental import pallas as pl
from jax.experimental.pallas import tpu as pltpu
from jax.sharding import PartitionSpec as P

HD = 128
BLK = 8
TQ = 256
TK = 512
NEG_FILL = -1e30
LONGEST = 4352


def attn_kernel(tiles_ref, q_ref, kv_ref, qpos_ref, lo_ref, o_ref, m_sc, l_sc, acc_sc):
    n_q = q_ref.shape[0] // TQ
    scale = HD ** (-0.5)

    def q_body(qi, carry):
        r0 = pl.multiple_of(qi * TQ, TQ)
        q = q_ref[pl.ds(r0, TQ), :]
        qpos = qpos_ref[pl.ds(r0, TQ), :]
        lo = lo_ref[pl.ds(r0, TQ), :]
        m_sc[...] = jnp.full(m_sc.shape, NEG_FILL, jnp.float32)
        l_sc[...] = jnp.zeros(l_sc.shape, jnp.float32)
        acc_sc[...] = jnp.zeros(acc_sc.shape, jnp.float32)

        def k_step(kj, masked):
            c0 = pl.multiple_of(kj * TK, TK)
            k = kv_ref[pl.ds(c0, TK), pl.ds(0, HD)]
            v = kv_ref[pl.ds(c0, TK), pl.ds(HD, HD)]
            s = lax.dot_general(
                q, k, (((1,), (1,)), ((), ())), preferred_element_type=jnp.float32
            ) * scale
            if masked:
                kpos = c0 + lax.broadcasted_iota(jnp.int32, (TQ, TK), 1)
                ok = (kpos >= lo) & (kpos <= qpos)
                s = jnp.where(ok, s, NEG_FILL)
            m_prev = m_sc[...]
            m_new = jnp.maximum(m_prev, jnp.max(s, axis=1, keepdims=True))
            p = jnp.exp(s - m_new)
            if masked:
                p = jnp.where(ok, p, 0.0)
            fade = jnp.exp(m_prev - m_new)
            l_sc[...] = l_sc[...] * fade + jnp.sum(p, axis=1, keepdims=True)
            acc_sc[...] = acc_sc[...] * fade + jnp.dot(
                p.astype(jnp.bfloat16), v, preferred_element_type=jnp.float32
            )
            m_sc[...] = m_new

        def masked_body(kj, c):
            k_step(kj, True)
            return c

        def open_body(kj, c):
            k_step(kj, False)
            return c

        lax.fori_loop(tiles_ref[qi, 0], tiles_ref[qi, 1], masked_body, 0)
        lax.fori_loop(tiles_ref[qi, 1], tiles_ref[qi, 2], open_body, 0)
        lax.fori_loop(tiles_ref[qi, 2], tiles_ref[qi, 3], masked_body, 0)
        o_ref[pl.ds(r0, TQ), :] = (acc_sc[...] / l_sc[...]).astype(o_ref.dtype)
        return carry

    lax.fori_loop(0, n_q, q_body, 0)


def attend(q_rows, kv_all, qpos_rows, lo_rows, tiles):
    rows = q_rows.shape[0]
    vmem = pltpu.MemorySpace.VMEM if hasattr(pltpu, "MemorySpace") else pltpu.VMEM
    return pl.pallas_call(
        attn_kernel,
        out_shape=jax.ShapeDtypeStruct((rows, HD), jnp.bfloat16),
        in_specs=[
            pl.BlockSpec(memory_space=pltpu.SMEM),
            pl.BlockSpec(memory_space=vmem),
            pl.BlockSpec(memory_space=vmem),
            pl.BlockSpec(memory_space=vmem),
            pl.BlockSpec(memory_space=vmem),
        ],
        out_specs=pl.BlockSpec(memory_space=vmem),
        scratch_shapes=[
            pltpu.VMEM((TQ, 1), jnp.float32),
            pltpu.VMEM((TQ, 1), jnp.float32),
            pltpu.VMEM((TQ, HD), jnp.float32),
        ],
    )(tiles, q_rows, kv_all, qpos_rows, lo_rows)


MESH_ID = pl.DeviceIdType.MESH


def window_kernel(reach, n_ctx, kv_ref, zero_ref, win_ref, send_sem, recv_sem, local_sem):
    del zero_ref
    me = lax.axis_index("ctx")
    h = lax.axis_index("head")
    rows = kv_ref.shape[0]
    barrier = pltpu.get_barrier_semaphore()
    for d in range(1, reach + 1):
        @pl.when(me + d < n_ctx)
        def _():
            pl.semaphore_signal(barrier, 1, device_id=(me + d, h), device_id_type=MESH_ID)

        @pl.when(me - d >= 0)
        def _():
            pl.semaphore_signal(barrier, 1, device_id=(me - d, h), device_id_type=MESH_ID)

    pl.semaphore_wait(barrier, jnp.minimum(reach, n_ctx - 1 - me) + jnp.minimum(reach, me))
    local = pltpu.make_async_copy(kv_ref, win_ref.at[pl.ds(reach * rows, rows)], local_sem)
    local.start()

    def push(d):
        return pltpu.make_async_remote_copy(
            src_ref=kv_ref,
            dst_ref=win_ref.at[pl.ds((reach - d) * rows, rows)],
            send_sem=send_sem.at[d - 1],
            recv_sem=recv_sem.at[d - 1],
            device_id=(me + d, h),
            device_id_type=MESH_ID,
        )

    for d in range(1, reach + 1):
        @pl.when(me + d < n_ctx)
        def _():
            push(d).start()

    for d in range(1, reach + 1):
        @pl.when(me + d < n_ctx)
        def _():
            push(d).wait_send()

        @pl.when(me - d >= 0)
        def _():
            push(d).wait_recv()

    local.wait()


def gather_window(kv_local, reach, n_ctx):
    rows, width = kv_local.shape
    zero = jnp.zeros(((reach + 1) * rows, width), kv_local.dtype)
    return pl.pallas_call(
        functools.partial(window_kernel, reach, n_ctx),
        out_shape=jax.ShapeDtypeStruct(zero.shape, zero.dtype),
        in_specs=[pl.BlockSpec(memory_space=pl.ANY), pl.BlockSpec(memory_space=pl.ANY)],
        out_specs=pl.BlockSpec(memory_space=pl.ANY),
        scratch_shapes=[
            pltpu.SemaphoreType.DMA((reach,)),
            pltpu.SemaphoreType.DMA((reach,)),
            pltpu.SemaphoreType.DMA(()),
        ],
        input_output_aliases={1: 0},
        compiler_params=pltpu.CompilerParams(collective_id=0, has_side_effects=True),
    )(kv_local, zero)


def swap_kernel(n_head, parts_ref, got_ref, send_sem, recv_sem, local_sem):
    me = lax.axis_index("head")
    row = lax.axis_index("ctx")
    barrier = pltpu.get_barrier_semaphore()
    for d in range(1, n_head):
        pl.semaphore_signal(
            barrier, 1, device_id=(row, lax.rem(me + d, n_head)), device_id_type=MESH_ID
        )
    pl.semaphore_wait(barrier, n_head - 1)
    local = pltpu.make_async_copy(parts_ref.at[me], got_ref.at[me], local_sem)
    local.start()

    def send(d):
        dst = lax.rem(me + d, n_head)
        return pltpu.make_async_remote_copy(
            src_ref=parts_ref.at[dst],
            dst_ref=got_ref.at[me],
            send_sem=send_sem.at[d - 1],
            recv_sem=recv_sem.at[d - 1],
            device_id=(row, dst),
            device_id_type=MESH_ID,
        )

    def arrival(d):
        src = lax.rem(me + n_head - d, n_head)
        return pltpu.make_async_remote_copy(
            src_ref=parts_ref.at[src],
            dst_ref=got_ref.at[src],
            send_sem=send_sem.at[d - 1],
            recv_sem=recv_sem.at[d - 1],
            device_id=(row, src),
            device_id_type=MESH_ID,
        )

    for d in range(1, n_head):
        send(d).start()
    for d in range(1, n_head):
        send(d).wait_send()
        arrival(d).wait_recv()
    local.wait()


def swap_parts(parts):
    n_head = parts.shape[0]
    return pl.pallas_call(
        functools.partial(swap_kernel, n_head),
        out_shape=jax.ShapeDtypeStruct(parts.shape, parts.dtype),
        in_specs=[pl.BlockSpec(memory_space=pl.ANY)],
        out_specs=pl.BlockSpec(memory_space=pl.ANY),
        scratch_shapes=[
            pltpu.SemaphoreType.DMA((n_head - 1,)),
            pltpu.SemaphoreType.DMA((n_head - 1,)),
            pltpu.SemaphoreType.DMA(()),
        ],
        compiler_params=pltpu.CompilerParams(collective_id=1, has_side_effects=True),
    )(parts)


def on_device(queries, key_rows, values, lengths, block_plan, inverse, mask_lo, out_weight):
    row_count, query_width = queries.shape
    group_size = query_width // HD
    here = lax.axis_index("ctx")
    first = here * row_count
    pos = first + jnp.arange(row_count, dtype=jnp.int32)
    doc_ends = jnp.cumsum(lengths).astype(jnp.int32)
    doc_start = jnp.max(jnp.where(doc_ends[None, :] <= pos[:, None], doc_ends[None, :], 0), axis=1)
    block_lo = lax.dynamic_slice_in_dim(mask_lo, here * (row_count // BLK), row_count // BLK)
    lo_tok = jnp.maximum(jnp.repeat(block_lo, BLK) * BLK, doc_start)
    qpos_rows = jnp.repeat(pos, group_size)[:, None]
    lo_rows = jnp.repeat(lo_tok, group_size)[:, None]
    tok_per_tile = TQ // group_size
    tile_lo = jnp.min(lo_tok.reshape(-1, tok_per_tile), axis=1)
    tile_hi = pos.reshape(-1, tok_per_tile)[:, -1]
    tile_lo_max = jnp.max(lo_tok.reshape(-1, tok_per_tile), axis=1)
    tile_hi_min = pos.reshape(-1, tok_per_tile)[:, 0]

    kv_local = jnp.concatenate([key_rows, values], axis=1)
    n_ctx = lax.axis_size("ctx")
    reach = min(n_ctx - 1, -(-(LONGEST - 1) // row_count))
    kv_win = gather_window(kv_local, reach, n_ctx)
    base = first - reach * row_count
    span = kv_win.shape[0]
    t0 = (tile_lo - base) // TK
    t3 = jnp.minimum((tile_hi - base) // TK + 1, span // TK)
    t1 = jnp.clip((tile_lo_max - base + TK - 1) // TK, t0, t3)
    t2 = jnp.clip((tile_hi_min - base + 1) // TK, t1, t3)
    tiles = jnp.stack([t0, t1, t2, t3], axis=1).astype(jnp.int32)
    q_rows = queries.reshape(row_count * group_size, HD)
    att = attend(q_rows, kv_win, qpos_rows - base, lo_rows - base, tiles).reshape(row_count, query_width)

    partial_value = jnp.dot(att, out_weight, preferred_element_type=jnp.float32).astype(jnp.bfloat16)
    n_head = lax.axis_size("head")
    cols = partial_value.shape[1] // n_head
    parts = partial_value.reshape(row_count, n_head, cols).transpose(1, 0, 2)
    got = swap_parts(parts)
    return jnp.sum(got.astype(jnp.float32), axis=0).astype(jnp.bfloat16)


def solution(mesh):
    in_specs = (
        P("ctx", "head"),
        P("ctx", "head"),
        P("ctx", "head"),
        P(),
        P("ctx"),
        P(),
        P(),
        P("head", None),
    )
    out_specs = P("ctx", "head")
    return jax.shard_map(
        on_device, mesh=mesh, in_specs=in_specs, out_specs=out_specs, check_vma=False
    )
```

```python
import functools

import jax
import jax.numpy as jnp
from jax import lax
from jax.experimental import pallas as pl
from jax.experimental.pallas import tpu as pltpu
from jax.sharding import PartitionSpec as P

HD = 128
BLK = 8
TQ = 256
TK = 256
NEG_FILL = -1e30
LONGEST = 4352
PLANE = 4


def attn_kernel(plane, slots, tiles_ref, q_ref, kv_ref, qpos_ref, lo_ref, o_ref, m_sc, l_sc, acc_sc):
    n_q = q_ref.shape[0] // TQ
    scale = HD ** (-0.5)

    def q_body(qi, carry):
        r0 = pl.multiple_of(qi * TQ, TQ)
        q = q_ref[pl.ds(r0, TQ), :]
        qpos = qpos_ref[pl.ds(r0, TQ), :]
        lo = lo_ref[pl.ds(r0, TQ), :]
        m_sc[...] = jnp.full(m_sc.shape, NEG_FILL, jnp.float32)
        l_sc[...] = jnp.zeros(l_sc.shape, jnp.float32)
        acc_sc[...] = jnp.zeros(acc_sc.shape, jnp.float32)

        def k_step(kj, masked):
            c0 = pl.multiple_of(kj * TK, TK)
            at = pl.multiple_of((lax.rem(kj, plane) * slots + kj // plane) * TK, TK)
            k = kv_ref[pl.ds(at, TK), pl.ds(0, HD)]
            v = kv_ref[pl.ds(at, TK), pl.ds(HD, HD)]
            s = lax.dot_general(
                q, k, (((1,), (1,)), ((), ())), preferred_element_type=jnp.float32
            ) * scale
            if masked:
                kpos = c0 + lax.broadcasted_iota(jnp.int32, (TQ, TK), 1)
                ok = (kpos >= lo) & (kpos <= qpos)
                s = jnp.where(ok, s, NEG_FILL)
            m_prev = m_sc[...]
            m_new = jnp.maximum(m_prev, jnp.max(s, axis=1, keepdims=True))
            p = jnp.exp(s - m_new)
            if masked:
                p = jnp.where(ok, p, 0.0)
            fade = jnp.exp(m_prev - m_new)
            l_sc[...] = l_sc[...] * fade + jnp.sum(p, axis=1, keepdims=True)
            acc_sc[...] = acc_sc[...] * fade + jnp.dot(
                p.astype(jnp.bfloat16), v, preferred_element_type=jnp.float32
            )
            m_sc[...] = m_new

        def masked_body(kj, c):
            k_step(kj, True)
            return c

        def open_body(kj, c):
            k_step(kj, False)
            return c

        lax.fori_loop(tiles_ref[qi, 0], tiles_ref[qi, 1], masked_body, 0)
        lax.fori_loop(tiles_ref[qi, 1], tiles_ref[qi, 2], open_body, 0)
        lax.fori_loop(tiles_ref[qi, 2], tiles_ref[qi, 3], masked_body, 0)
        o_ref[pl.ds(r0, TQ), :] = (acc_sc[...] / l_sc[...]).astype(o_ref.dtype)
        return carry

    lax.fori_loop(0, n_q, q_body, 0)


def attend(q_rows, kv_all, qpos_rows, lo_rows, tiles, plane, slots):
    rows = q_rows.shape[0]
    vmem = pltpu.MemorySpace.VMEM if hasattr(pltpu, "MemorySpace") else pltpu.VMEM
    return pl.pallas_call(
        functools.partial(attn_kernel, plane, slots),
        out_shape=jax.ShapeDtypeStruct((rows, HD), jnp.bfloat16),
        in_specs=[
            pl.BlockSpec(memory_space=pltpu.SMEM),
            pl.BlockSpec(memory_space=vmem),
            pl.BlockSpec(memory_space=vmem),
            pl.BlockSpec(memory_space=vmem),
            pl.BlockSpec(memory_space=vmem),
        ],
        out_specs=pl.BlockSpec(memory_space=vmem),
        scratch_shapes=[
            pltpu.VMEM((TQ, 1), jnp.float32),
            pltpu.VMEM((TQ, 1), jnp.float32),
            pltpu.VMEM((TQ, HD), jnp.float32),
        ],
    )(tiles, q_rows, kv_all, qpos_rows, lo_rows)


MESH_ID = pl.DeviceIdType.MESH


def window_kernel(depth, plane, n_ctx, kv_ref, zero_ref, win_ref, send1, recv1, send2, recv2, local_sem):
    del zero_ref
    me = lax.axis_index("ctx")
    h = lax.axis_index("head")
    z = me // plane
    r = me % plane
    n_z = n_ctx // plane
    barrier = pltpu.get_barrier_semaphore()
    for d in range(1, depth + 1):
        @pl.when(z + d < n_z)
        def _():
            pl.semaphore_signal(barrier, 1, device_id=(me + d * plane, h), device_id_type=MESH_ID)

        @pl.when(z - d >= 0)
        def _():
            pl.semaphore_signal(barrier, 1, device_id=(me - d * plane, h), device_id_type=MESH_ID)

    for e in range(1, plane):
        peer = z * plane + lax.rem(r + e, plane)
        pl.semaphore_signal(barrier, 1, device_id=(peer, h), device_id_type=MESH_ID)
    pl.semaphore_wait(
        barrier, jnp.minimum(depth, n_z - 1 - z) + jnp.minimum(depth, z) + (plane - 1)
    )
    local = pltpu.make_async_copy(kv_ref, win_ref.at[r, depth], local_sem)
    local.start()

    def down(d):
        return pltpu.make_async_remote_copy(
            src_ref=kv_ref,
            dst_ref=win_ref.at[r, depth - d],
            send_sem=send1.at[d - 1],
            recv_sem=recv1.at[d - 1],
            device_id=(me + d * plane, h),
            device_id_type=MESH_ID,
        )

    for d in range(1, depth + 1):
        @pl.when(z + d < n_z)
        def _():
            down(d).start()

    for d in range(1, depth + 1):
        @pl.when(z + d < n_z)
        def _():
            down(d).wait_send()

        @pl.when(z - d >= 0)
        def _():
            down(d).wait_recv()

    local.wait()

    def across(e, col):
        return pltpu.make_async_remote_copy(
            src_ref=win_ref.at[col],
            dst_ref=win_ref.at[col],
            send_sem=send2.at[e - 1],
            recv_sem=recv2.at[e - 1],
            device_id=(z * plane + lax.rem(r + e, plane), h),
            device_id_type=MESH_ID,
        )

    for e in range(1, plane):
        across(e, r).start()
    for e in range(1, plane):
        across(e, r).wait_send()
        across(e, lax.rem(r + plane - e, plane)).wait_recv()


def gather_window(kv_local, depth, plane, n_ctx):
    rows, width = kv_local.shape
    zero = jnp.zeros((plane, depth + 1, rows, width), kv_local.dtype)
    return pl.pallas_call(
        functools.partial(window_kernel, depth, plane, n_ctx),
        out_shape=jax.ShapeDtypeStruct(zero.shape, zero.dtype),
        in_specs=[pl.BlockSpec(memory_space=pl.ANY), pl.BlockSpec(memory_space=pl.ANY)],
        out_specs=pl.BlockSpec(memory_space=pl.ANY),
        scratch_shapes=[
            pltpu.SemaphoreType.DMA((depth,)),
            pltpu.SemaphoreType.DMA((depth,)),
            pltpu.SemaphoreType.DMA((plane - 1,)),
            pltpu.SemaphoreType.DMA((plane - 1,)),
            pltpu.SemaphoreType.DMA(()),
        ],
        input_output_aliases={1: 0},
        compiler_params=pltpu.CompilerParams(collective_id=0, has_side_effects=True),
    )(kv_local, zero)


def swap_kernel(n_head, parts_ref, got_ref, send_sem, recv_sem, local_sem):
    me = lax.axis_index("head")
    row = lax.axis_index("ctx")
    barrier = pltpu.get_barrier_semaphore()
    for d in range(1, n_head):
        pl.semaphore_signal(
            barrier, 1, device_id=(row, lax.rem(me + d, n_head)), device_id_type=MESH_ID
        )
    pl.semaphore_wait(barrier, n_head - 1)
    local = pltpu.make_async_copy(parts_ref.at[me], got_ref.at[me], local_sem)
    local.start()

    def send(d):
        dst = lax.rem(me + d, n_head)
        return pltpu.make_async_remote_copy(
            src_ref=parts_ref.at[dst],
            dst_ref=got_ref.at[me],
            send_sem=send_sem.at[d - 1],
            recv_sem=recv_sem.at[d - 1],
            device_id=(row, dst),
            device_id_type=MESH_ID,
        )

    def arrival(d):
        src = lax.rem(me + n_head - d, n_head)
        return pltpu.make_async_remote_copy(
            src_ref=parts_ref.at[src],
            dst_ref=got_ref.at[src],
            send_sem=send_sem.at[d - 1],
            recv_sem=recv_sem.at[d - 1],
            device_id=(row, src),
            device_id_type=MESH_ID,
        )

    for d in range(1, n_head):
        send(d).start()
    for d in range(1, n_head):
        send(d).wait_send()
        arrival(d).wait_recv()
    local.wait()


def swap_parts(parts):
    n_head = parts.shape[0]
    return pl.pallas_call(
        functools.partial(swap_kernel, n_head),
        out_shape=jax.ShapeDtypeStruct(parts.shape, parts.dtype),
        in_specs=[pl.BlockSpec(memory_space=pl.ANY)],
        out_specs=pl.BlockSpec(memory_space=pl.ANY),
        scratch_shapes=[
            pltpu.SemaphoreType.DMA((n_head - 1,)),
            pltpu.SemaphoreType.DMA((n_head - 1,)),
            pltpu.SemaphoreType.DMA(()),
        ],
        compiler_params=pltpu.CompilerParams(collective_id=1, has_side_effects=True),
    )(parts)


def on_device(queries, key_rows, values, lengths, block_plan, inverse, mask_lo, out_weight):
    row_count, query_width = queries.shape
    group_size = query_width // HD
    here = lax.axis_index("ctx")
    first = here * row_count
    pos = first + jnp.arange(row_count, dtype=jnp.int32)
    doc_ends = jnp.cumsum(lengths).astype(jnp.int32)
    doc_start = jnp.max(jnp.where(doc_ends[None, :] <= pos[:, None], doc_ends[None, :], 0), axis=1)
    block_lo = lax.dynamic_slice_in_dim(mask_lo, here * (row_count // BLK), row_count // BLK)
    lo_tok = jnp.maximum(jnp.repeat(block_lo, BLK) * BLK, doc_start)
    qpos_rows = jnp.repeat(pos, group_size)[:, None]
    lo_rows = jnp.repeat(lo_tok, group_size)[:, None]
    tok_per_tile = TQ // group_size
    tile_lo = jnp.min(lo_tok.reshape(-1, tok_per_tile), axis=1)
    tile_hi = pos.reshape(-1, tok_per_tile)[:, -1]
    tile_lo_max = jnp.max(lo_tok.reshape(-1, tok_per_tile), axis=1)
    tile_hi_min = pos.reshape(-1, tok_per_tile)[:, 0]

    kv_local = jnp.concatenate([key_rows, values], axis=1)
    n_ctx = lax.axis_size("ctx")
    plane = PLANE
    depth = min(n_ctx // plane - 1, -(-(LONGEST - 1) // (plane * row_count)))
    kv_win = gather_window(kv_local, depth, plane, n_ctx)
    kv_win = kv_win.reshape(-1, kv_win.shape[-1])
    base = (here // plane - depth) * plane * row_count
    span = kv_win.shape[0]
    t0 = (tile_lo - base) // TK
    t3 = jnp.minimum((tile_hi - base) // TK + 1, span // TK)
    t1 = jnp.clip((tile_lo_max - base + TK - 1) // TK, t0, t3)
    t2 = jnp.clip((tile_hi_min - base + 1) // TK, t1, t3)
    tiles = jnp.stack([t0, t1, t2, t3], axis=1).astype(jnp.int32)
    q_rows = queries.reshape(row_count * group_size, HD)
    att = attend(q_rows, kv_win, qpos_rows - base, lo_rows - base, tiles, plane, depth + 1).reshape(row_count, query_width)

    partial_value = jnp.dot(att, out_weight, preferred_element_type=jnp.float32).astype(jnp.bfloat16)
    n_head = lax.axis_size("head")
    cols = partial_value.shape[1] // n_head
    parts = partial_value.reshape(row_count, n_head, cols).transpose(1, 0, 2)
    got = swap_parts(parts)
    return jnp.sum(got.astype(jnp.float32), axis=0).astype(jnp.bfloat16)


def solution(mesh):
    in_specs = (
        P("ctx", "head"),
        P("ctx", "head"),
        P("ctx", "head"),
        P(),
        P("ctx"),
        P(),
        P(),
        P("head", None),
    )
    out_specs = P("ctx", "head")
    return jax.shard_map(
        on_device, mesh=mesh, in_specs=in_specs, out_specs=out_specs, check_vma=False
    )
```

```python
import functools

import jax
import jax.numpy as jnp
from jax import lax
from jax.experimental import pallas as pl
from jax.experimental.pallas import tpu as pltpu
from jax.sharding import PartitionSpec as P

HD = 128
BLK = 8
TQ = 1024
TK = 512
NEG_FILL = -1e30
LONGEST = 4352
PLANE = 4


def attn_kernel(tiles_ref, q_ref, kv_ref, qpos_ref, lo_ref, o_ref, m_sc, l_sc, acc_sc):
    n_q = q_ref.shape[0] // TQ
    scale = HD ** (-0.5)

    def q_body(qi, carry):
        r0 = pl.multiple_of(qi * TQ, TQ)
        q = q_ref[pl.ds(r0, TQ), :]
        qpos = qpos_ref[:, pl.ds(r0, TQ)]
        lo = lo_ref[:, pl.ds(r0, TQ)]
        m_sc[...] = jnp.full(m_sc.shape, NEG_FILL, jnp.float32)
        l_sc[...] = jnp.zeros(l_sc.shape, jnp.float32)
        acc_sc[...] = jnp.zeros(acc_sc.shape, jnp.float32)

        def k_step(kj, masked):
            c0 = pl.multiple_of(kj * TK, TK)
            k = kv_ref[pl.ds(c0, TK), pl.ds(0, HD)]
            v = kv_ref[pl.ds(c0, TK), pl.ds(HD, HD)]
            s = lax.dot_general(
                k, q, (((1,), (1,)), ((), ())), preferred_element_type=jnp.float32
            ) * scale
            if masked:
                kpos = c0 + lax.broadcasted_iota(jnp.int32, (TK, TQ), 0)
                ok = (kpos >= lo) & (kpos <= qpos)
                s = jnp.where(ok, s, NEG_FILL)
            m_prev = m_sc[...]
            m_new = jnp.maximum(m_prev, jnp.max(s, axis=0, keepdims=True))
            p = jnp.exp(s - m_new)
            if masked:
                p = jnp.where(ok, p, 0.0)
            fade = jnp.exp(m_prev - m_new)
            l_sc[...] = l_sc[...] * fade + jnp.sum(p, axis=0, keepdims=True)
            acc_sc[...] = acc_sc[...] * fade + lax.dot_general(
                v, p.astype(jnp.bfloat16), (((0,), (0,)), ((), ())),
                preferred_element_type=jnp.float32,
            )
            m_sc[...] = m_new

        def masked_body(kj, c):
            k_step(kj, True)
            return c

        def open_body(kj, c):
            k_step(kj, False)
            return c

        lax.fori_loop(tiles_ref[qi, 0], tiles_ref[qi, 1], masked_body, 0)
        lax.fori_loop(tiles_ref[qi, 1], tiles_ref[qi, 2], open_body, 0)
        lax.fori_loop(tiles_ref[qi, 2], tiles_ref[qi, 3], masked_body, 0)
        o_ref[pl.ds(r0, TQ), :] = (acc_sc[...] / l_sc[...]).T.astype(o_ref.dtype)
        return carry

    lax.fori_loop(0, n_q, q_body, 0)


def attend(q_rows, kv_all, qpos_rows, lo_rows, tiles):
    rows = q_rows.shape[0]
    vmem = pltpu.MemorySpace.VMEM if hasattr(pltpu, "MemorySpace") else pltpu.VMEM
    return pl.pallas_call(
        attn_kernel,
        out_shape=jax.ShapeDtypeStruct((rows, HD), jnp.bfloat16),
        in_specs=[
            pl.BlockSpec(memory_space=pltpu.SMEM),
            pl.BlockSpec(memory_space=vmem),
            pl.BlockSpec(memory_space=vmem),
            pl.BlockSpec(memory_space=vmem),
            pl.BlockSpec(memory_space=vmem),
        ],
        out_specs=pl.BlockSpec(memory_space=vmem),
        scratch_shapes=[
            pltpu.VMEM((1, TQ), jnp.float32),
            pltpu.VMEM((1, TQ), jnp.float32),
            pltpu.VMEM((HD, TQ), jnp.float32),
        ],
    )(tiles, q_rows, kv_all, qpos_rows, lo_rows)


MESH_ID = pl.DeviceIdType.MESH


def window_kernel(depth, plane, n_ctx, kv_ref, zero_ref, win_ref, send1, recv1, send2, recv2, local_sem):
    del zero_ref
    me = lax.axis_index("ctx")
    h = lax.axis_index("head")
    z = me // plane
    r = me % plane
    n_z = n_ctx // plane
    barrier = pltpu.get_barrier_semaphore()
    for d in range(1, depth + 1):
        @pl.when(z + d < n_z)
        def _():
            pl.semaphore_signal(barrier, 1, device_id=(me + d * plane, h), device_id_type=MESH_ID)

        @pl.when(z - d >= 0)
        def _():
            pl.semaphore_signal(barrier, 1, device_id=(me - d * plane, h), device_id_type=MESH_ID)

    for e in range(1, plane):
        peer = z * plane + lax.rem(r + e, plane)
        pl.semaphore_signal(barrier, 1, device_id=(peer, h), device_id_type=MESH_ID)
    pl.semaphore_wait(
        barrier, jnp.minimum(depth, n_z - 1 - z) + jnp.minimum(depth, z) + (plane - 1)
    )
    local = pltpu.make_async_copy(kv_ref, win_ref.at[r, depth], local_sem)
    local.start()

    def down(d):
        return pltpu.make_async_remote_copy(
            src_ref=kv_ref,
            dst_ref=win_ref.at[r, depth - d],
            send_sem=send1.at[d - 1],
            recv_sem=recv1.at[d - 1],
            device_id=(me + d * plane, h),
            device_id_type=MESH_ID,
        )

    for d in range(1, depth + 1):
        @pl.when(z + d < n_z)
        def _():
            down(d).start()

    for d in range(1, depth + 1):
        @pl.when(z + d < n_z)
        def _():
            down(d).wait_send()

        @pl.when(z - d >= 0)
        def _():
            down(d).wait_recv()

    local.wait()

    def across(e, col):
        return pltpu.make_async_remote_copy(
            src_ref=win_ref.at[col],
            dst_ref=win_ref.at[col],
            send_sem=send2.at[e - 1],
            recv_sem=recv2.at[e - 1],
            device_id=(z * plane + lax.rem(r + e, plane), h),
            device_id_type=MESH_ID,
        )

    for e in range(1, plane):
        across(e, r).start()
    for e in range(1, plane):
        across(e, r).wait_send()
        across(e, lax.rem(r + plane - e, plane)).wait_recv()


def gather_window(kv_local, depth, plane, n_ctx):
    rows, width = kv_local.shape
    zero = jnp.zeros((plane, depth + 1, rows, width), kv_local.dtype)
    return pl.pallas_call(
        functools.partial(window_kernel, depth, plane, n_ctx),
        out_shape=jax.ShapeDtypeStruct(zero.shape, zero.dtype),
        in_specs=[pl.BlockSpec(memory_space=pl.ANY), pl.BlockSpec(memory_space=pl.ANY)],
        out_specs=pl.BlockSpec(memory_space=pl.ANY),
        scratch_shapes=[
            pltpu.SemaphoreType.DMA((depth,)),
            pltpu.SemaphoreType.DMA((depth,)),
            pltpu.SemaphoreType.DMA((plane - 1,)),
            pltpu.SemaphoreType.DMA((plane - 1,)),
            pltpu.SemaphoreType.DMA(()),
        ],
        input_output_aliases={1: 0},
        compiler_params=pltpu.CompilerParams(collective_id=0, has_side_effects=True),
    )(kv_local, zero)


def swap_kernel(n_head, parts_ref, got_ref, send_sem, recv_sem, local_sem):
    me = lax.axis_index("head")
    row = lax.axis_index("ctx")
    barrier = pltpu.get_barrier_semaphore()
    for d in range(1, n_head):
        pl.semaphore_signal(
            barrier, 1, device_id=(row, lax.rem(me + d, n_head)), device_id_type=MESH_ID
        )
    pl.semaphore_wait(barrier, n_head - 1)
    local = pltpu.make_async_copy(parts_ref.at[me], got_ref.at[me], local_sem)
    local.start()

    def send(d):
        dst = lax.rem(me + d, n_head)
        return pltpu.make_async_remote_copy(
            src_ref=parts_ref.at[dst],
            dst_ref=got_ref.at[me],
            send_sem=send_sem.at[d - 1],
            recv_sem=recv_sem.at[d - 1],
            device_id=(row, dst),
            device_id_type=MESH_ID,
        )

    def arrival(d):
        src = lax.rem(me + n_head - d, n_head)
        return pltpu.make_async_remote_copy(
            src_ref=parts_ref.at[src],
            dst_ref=got_ref.at[src],
            send_sem=send_sem.at[d - 1],
            recv_sem=recv_sem.at[d - 1],
            device_id=(row, src),
            device_id_type=MESH_ID,
        )

    for d in range(1, n_head):
        send(d).start()
    for d in range(1, n_head):
        send(d).wait_send()
        arrival(d).wait_recv()
    local.wait()


def swap_parts(parts):
    n_head = parts.shape[0]
    return pl.pallas_call(
        functools.partial(swap_kernel, n_head),
        out_shape=jax.ShapeDtypeStruct(parts.shape, parts.dtype),
        in_specs=[pl.BlockSpec(memory_space=pl.ANY)],
        out_specs=pl.BlockSpec(memory_space=pl.ANY),
        scratch_shapes=[
            pltpu.SemaphoreType.DMA((n_head - 1,)),
            pltpu.SemaphoreType.DMA((n_head - 1,)),
            pltpu.SemaphoreType.DMA(()),
        ],
        compiler_params=pltpu.CompilerParams(collective_id=1, has_side_effects=True),
    )(parts)


def on_device(queries, key_rows, values, lengths, block_plan, inverse, mask_lo, out_weight):
    row_count, query_width = queries.shape
    group_size = query_width // HD
    here = lax.axis_index("ctx")
    first = here * row_count
    pos = first + jnp.arange(row_count, dtype=jnp.int32)
    doc_ends = jnp.cumsum(lengths).astype(jnp.int32)
    doc_start = jnp.max(jnp.where(doc_ends[None, :] <= pos[:, None], doc_ends[None, :], 0), axis=1)
    block_lo = lax.dynamic_slice_in_dim(mask_lo, here * (row_count // BLK), row_count // BLK)
    lo_tok = jnp.maximum(jnp.repeat(block_lo, BLK) * BLK, doc_start)
    qpos_rows = jnp.repeat(pos, group_size)[None, :]
    lo_rows = jnp.repeat(lo_tok, group_size)[None, :]
    tok_per_tile = TQ // group_size
    tile_lo = jnp.min(lo_tok.reshape(-1, tok_per_tile), axis=1)
    tile_hi = pos.reshape(-1, tok_per_tile)[:, -1]
    tile_lo_max = jnp.max(lo_tok.reshape(-1, tok_per_tile), axis=1)
    tile_hi_min = pos.reshape(-1, tok_per_tile)[:, 0]

    kv_local = jnp.concatenate([key_rows, values], axis=1)
    n_ctx = lax.axis_size("ctx")
    plane = PLANE
    depth = min(n_ctx // plane - 1, -(-(LONGEST - 1) // (plane * row_count)))
    kv_win = gather_window(kv_local, depth, plane, n_ctx)
    kv_win = kv_win.transpose(1, 0, 2, 3).reshape(-1, kv_win.shape[-1])
    base = (here // plane - depth) * plane * row_count
    span = kv_win.shape[0]
    t0 = (tile_lo - base) // TK
    t3 = jnp.minimum((tile_hi - base) // TK + 1, span // TK)
    t1 = jnp.clip((tile_lo_max - base + TK - 1) // TK, t0, t3)
    t2 = jnp.clip((tile_hi_min - base + 1) // TK, t1, t3)
    tiles = jnp.stack([t0, t1, t2, t3], axis=1).astype(jnp.int32)
    q_rows = queries.reshape(row_count * group_size, HD)
    att = attend(q_rows, kv_win, qpos_rows - base, lo_rows - base, tiles).reshape(row_count, query_width)

    partial_value = jnp.dot(att, out_weight, preferred_element_type=jnp.float32).astype(jnp.bfloat16)
    n_head = lax.axis_size("head")
    cols = partial_value.shape[1] // n_head
    parts = partial_value.reshape(row_count, n_head, cols).transpose(1, 0, 2)
    got = swap_parts(parts)
    return jnp.sum(got.astype(jnp.float32), axis=0).astype(jnp.bfloat16)


def solution(mesh):
    in_specs = (
        P("ctx", "head"),
        P("ctx", "head"),
        P("ctx", "head"),
        P(),
        P("ctx"),
        P(),
        P(),
        P("head", None),
    )
    out_specs = P("ctx", "head")
    return jax.shard_map(
        on_device, mesh=mesh, in_specs=in_specs, out_specs=out_specs, check_vma=False
    )
```

```python
import functools

import jax
import jax.numpy as jnp
from jax import lax
from jax.experimental import pallas as pl
from jax.experimental.pallas import tpu as pltpu
from jax.sharding import PartitionSpec as P

HD = 128
BLK = 8
TQ = 1024
TK = 512
NEG_FILL = -1e30
LONGEST = 4352
PLANE = 4


def attn_kernel(tiles_ref, q_ref, kv_ref, qpos_ref, lo_ref, o_ref, m_sc, l_sc, acc_sc):
    n_q = q_ref.shape[0] // TQ
    scale = HD ** (-0.5)

    def q_body(qi, carry):
        r0 = pl.multiple_of(qi * TQ, TQ)
        q = q_ref[pl.ds(r0, TQ), :]
        qpos = qpos_ref[:, pl.ds(r0, TQ)]
        lo = lo_ref[:, pl.ds(r0, TQ)]
        m_sc[...] = jnp.full(m_sc.shape, NEG_FILL, jnp.float32)
        l_sc[...] = jnp.zeros(l_sc.shape, jnp.float32)
        acc_sc[...] = jnp.zeros(acc_sc.shape, jnp.float32)

        def k_step(kj, masked):
            c0 = pl.multiple_of(kj * TK, TK)
            k = kv_ref[pl.ds(c0, TK), pl.ds(0, HD)]
            v = kv_ref[pl.ds(c0, TK), pl.ds(HD, HD)]
            s = lax.dot_general(
                k, q, (((1,), (1,)), ((), ())), preferred_element_type=jnp.float32
            ) * scale
            if masked:
                kpos = c0 + lax.broadcasted_iota(jnp.int32, (TK, TQ), 0)
                ok = (kpos >= lo) & (kpos <= qpos)
                s = jnp.where(ok, s, NEG_FILL)
            m_prev = m_sc[...]
            m_new = jnp.maximum(m_prev, jnp.max(s, axis=0, keepdims=True))
            p = jnp.exp(s - m_new)
            if masked:
                p = jnp.where(ok, p, 0.0)
            fade = jnp.exp(m_prev - m_new)
            l_sc[...] = l_sc[...] * fade + jnp.sum(p, axis=0, keepdims=True)
            acc_sc[...] = acc_sc[...] * fade + lax.dot_general(
                v, p.astype(jnp.bfloat16), (((0,), (0,)), ((), ())),
                preferred_element_type=jnp.float32,
            )
            m_sc[...] = m_new

        def masked_body(kj, c):
            k_step(kj, True)
            return c

        def open_body(kj, c):
            k_step(kj, False)
            return c

        lax.fori_loop(tiles_ref[qi, 0], tiles_ref[qi, 1], masked_body, 0)
        lax.fori_loop(tiles_ref[qi, 1], tiles_ref[qi, 2], open_body, 0)
        lax.fori_loop(tiles_ref[qi, 2], tiles_ref[qi, 3], masked_body, 0)
        o_ref[pl.ds(r0, TQ), :] = (acc_sc[...] / l_sc[...]).T.astype(o_ref.dtype)
        return carry

    lax.fori_loop(0, n_q, q_body, 0)


def attend(q_rows, kv_all, qpos_rows, lo_rows, tiles):
    rows = q_rows.shape[0]
    vmem = pltpu.MemorySpace.VMEM if hasattr(pltpu, "MemorySpace") else pltpu.VMEM
    return pl.pallas_call(
        attn_kernel,
        out_shape=jax.ShapeDtypeStruct((rows, HD), jnp.bfloat16),
        in_specs=[
            pl.BlockSpec(memory_space=pltpu.SMEM),
            pl.BlockSpec(memory_space=vmem),
            pl.BlockSpec(memory_space=vmem),
            pl.BlockSpec(memory_space=vmem),
            pl.BlockSpec(memory_space=vmem),
        ],
        out_specs=pl.BlockSpec(memory_space=vmem),
        scratch_shapes=[
            pltpu.VMEM((1, TQ), jnp.float32),
            pltpu.VMEM((1, TQ), jnp.float32),
            pltpu.VMEM((HD, TQ), jnp.float32),
        ],
    )(tiles, q_rows, kv_all, qpos_rows, lo_rows)


MESH_ID = pl.DeviceIdType.MESH


def window_kernel(depth, plane, n_ctx, kv_ref, zero_ref, win_ref, send1, recv1, send2, recv2, local_sem):
    del zero_ref
    me = lax.axis_index("ctx")
    h = lax.axis_index("head")
    z = me // plane
    r = me % plane
    n_z = n_ctx // plane
    barrier = pltpu.get_barrier_semaphore()
    for d in range(1, depth + 1):
        @pl.when(z + d < n_z)
        def _():
            pl.semaphore_signal(barrier, 1, device_id=(me + d * plane, h), device_id_type=MESH_ID)

        @pl.when(z - d >= 0)
        def _():
            pl.semaphore_signal(barrier, 1, device_id=(me - d * plane, h), device_id_type=MESH_ID)

    for e in range(1, plane):
        peer = z * plane + lax.rem(r + e, plane)
        pl.semaphore_signal(barrier, 1, device_id=(peer, h), device_id_type=MESH_ID)
    pl.semaphore_wait(
        barrier, jnp.minimum(depth, n_z - 1 - z) + jnp.minimum(depth, z) + (plane - 1)
    )
    local = pltpu.make_async_copy(kv_ref, win_ref.at[r, depth], local_sem)
    local.start()

    def down(d):
        return pltpu.make_async_remote_copy(
            src_ref=kv_ref,
            dst_ref=win_ref.at[r, depth - d],
            send_sem=send1.at[d - 1],
            recv_sem=recv1.at[d - 1],
            device_id=(me + d * plane, h),
            device_id_type=MESH_ID,
        )

    for d in range(1, depth + 1):
        @pl.when(z + d < n_z)
        def _():
            down(d).start()

    local.wait()

    def across(e, col, slot):
        return pltpu.make_async_remote_copy(
            src_ref=win_ref.at[col, slot],
            dst_ref=win_ref.at[col, slot],
            send_sem=send2.at[e - 1, slot],
            recv_sem=recv2.at[e - 1, slot],
            device_id=(z * plane + lax.rem(r + e, plane), h),
            device_id_type=MESH_ID,
        )

    for e in range(1, plane):
        across(e, r, depth).start()
    for d in range(1, depth + 1):
        @pl.when(z + d < n_z)
        def _():
            down(d).wait_send()

        @pl.when(z - d >= 0)
        def _():
            down(d).wait_recv()
            for e in range(1, plane):
                across(e, r, depth - d).start()

    for slot in range(depth + 1):
        @pl.when(z - (depth - slot) >= 0)
        def _():
            for e in range(1, plane):
                across(e, r, slot).wait_send()
                across(e, lax.rem(r + plane - e, plane), slot).wait_recv()


def gather_window(kv_local, depth, plane, n_ctx):
    rows, width = kv_local.shape
    zero = jnp.zeros((plane, depth + 1, rows, width), kv_local.dtype)
    return pl.pallas_call(
        functools.partial(window_kernel, depth, plane, n_ctx),
        out_shape=jax.ShapeDtypeStruct(zero.shape, zero.dtype),
        in_specs=[pl.BlockSpec(memory_space=pl.ANY), pl.BlockSpec(memory_space=pl.ANY)],
        out_specs=pl.BlockSpec(memory_space=pl.ANY),
        scratch_shapes=[
            pltpu.SemaphoreType.DMA((depth,)),
            pltpu.SemaphoreType.DMA((depth,)),
            pltpu.SemaphoreType.DMA((plane - 1, depth + 1)),
            pltpu.SemaphoreType.DMA((plane - 1, depth + 1)),
            pltpu.SemaphoreType.DMA(()),
        ],
        input_output_aliases={1: 0},
        compiler_params=pltpu.CompilerParams(collective_id=0, has_side_effects=True),
    )(kv_local, zero)


def swap_kernel(n_head, partial_ref, got_ref, send_sem, recv_sem, local_sem):
    me = lax.axis_index("head")
    cols = got_ref.shape[2]
    row = lax.axis_index("ctx")
    barrier = pltpu.get_barrier_semaphore()
    for d in range(1, n_head):
        pl.semaphore_signal(
            barrier, 1, device_id=(row, lax.rem(me + d, n_head)), device_id_type=MESH_ID
        )
    pl.semaphore_wait(barrier, n_head - 1)
    local = pltpu.make_async_copy(
        partial_ref.at[:, pl.ds(me * cols, cols)], got_ref.at[me], local_sem
    )
    local.start()

    def send(d):
        dst = lax.rem(me + d, n_head)
        return pltpu.make_async_remote_copy(
            src_ref=partial_ref.at[:, pl.ds(dst * cols, cols)],
            dst_ref=got_ref.at[me],
            send_sem=send_sem.at[d - 1],
            recv_sem=recv_sem.at[d - 1],
            device_id=(row, dst),
            device_id_type=MESH_ID,
        )

    def arrival(d):
        src = lax.rem(me + n_head - d, n_head)
        return pltpu.make_async_remote_copy(
            src_ref=partial_ref.at[:, pl.ds(src * cols, cols)],
            dst_ref=got_ref.at[src],
            send_sem=send_sem.at[d - 1],
            recv_sem=recv_sem.at[d - 1],
            device_id=(row, src),
            device_id_type=MESH_ID,
        )

    for d in range(1, n_head):
        send(d).start()
    for d in range(1, n_head):
        send(d).wait_send()
        arrival(d).wait_recv()
    local.wait()


def swap_parts(partial_value, n_head):
    rows, width = partial_value.shape
    return pl.pallas_call(
        functools.partial(swap_kernel, n_head),
        out_shape=jax.ShapeDtypeStruct((n_head, rows, width // n_head), partial_value.dtype),
        in_specs=[pl.BlockSpec(memory_space=pl.ANY)],
        out_specs=pl.BlockSpec(memory_space=pl.ANY),
        scratch_shapes=[
            pltpu.SemaphoreType.DMA((n_head - 1,)),
            pltpu.SemaphoreType.DMA((n_head - 1,)),
            pltpu.SemaphoreType.DMA(()),
        ],
        compiler_params=pltpu.CompilerParams(collective_id=1, has_side_effects=True),
    )(partial_value)


def on_device(queries, key_rows, values, lengths, block_plan, inverse, mask_lo, out_weight):
    row_count, query_width = queries.shape
    group_size = query_width // HD
    here = lax.axis_index("ctx")
    first = here * row_count
    pos = first + jnp.arange(row_count, dtype=jnp.int32)
    doc_ends = jnp.cumsum(lengths).astype(jnp.int32)
    doc_start = jnp.max(jnp.where(doc_ends[None, :] <= pos[:, None], doc_ends[None, :], 0), axis=1)
    block_lo = lax.dynamic_slice_in_dim(mask_lo, here * (row_count // BLK), row_count // BLK)
    lo_tok = jnp.maximum(jnp.repeat(block_lo, BLK) * BLK, doc_start)
    qpos_rows = jnp.repeat(pos, group_size)[None, :]
    lo_rows = jnp.repeat(lo_tok, group_size)[None, :]
    tok_per_tile = TQ // group_size
    tile_lo = jnp.min(lo_tok.reshape(-1, tok_per_tile), axis=1)
    tile_hi = pos.reshape(-1, tok_per_tile)[:, -1]
    tile_lo_max = jnp.max(lo_tok.reshape(-1, tok_per_tile), axis=1)
    tile_hi_min = pos.reshape(-1, tok_per_tile)[:, 0]

    kv_local = jnp.concatenate([key_rows, values], axis=1)
    n_ctx = lax.axis_size("ctx")
    plane = PLANE
    depth = min(n_ctx // plane - 1, -(-(LONGEST - 1) // (plane * row_count)))
    kv_win = gather_window(kv_local, depth, plane, n_ctx)
    kv_win = kv_win.transpose(1, 0, 2, 3).reshape(-1, kv_win.shape[-1])
    base = (here // plane - depth) * plane * row_count
    span = kv_win.shape[0]
    t0 = (tile_lo - base) // TK
    t3 = jnp.minimum((tile_hi - base) // TK + 1, span // TK)
    t1 = jnp.clip((tile_lo_max - base + TK - 1) // TK, t0, t3)
    t2 = jnp.clip((tile_hi_min - base + 1) // TK, t1, t3)
    tiles = jnp.stack([t0, t1, t2, t3], axis=1).astype(jnp.int32)
    q_rows = queries.reshape(row_count * group_size, HD)
    att = attend(q_rows, kv_win, qpos_rows - base, lo_rows - base, tiles).reshape(row_count, query_width)

    partial_value = jnp.dot(att, out_weight, preferred_element_type=jnp.float32).astype(jnp.bfloat16)
    n_head = lax.axis_size("head")
    got = swap_parts(partial_value, n_head)
    return jnp.sum(got.astype(jnp.float32), axis=0).astype(jnp.bfloat16)


def solution(mesh):
    in_specs = (
        P("ctx", "head"),
        P("ctx", "head"),
        P("ctx", "head"),
        P(),
        P("ctx"),
        P(),
        P(),
        P("head", None),
    )
    out_specs = P("ctx", "head")
    return jax.shard_map(
        on_device, mesh=mesh, in_specs=in_specs, out_specs=out_specs, check_vma=False
    )
```

```python
import functools

import jax
import jax.numpy as jnp
from jax import lax
from jax.experimental import pallas as pl
from jax.experimental.pallas import tpu as pltpu
from jax.sharding import PartitionSpec as P

HD = 128
BLK = 8
TQ = 1024
TK = 512
NEG_FILL = -1e30
LONGEST = 4352
PLANE = 4


def attn_kernel(tiles_ref, q_ref, kv_ref, qpos_ref, lo_ref, o_ref, m_sc, l_sc, acc_sc):
    n_q = q_ref.shape[0] // TQ
    scale = HD ** (-0.5)

    def q_body(qi, carry):
        r0 = pl.multiple_of(qi * TQ, TQ)
        q = q_ref[pl.ds(r0, TQ), :]
        qpos = qpos_ref[:, pl.ds(r0, TQ)]
        lo = lo_ref[:, pl.ds(r0, TQ)]
        m_sc[...] = jnp.full(m_sc.shape, NEG_FILL, jnp.float32)
        l_sc[...] = jnp.zeros(l_sc.shape, jnp.float32)
        acc_sc[...] = jnp.zeros(acc_sc.shape, jnp.float32)

        def k_step(kj, masked):
            c0 = pl.multiple_of(kj * TK, TK)
            k = kv_ref[pl.ds(c0, TK), pl.ds(0, HD)]
            v = kv_ref[pl.ds(c0, TK), pl.ds(HD, HD)]
            s = lax.dot_general(
                k, q, (((1,), (1,)), ((), ())), preferred_element_type=jnp.float32
            ) * scale
            if masked:
                kpos = c0 + lax.broadcasted_iota(jnp.int32, (TK, TQ), 0)
                ok = (kpos >= lo) & (kpos <= qpos)
                s = jnp.where(ok, s, NEG_FILL)
            m_prev = m_sc[...]
            m_new = jnp.maximum(m_prev, jnp.max(s, axis=0, keepdims=True))
            p = jnp.exp(s - m_new)
            if masked:
                p = jnp.where(ok, p, 0.0)
            fade = jnp.exp(m_prev - m_new)
            l_sc[...] = l_sc[...] * fade + jnp.sum(p, axis=0, keepdims=True)
            acc_sc[...] = acc_sc[...] * fade + lax.dot_general(
                v, p.astype(jnp.bfloat16), (((0,), (0,)), ((), ())),
                preferred_element_type=jnp.float32,
            )
            m_sc[...] = m_new

        def masked_body(kj, c):
            k_step(kj, True)
            return c

        def open_body(kj, c):
            k_step(kj, False)
            return c

        lax.fori_loop(tiles_ref[qi, 0], tiles_ref[qi, 1], masked_body, 0)
        lax.fori_loop(tiles_ref[qi, 1], tiles_ref[qi, 2], open_body, 0)
        lax.fori_loop(tiles_ref[qi, 2], tiles_ref[qi, 3], masked_body, 0)
        o_ref[pl.ds(r0, TQ), :] = (acc_sc[...] / l_sc[...]).T.astype(o_ref.dtype)
        return carry

    lax.fori_loop(0, n_q, q_body, 0)


def attend(q_rows, kv_all, qpos_rows, lo_rows, tiles):
    rows = q_rows.shape[0]
    vmem = pltpu.MemorySpace.VMEM if hasattr(pltpu, "MemorySpace") else pltpu.VMEM
    return pl.pallas_call(
        attn_kernel,
        out_shape=jax.ShapeDtypeStruct((rows, HD), jnp.bfloat16),
        in_specs=[
            pl.BlockSpec(memory_space=pltpu.SMEM),
            pl.BlockSpec(memory_space=vmem),
            pl.BlockSpec(memory_space=vmem),
            pl.BlockSpec(memory_space=vmem),
            pl.BlockSpec(memory_space=vmem),
        ],
        out_specs=pl.BlockSpec(memory_space=vmem),
        scratch_shapes=[
            pltpu.VMEM((1, TQ), jnp.float32),
            pltpu.VMEM((1, TQ), jnp.float32),
            pltpu.VMEM((HD, TQ), jnp.float32),
        ],
    )(tiles, q_rows, kv_all, qpos_rows, lo_rows)


MESH_ID = pl.DeviceIdType.MESH


def window_kernel(depth, plane, n_ctx, need_col, kv_ref, zero_ref, win_ref, send1, recv1, send2, recv2, local_sem):
    del zero_ref
    me = lax.axis_index("ctx")
    h = lax.axis_index("head")
    z = me // plane
    r = me % plane
    n_z = n_ctx // plane
    mate = r + 1 - 2 * (r % 2)
    across = (r + 2) % plane
    far = across + 1 - 2 * (across % 2)
    barrier = pltpu.get_barrier_semaphore()
    for d in range(1, depth + 1):
        @pl.when(z + d < n_z)
        def _():
            pl.semaphore_signal(barrier, 1, device_id=(me + d * plane, h), device_id_type=MESH_ID)

        @pl.when(z - d >= 0)
        def _():
            pl.semaphore_signal(barrier, 1, device_id=(me - d * plane, h), device_id_type=MESH_ID)

    for peer in (mate, across):
        pl.semaphore_signal(barrier, 1, device_id=(z * plane + peer, h), device_id_type=MESH_ID)
    pl.semaphore_wait(barrier, jnp.minimum(depth, n_z - 1 - z) + jnp.minimum(depth, z) + 2)
    local = pltpu.make_async_copy(kv_ref, win_ref.at[r, depth], local_sem)
    local.start()

    def wanted(d):
        return (d < depth) | (r >= need_col)

    def down(d):
        return pltpu.make_async_remote_copy(
            src_ref=kv_ref,
            dst_ref=win_ref.at[r, depth - d],
            send_sem=send1.at[d - 1],
            recv_sem=recv1.at[d - 1],
            device_id=(me + d * plane, h),
            device_id_type=MESH_ID,
        )

    for d in range(1, depth + 1):
        @pl.when((z + d < n_z) & wanted(d))
        def _():
            down(d).start()

    def has(slot, col):
        return (z - (depth - slot) >= 0) & ((slot > 0) | (col >= need_col))

    def hop(idx, col, slot, to):
        return pltpu.make_async_remote_copy(
            src_ref=win_ref.at[col, slot],
            dst_ref=win_ref.at[col, slot],
            send_sem=send2.at[idx, slot],
            recv_sem=recv2.at[idx, slot],
            device_id=(z * plane + to, h),
            device_id_type=MESH_ID,
        )

    local.wait()
    hop(0, r, depth, mate).start()
    hop(1, r, depth, across).start()
    for d in range(1, depth + 1):
        @pl.when((z + d < n_z) & wanted(d))
        def _():
            down(d).wait_send()

        @pl.when((z - d >= 0) & wanted(d))
        def _():
            down(d).wait_recv()
            hop(0, r, depth - d, mate).start()
            hop(1, r, depth - d, across).start()

    for slot in range(depth, -1, -1):
        @pl.when(has(slot, across))
        def _():
            hop(1, across, slot, across).wait_recv()
            hop(2, across, slot, mate).start()

    for slot in range(depth + 1):
        @pl.when(has(slot, r))
        def _():
            hop(0, r, slot, mate).wait_send()
            hop(1, r, slot, across).wait_send()

        @pl.when(has(slot, across))
        def _():
            hop(2, across, slot, mate).wait_send()

        @pl.when(has(slot, mate))
        def _():
            hop(0, mate, slot, mate).wait_recv()

        @pl.when(has(slot, far))
        def _():
            hop(2, far, slot, mate).wait_recv()


def gather_window(kv_local, depth, plane, n_ctx, need_col):
    rows, width = kv_local.shape
    zero = jnp.zeros((plane, depth + 1, rows, width), kv_local.dtype)
    return pl.pallas_call(
        functools.partial(window_kernel, depth, plane, n_ctx, need_col),
        out_shape=jax.ShapeDtypeStruct(zero.shape, zero.dtype),
        in_specs=[pl.BlockSpec(memory_space=pl.ANY), pl.BlockSpec(memory_space=pl.ANY)],
        out_specs=pl.BlockSpec(memory_space=pl.ANY),
        scratch_shapes=[
            pltpu.SemaphoreType.DMA((depth,)),
            pltpu.SemaphoreType.DMA((depth,)),
            pltpu.SemaphoreType.DMA((3, depth + 1)),
            pltpu.SemaphoreType.DMA((3, depth + 1)),
            pltpu.SemaphoreType.DMA(()),
        ],
        input_output_aliases={1: 0},
        compiler_params=pltpu.CompilerParams(collective_id=0, has_side_effects=True),
    )(kv_local, zero)


def swap_kernel(n_head, partial_ref, got_ref, send_sem, recv_sem, local_sem):
    me = lax.axis_index("head")
    cols = got_ref.shape[2]
    row = lax.axis_index("ctx")
    barrier = pltpu.get_barrier_semaphore()
    for d in range(1, n_head):
        pl.semaphore_signal(
            barrier, 1, device_id=(row, lax.rem(me + d, n_head)), device_id_type=MESH_ID
        )
    pl.semaphore_wait(barrier, n_head - 1)
    local = pltpu.make_async_copy(
        partial_ref.at[:, pl.ds(me * cols, cols)], got_ref.at[me], local_sem
    )
    local.start()

    def send(d):
        dst = lax.rem(me + d, n_head)
        return pltpu.make_async_remote_copy(
            src_ref=partial_ref.at[:, pl.ds(dst * cols, cols)],
            dst_ref=got_ref.at[me],
            send_sem=send_sem.at[d - 1],
            recv_sem=recv_sem.at[d - 1],
            device_id=(row, dst),
            device_id_type=MESH_ID,
        )

    def arrival(d):
        src = lax.rem(me + n_head - d, n_head)
        return pltpu.make_async_remote_copy(
            src_ref=partial_ref.at[:, pl.ds(src * cols, cols)],
            dst_ref=got_ref.at[src],
            send_sem=send_sem.at[d - 1],
            recv_sem=recv_sem.at[d - 1],
            device_id=(row, src),
            device_id_type=MESH_ID,
        )

    for d in range(1, n_head):
        send(d).start()
    for d in range(1, n_head):
        send(d).wait_send()
        arrival(d).wait_recv()
    local.wait()


def swap_parts(partial_value, n_head):
    rows, width = partial_value.shape
    return pl.pallas_call(
        functools.partial(swap_kernel, n_head),
        out_shape=jax.ShapeDtypeStruct((n_head, rows, width // n_head), partial_value.dtype),
        in_specs=[pl.BlockSpec(memory_space=pl.ANY)],
        out_specs=pl.BlockSpec(memory_space=pl.ANY),
        scratch_shapes=[
            pltpu.SemaphoreType.DMA((n_head - 1,)),
            pltpu.SemaphoreType.DMA((n_head - 1,)),
            pltpu.SemaphoreType.DMA(()),
        ],
        compiler_params=pltpu.CompilerParams(collective_id=1, has_side_effects=True),
    )(partial_value)


def on_device(queries, key_rows, values, lengths, block_plan, inverse, mask_lo, out_weight):
    row_count, query_width = queries.shape
    group_size = query_width // HD
    here = lax.axis_index("ctx")
    first = here * row_count
    pos = first + jnp.arange(row_count, dtype=jnp.int32)
    doc_ends = jnp.cumsum(lengths).astype(jnp.int32)
    doc_start = jnp.max(jnp.where(doc_ends[None, :] <= pos[:, None], doc_ends[None, :], 0), axis=1)
    block_lo = lax.dynamic_slice_in_dim(mask_lo, here * (row_count // BLK), row_count // BLK)
    lo_tok = jnp.maximum(jnp.repeat(block_lo, BLK) * BLK, doc_start)
    qpos_rows = jnp.repeat(pos, group_size)[None, :]
    lo_rows = jnp.repeat(lo_tok, group_size)[None, :]
    tok_per_tile = TQ // group_size
    tile_lo = jnp.min(lo_tok.reshape(-1, tok_per_tile), axis=1)
    tile_hi = pos.reshape(-1, tok_per_tile)[:, -1]
    tile_lo_max = jnp.max(lo_tok.reshape(-1, tok_per_tile), axis=1)
    tile_hi_min = pos.reshape(-1, tok_per_tile)[:, 0]

    kv_local = jnp.concatenate([key_rows, values], axis=1)
    n_ctx = lax.axis_size("ctx")
    plane = PLANE
    depth = min(n_ctx // plane - 1, -(-(LONGEST - 1) // (plane * row_count)))
    need_col = max(0, -(-(plane * row_count * depth - (LONGEST - 1) - (row_count - 1)) // row_count))
    kv_win = gather_window(kv_local, depth, plane, n_ctx, need_col)
    kv_win = kv_win.transpose(1, 0, 2, 3).reshape(-1, kv_win.shape[-1])
    base = (here // plane - depth) * plane * row_count
    span = kv_win.shape[0]
    t0 = (tile_lo - base) // TK
    t3 = jnp.minimum((tile_hi - base) // TK + 1, span // TK)
    t1 = jnp.clip((tile_lo_max - base + TK - 1) // TK, t0, t3)
    t2 = jnp.clip((tile_hi_min - base + 1) // TK, t1, t3)
    tiles = jnp.stack([t0, t1, t2, t3], axis=1).astype(jnp.int32)
    q_rows = queries.reshape(row_count * group_size, HD)
    att = attend(q_rows, kv_win, qpos_rows - base, lo_rows - base, tiles).reshape(row_count, query_width)

    partial_value = jnp.dot(att, out_weight, preferred_element_type=jnp.float32).astype(jnp.bfloat16)
    n_head = lax.axis_size("head")
    got = swap_parts(partial_value, n_head)
    return jnp.sum(got.astype(jnp.float32), axis=0).astype(jnp.bfloat16)


def solution(mesh):
    in_specs = (
        P("ctx", "head"),
        P("ctx", "head"),
        P("ctx", "head"),
        P(),
        P("ctx"),
        P(),
        P(),
        P("head", None),
    )
    out_specs = P("ctx", "head")
    return jax.shard_map(
        on_device, mesh=mesh, in_specs=in_specs, out_specs=out_specs, check_vma=False
    )
```

```python
import functools

import jax
import jax.numpy as jnp
from jax import lax
from jax.experimental import pallas as pl
from jax.experimental.pallas import tpu as pltpu
from jax.sharding import PartitionSpec as P

HD = 128
BLK = 8
TQ = 1024
TK = 512
SHARD = 256
NEG_FILL = -1e30
LONGEST = 4352
PLANE = 4


def attn_kernel(plane, slots, tiles_ref, q_ref, kv_ref, qpos_ref, lo_ref, o_ref, m_sc, l_sc, acc_sc):
    n_q = q_ref.shape[0] // TQ
    scale = HD ** (-0.5)

    def q_body(qi, carry):
        r0 = pl.multiple_of(qi * TQ, TQ)
        q = q_ref[pl.ds(r0, TQ), :]
        qpos = qpos_ref[:, pl.ds(r0, TQ)]
        lo = lo_ref[:, pl.ds(r0, TQ)]
        m_sc[...] = jnp.full(m_sc.shape, NEG_FILL, jnp.float32)
        l_sc[...] = jnp.zeros(l_sc.shape, jnp.float32)
        acc_sc[...] = jnp.zeros(acc_sc.shape, jnp.float32)

        def k_step(kj, masked):
            c0 = pl.multiple_of(kj * TK, TK)
            at = []
            for piece in range(TK // SHARD):
                i = kj * (TK // SHARD) + piece
                at.append(pl.multiple_of((lax.rem(i, plane) * slots + i // plane) * SHARD, SHARD))
            s = jnp.concatenate([
                lax.dot_general(
                    kv_ref[pl.ds(a, SHARD), pl.ds(0, HD)], q, (((1,), (1,)), ((), ())),
                    preferred_element_type=jnp.float32,
                )
                for a in at
            ], axis=0) * scale
            if masked:
                kpos = c0 + lax.broadcasted_iota(jnp.int32, (TK, TQ), 0)
                ok = (kpos >= lo) & (kpos <= qpos)
                s = jnp.where(ok, s, NEG_FILL)
            m_prev = m_sc[...]
            m_new = jnp.maximum(m_prev, jnp.max(s, axis=0, keepdims=True))
            p = jnp.exp(s - m_new)
            if masked:
                p = jnp.where(ok, p, 0.0)
            fade = jnp.exp(m_prev - m_new)
            l_sc[...] = l_sc[...] * fade + jnp.sum(p, axis=0, keepdims=True)
            pb = p.astype(jnp.bfloat16)
            update = acc_sc[...] * fade
            for piece, a in enumerate(at):
                update = update + lax.dot_general(
                    kv_ref[pl.ds(a, SHARD), pl.ds(HD, HD)], pb[piece * SHARD:(piece + 1) * SHARD],
                    (((0,), (0,)), ((), ())), preferred_element_type=jnp.float32,
                )
            acc_sc[...] = update
            m_sc[...] = m_new

        def masked_body(kj, c):
            k_step(kj, True)
            return c

        def open_body(kj, c):
            k_step(kj, False)
            return c

        lax.fori_loop(tiles_ref[qi, 0], tiles_ref[qi, 1], masked_body, 0)
        lax.fori_loop(tiles_ref[qi, 1], tiles_ref[qi, 2], open_body, 0)
        lax.fori_loop(tiles_ref[qi, 2], tiles_ref[qi, 3], masked_body, 0)
        o_ref[pl.ds(r0, TQ), :] = (acc_sc[...] / l_sc[...]).T.astype(o_ref.dtype)
        return carry

    lax.fori_loop(0, n_q, q_body, 0)


def attend(q_rows, kv_all, qpos_rows, lo_rows, tiles, plane, slots):
    rows = q_rows.shape[0]
    vmem = pltpu.MemorySpace.VMEM if hasattr(pltpu, "MemorySpace") else pltpu.VMEM
    return pl.pallas_call(
        functools.partial(attn_kernel, plane, slots),
        out_shape=jax.ShapeDtypeStruct((rows, HD), jnp.bfloat16),
        in_specs=[
            pl.BlockSpec(memory_space=pltpu.SMEM),
            pl.BlockSpec(memory_space=vmem),
            pl.BlockSpec(memory_space=vmem),
            pl.BlockSpec(memory_space=vmem),
            pl.BlockSpec(memory_space=vmem),
        ],
        out_specs=pl.BlockSpec(memory_space=vmem),
        scratch_shapes=[
            pltpu.VMEM((1, TQ), jnp.float32),
            pltpu.VMEM((1, TQ), jnp.float32),
            pltpu.VMEM((HD, TQ), jnp.float32),
        ],
    )(tiles, q_rows, kv_all, qpos_rows, lo_rows)


MESH_ID = pl.DeviceIdType.MESH


def window_kernel(depth, plane, n_ctx, need_col, kv_ref, zero_ref, win_ref, send1, recv1, send2, recv2, local_sem):
    del zero_ref
    me = lax.axis_index("ctx")
    h = lax.axis_index("head")
    z = me // plane
    r = me % plane
    n_z = n_ctx // plane
    mate = r + 1 - 2 * (r % 2)
    across = (r + 2) % plane
    far = across + 1 - 2 * (across % 2)
    barrier = pltpu.get_barrier_semaphore()
    for d in range(1, depth + 1):
        @pl.when(z + d < n_z)
        def _():
            pl.semaphore_signal(barrier, 1, device_id=(me + d * plane, h), device_id_type=MESH_ID)

        @pl.when(z - d >= 0)
        def _():
            pl.semaphore_signal(barrier, 1, device_id=(me - d * plane, h), device_id_type=MESH_ID)

    for peer in (mate, across):
        pl.semaphore_signal(barrier, 1, device_id=(z * plane + peer, h), device_id_type=MESH_ID)
    pl.semaphore_wait(barrier, jnp.minimum(depth, n_z - 1 - z) + jnp.minimum(depth, z) + 2)
    local = pltpu.make_async_copy(kv_ref, win_ref.at[r, depth], local_sem)
    local.start()

    def wanted(d):
        return (d < depth) | (r >= need_col)

    def down(d):
        return pltpu.make_async_remote_copy(
            src_ref=kv_ref,
            dst_ref=win_ref.at[r, depth - d],
            send_sem=send1.at[d - 1],
            recv_sem=recv1.at[d - 1],
            device_id=(me + d * plane, h),
            device_id_type=MESH_ID,
        )

    for d in range(1, depth + 1):
        @pl.when((z + d < n_z) & wanted(d))
        def _():
            down(d).start()

    def has(slot, col):
        return (z - (depth - slot) >= 0) & ((slot > 0) | (col >= need_col))

    def hop(idx, col, slot, to):
        return pltpu.make_async_remote_copy(
            src_ref=win_ref.at[col, slot],
            dst_ref=win_ref.at[col, slot],
            send_sem=send2.at[idx, slot],
            recv_sem=recv2.at[idx, slot],
            device_id=(z * plane + to, h),
            device_id_type=MESH_ID,
        )

    local.wait()
    hop(0, r, depth, mate).start()
    hop(1, r, depth, across).start()
    for d in range(1, depth + 1):
        @pl.when((z + d < n_z) & wanted(d))
        def _():
            down(d).wait_send()

        @pl.when((z - d >= 0) & wanted(d))
        def _():
            down(d).wait_recv()
            hop(0, r, depth - d, mate).start()
            hop(1, r, depth - d, across).start()

    for slot in range(depth, -1, -1):
        @pl.when(has(slot, across))
        def _():
            hop(1, across, slot, across).wait_recv()
            hop(2, across, slot, mate).start()

    for slot in range(depth + 1):
        @pl.when(has(slot, r))
        def _():
            hop(0, r, slot, mate).wait_send()
            hop(1, r, slot, across).wait_send()

        @pl.when(has(slot, across))
        def _():
            hop(2, across, slot, mate).wait_send()

        @pl.when(has(slot, mate))
        def _():
            hop(0, mate, slot, mate).wait_recv()

        @pl.when(has(slot, far))
        def _():
            hop(2, far, slot, mate).wait_recv()


def gather_window(kv_local, depth, plane, n_ctx, need_col):
    rows, width = kv_local.shape
    zero = jnp.zeros((plane, depth + 1, rows, width), kv_local.dtype)
    return pl.pallas_call(
        functools.partial(window_kernel, depth, plane, n_ctx, need_col),
        out_shape=jax.ShapeDtypeStruct(zero.shape, zero.dtype),
        in_specs=[pl.BlockSpec(memory_space=pl.ANY), pl.BlockSpec(memory_space=pl.ANY)],
        out_specs=pl.BlockSpec(memory_space=pl.ANY),
        scratch_shapes=[
            pltpu.SemaphoreType.DMA((depth,)),
            pltpu.SemaphoreType.DMA((depth,)),
            pltpu.SemaphoreType.DMA((3, depth + 1)),
            pltpu.SemaphoreType.DMA((3, depth + 1)),
            pltpu.SemaphoreType.DMA(()),
        ],
        input_output_aliases={1: 0},
        compiler_params=pltpu.CompilerParams(collective_id=0, has_side_effects=True),
    )(kv_local, zero)


def project_kernel(n_head, att_ref, w_ref, o_ref, send_buf, got, send_sem, recv_sem):
    me = lax.axis_index("head")
    row = lax.axis_index("ctx")
    cols = o_ref.shape[1]
    barrier = pltpu.get_barrier_semaphore()
    for d in range(1, n_head):
        pl.semaphore_signal(
            barrier, 1, device_id=(row, lax.rem(me + d, n_head)), device_id_type=MESH_ID
        )
    pl.semaphore_wait(barrier, n_head - 1)

    def part(dst):
        c0 = pl.multiple_of(dst * cols, cols)
        return jnp.dot(
            att_ref[...], w_ref[:, pl.ds(c0, cols)], preferred_element_type=jnp.float32
        ).astype(jnp.bfloat16)

    def send(d):
        dst = lax.rem(me + d, n_head)
        return pltpu.make_async_remote_copy(
            src_ref=send_buf.at[d - 1],
            dst_ref=got.at[me],
            send_sem=send_sem.at[d - 1],
            recv_sem=recv_sem.at[d - 1],
            device_id=(row, dst),
            device_id_type=MESH_ID,
        )

    def arrival(d):
        src = lax.rem(me + n_head - d, n_head)
        return pltpu.make_async_remote_copy(
            src_ref=send_buf.at[d - 1],
            dst_ref=got.at[src],
            send_sem=send_sem.at[d - 1],
            recv_sem=recv_sem.at[d - 1],
            device_id=(row, src),
            device_id_type=MESH_ID,
        )

    send_buf[0] = part(lax.rem(me + 1, n_head))
    for d in range(1, n_head):
        if d + 1 < n_head:
            send_buf[d] = part(lax.rem(me + d + 1, n_head))
        send(d).start()
    total = part(me).astype(jnp.float32)
    for d in range(1, n_head):
        send(d).wait_send()
        arrival(d).wait_recv()
        total = total + got[lax.rem(me + n_head - d, n_head)].astype(jnp.float32)
    o_ref[...] = total.astype(o_ref.dtype)


def project(att, out_weight, n_head):
    rows = att.shape[0]
    cols = out_weight.shape[1] // n_head
    vmem = pltpu.MemorySpace.VMEM if hasattr(pltpu, "MemorySpace") else pltpu.VMEM
    return pl.pallas_call(
        functools.partial(project_kernel, n_head),
        out_shape=jax.ShapeDtypeStruct((rows, cols), jnp.bfloat16),
        in_specs=[pl.BlockSpec(memory_space=vmem), pl.BlockSpec(memory_space=vmem)],
        out_specs=pl.BlockSpec(memory_space=vmem),
        scratch_shapes=[
            pltpu.VMEM((n_head - 1, rows, cols), jnp.bfloat16),
            pltpu.VMEM((n_head, rows, cols), jnp.bfloat16),
            pltpu.SemaphoreType.DMA((n_head - 1,)),
            pltpu.SemaphoreType.DMA((n_head - 1,)),
        ],
        compiler_params=pltpu.CompilerParams(collective_id=1, has_side_effects=True),
    )(att, out_weight)


def on_device(queries, key_rows, values, lengths, block_plan, inverse, mask_lo, out_weight):
    row_count, query_width = queries.shape
    group_size = query_width // HD
    here = lax.axis_index("ctx")
    first = here * row_count
    pos = first + jnp.arange(row_count, dtype=jnp.int32)
    doc_ends = jnp.cumsum(lengths).astype(jnp.int32)
    doc_start = jnp.max(jnp.where(doc_ends[None, :] <= pos[:, None], doc_ends[None, :], 0), axis=1)
    block_lo = lax.dynamic_slice_in_dim(mask_lo, here * (row_count // BLK), row_count // BLK)
    lo_tok = jnp.maximum(jnp.repeat(block_lo, BLK) * BLK, doc_start)
    qpos_rows = jnp.repeat(pos, group_size)[None, :]
    lo_rows = jnp.repeat(lo_tok, group_size)[None, :]
    tok_per_tile = TQ // group_size
    tile_lo = jnp.min(lo_tok.reshape(-1, tok_per_tile), axis=1)
    tile_hi = pos.reshape(-1, tok_per_tile)[:, -1]
    tile_lo_max = jnp.max(lo_tok.reshape(-1, tok_per_tile), axis=1)
    tile_hi_min = pos.reshape(-1, tok_per_tile)[:, 0]

    kv_local = jnp.concatenate([key_rows, values], axis=1)
    n_ctx = lax.axis_size("ctx")
    plane = PLANE
    depth = min(n_ctx // plane - 1, -(-(LONGEST - 1) // (plane * row_count)))
    need_col = max(0, -(-(plane * row_count * depth - (LONGEST - 1) - (row_count - 1)) // row_count))
    kv_win = gather_window(kv_local, depth, plane, n_ctx, need_col)
    kv_win = kv_win.reshape(-1, kv_win.shape[-1])
    base = (here // plane - depth) * plane * row_count
    span = kv_win.shape[0]
    t0 = (tile_lo - base) // TK
    t3 = jnp.minimum((tile_hi - base) // TK + 1, span // TK)
    t1 = jnp.clip((tile_lo_max - base + TK - 1) // TK, t0, t3)
    t2 = jnp.clip((tile_hi_min - base + 1) // TK, t1, t3)
    tiles = jnp.stack([t0, t1, t2, t3], axis=1).astype(jnp.int32)
    q_rows = queries.reshape(row_count * group_size, HD)
    att = attend(q_rows, kv_win, qpos_rows - base, lo_rows - base, tiles, plane, depth + 1).reshape(row_count, query_width)

    return project(att, out_weight, lax.axis_size("head"))


def solution(mesh):
    in_specs = (
        P("ctx", "head"),
        P("ctx", "head"),
        P("ctx", "head"),
        P(),
        P("ctx"),
        P(),
        P(),
        P("head", None),
    )
    out_specs = P("ctx", "head")
    return jax.shard_map(
        on_device, mesh=mesh, in_specs=in_specs, out_specs=out_specs, check_vma=False
    )
```

```python
import functools

import jax
import jax.numpy as jnp
from jax import lax
from jax.experimental import pallas as pl
from jax.experimental.pallas import tpu as pltpu
from jax.sharding import PartitionSpec as P

HD = 128
BLK = 8
TQ = 1024
TK = 512
SHARD = 256
NEG_FILL = -1e30
LONGEST = 4352
PLANE = 4


def attn_kernel(plane, slots, tiles_ref, q_ref, kv_ref, qpos_ref, lo_ref, o_ref, m_sc, l_sc, acc_sc):
    n_q = q_ref.shape[0] // TQ
    scale = HD ** (-0.5)

    def q_body(qi, carry):
        r0 = pl.multiple_of(qi * TQ, TQ)
        q = q_ref[pl.ds(r0, TQ), :]
        qpos = qpos_ref[:, pl.ds(r0, TQ)]
        lo = lo_ref[:, pl.ds(r0, TQ)]
        m_sc[...] = jnp.full(m_sc.shape, NEG_FILL, jnp.float32)
        l_sc[...] = jnp.zeros(l_sc.shape, jnp.float32)
        acc_sc[...] = jnp.zeros(acc_sc.shape, jnp.float32)

        def k_step(kj, masked):
            c0 = pl.multiple_of(kj * TK, TK)
            at = []
            for piece in range(TK // SHARD):
                i = kj * (TK // SHARD) + piece
                at.append(pl.multiple_of((lax.rem(i, plane) * slots + i // plane) * SHARD, SHARD))
            s = jnp.concatenate([
                lax.dot_general(
                    kv_ref[pl.ds(a, SHARD), pl.ds(0, HD)], q, (((1,), (1,)), ((), ())),
                    preferred_element_type=jnp.float32,
                )
                for a in at
            ], axis=0) * scale
            if masked:
                kpos = c0 + lax.broadcasted_iota(jnp.int32, (TK, TQ), 0)
                ok = (kpos >= lo) & (kpos <= qpos)
                s = jnp.where(ok, s, NEG_FILL)
            m_prev = m_sc[...]
            m_new = jnp.maximum(m_prev, jnp.max(s, axis=0, keepdims=True))
            p = jnp.exp(s - m_new)
            if masked:
                p = jnp.where(ok, p, 0.0)
            fade = jnp.exp(m_prev - m_new)
            l_sc[...] = l_sc[...] * fade + jnp.sum(p, axis=0, keepdims=True)
            pb = p.astype(jnp.bfloat16)
            update = acc_sc[...] * fade
            for piece, a in enumerate(at):
                update = update + lax.dot_general(
                    kv_ref[pl.ds(a, SHARD), pl.ds(HD, HD)], pb[piece * SHARD:(piece + 1) * SHARD],
                    (((0,), (0,)), ((), ())), preferred_element_type=jnp.float32,
                )
            acc_sc[...] = update
            m_sc[...] = m_new

        def masked_body(kj, c):
            k_step(kj, True)
            return c

        def open_body(kj, c):
            k_step(kj, False)
            return c

        lax.fori_loop(tiles_ref[qi, 0], tiles_ref[qi, 1], masked_body, 0)
        lax.fori_loop(tiles_ref[qi, 1], tiles_ref[qi, 2], open_body, 0)
        lax.fori_loop(tiles_ref[qi, 2], tiles_ref[qi, 3], masked_body, 0)
        o_ref[pl.ds(r0, TQ), :] = (acc_sc[...] / l_sc[...]).T.astype(o_ref.dtype)
        return carry

    lax.fori_loop(0, n_q, q_body, 0)


def attend(q_rows, kv_all, qpos_rows, lo_rows, tiles, plane, slots):
    rows = q_rows.shape[0]
    vmem = pltpu.MemorySpace.VMEM if hasattr(pltpu, "MemorySpace") else pltpu.VMEM
    return pl.pallas_call(
        functools.partial(attn_kernel, plane, slots),
        out_shape=jax.ShapeDtypeStruct((rows, HD), jnp.bfloat16),
        in_specs=[
            pl.BlockSpec(memory_space=pltpu.SMEM),
            pl.BlockSpec(memory_space=vmem),
            pl.BlockSpec(memory_space=vmem),
            pl.BlockSpec(memory_space=vmem),
            pl.BlockSpec(memory_space=vmem),
        ],
        out_specs=pl.BlockSpec(memory_space=vmem),
        scratch_shapes=[
            pltpu.VMEM((1, TQ), jnp.float32),
            pltpu.VMEM((1, TQ), jnp.float32),
            pltpu.VMEM((HD, TQ), jnp.float32),
        ],
    )(tiles, q_rows, kv_all, qpos_rows, lo_rows)


MESH_ID = pl.DeviceIdType.MESH


def window_kernel(depth, plane, n_ctx, need_col, kv_ref, zero_ref, win_ref, send1, recv1, send2, recv2, local_sem):
    del zero_ref
    me = lax.axis_index("ctx")
    h = lax.axis_index("head")
    z = me // plane
    r = me % plane
    n_z = n_ctx // plane
    mate = r + 1 - 2 * (r % 2)
    across = (r + 2) % plane
    far = across + 1 - 2 * (across % 2)
    barrier = pltpu.get_barrier_semaphore()
    for d in range(1, depth + 1):
        @pl.when(z + d < n_z)
        def _():
            pl.semaphore_signal(barrier, 1, device_id=(me + d * plane, h), device_id_type=MESH_ID)

        @pl.when(z - d >= 0)
        def _():
            pl.semaphore_signal(barrier, 1, device_id=(me - d * plane, h), device_id_type=MESH_ID)

    for peer in (mate, across):
        pl.semaphore_signal(barrier, 1, device_id=(z * plane + peer, h), device_id_type=MESH_ID)
    pl.semaphore_wait(barrier, jnp.minimum(depth, n_z - 1 - z) + jnp.minimum(depth, z) + 2)
    local = pltpu.make_async_copy(kv_ref, win_ref.at[r, depth], local_sem)
    local.start()

    def wanted(d):
        return (d < depth) | (r >= need_col)

    def down(d):
        return pltpu.make_async_remote_copy(
            src_ref=kv_ref,
            dst_ref=win_ref.at[r, depth - d],
            send_sem=send1.at[d - 1],
            recv_sem=recv1.at[d - 1],
            device_id=(me + d * plane, h),
            device_id_type=MESH_ID,
        )

    for d in range(1, depth + 1):
        @pl.when((z + d < n_z) & wanted(d))
        def _():
            down(d).start()

    def has(slot, col):
        return (z - (depth - slot) >= 0) & ((slot > 0) | (col >= need_col))

    def hop(idx, col, slot, to):
        return pltpu.make_async_remote_copy(
            src_ref=win_ref.at[col, slot],
            dst_ref=win_ref.at[col, slot],
            send_sem=send2.at[idx, slot],
            recv_sem=recv2.at[idx, slot],
            device_id=(z * plane + to, h),
            device_id_type=MESH_ID,
        )

    local.wait()
    hop(0, r, depth, mate).start()
    hop(1, r, depth, across).start()
    for d in range(1, depth + 1):
        @pl.when((z + d < n_z) & wanted(d))
        def _():
            down(d).wait_send()

        @pl.when((z - d >= 0) & wanted(d))
        def _():
            down(d).wait_recv()
            hop(0, r, depth - d, mate).start()
            hop(1, r, depth - d, across).start()

    for slot in range(depth, -1, -1):
        @pl.when(has(slot, across))
        def _():
            hop(1, across, slot, across).wait_recv()
            hop(2, across, slot, mate).start()

    for slot in range(depth + 1):
        @pl.when(has(slot, r))
        def _():
            hop(0, r, slot, mate).wait_send()
            hop(1, r, slot, across).wait_send()

        @pl.when(has(slot, across))
        def _():
            hop(2, across, slot, mate).wait_send()

        @pl.when(has(slot, mate))
        def _():
            hop(0, mate, slot, mate).wait_recv()

        @pl.when(has(slot, far))
        def _():
            hop(2, far, slot, mate).wait_recv()


def gather_window(kv_local, depth, plane, n_ctx, need_col):
    rows, width = kv_local.shape
    zero = jnp.zeros((plane, depth + 1, rows, width), kv_local.dtype)
    return pl.pallas_call(
        functools.partial(window_kernel, depth, plane, n_ctx, need_col),
        out_shape=jax.ShapeDtypeStruct(zero.shape, zero.dtype),
        in_specs=[pl.BlockSpec(memory_space=pl.ANY), pl.BlockSpec(memory_space=pl.ANY)],
        out_specs=pl.BlockSpec(memory_space=pl.ANY),
        scratch_shapes=[
            pltpu.SemaphoreType.DMA((depth,)),
            pltpu.SemaphoreType.DMA((depth,)),
            pltpu.SemaphoreType.DMA((3, depth + 1)),
            pltpu.SemaphoreType.DMA((3, depth + 1)),
            pltpu.SemaphoreType.DMA(()),
        ],
        input_output_aliases={1: 0},
        compiler_params=pltpu.CompilerParams(collective_id=0, has_side_effects=True),
    )(kv_local, zero)


def window_attend_kernel(depth, plane, n_ctx, need_col, kv_ref, q_ref, qpos_ref, lo_ref, o_ref,
                         win, send1, recv1, send2, recv2, local_sem, m_sc, l_sc, acc_sc):
    me = lax.axis_index("ctx")
    h = lax.axis_index("head")
    z = me // plane
    r = me % plane
    n_z = n_ctx // plane
    slots = depth + 1
    mate = r + 1 - 2 * (r % 2)
    across = (r + 2) % plane
    far = across + 1 - 2 * (across % 2)
    rows = kv_ref.shape[0]
    tq = q_ref.shape[0] // 2
    scale = HD ** (-0.5)

    def wanted(d):
        return (d < depth) | (r >= need_col)

    def has(slot, col):
        return (z - (depth - slot) >= 0) & ((slot > 0) | (col >= need_col))

    for col in range(plane):
        for slot in range(slots):
            @pl.when(jnp.logical_not(has(slot, col)))
            def _():
                win[col, slot] = jnp.zeros(win.shape[2:], win.dtype)

    barrier = pltpu.get_barrier_semaphore()
    for d in range(1, depth + 1):
        @pl.when(z + d < n_z)
        def _():
            pl.semaphore_signal(barrier, 1, device_id=(me + d * plane, h), device_id_type=MESH_ID)

        @pl.when(z - d >= 0)
        def _():
            pl.semaphore_signal(barrier, 1, device_id=(me - d * plane, h), device_id_type=MESH_ID)

    for peer in (mate, across):
        pl.semaphore_signal(barrier, 1, device_id=(z * plane + peer, h), device_id_type=MESH_ID)
    pl.semaphore_wait(barrier, jnp.minimum(depth, n_z - 1 - z) + jnp.minimum(depth, z) + 2)
    local = pltpu.make_async_copy(kv_ref, win.at[r, depth], local_sem)
    local.start()

    def down(d):
        return pltpu.make_async_remote_copy(
            src_ref=kv_ref,
            dst_ref=win.at[r, depth - d],
            send_sem=send1.at[d - 1],
            recv_sem=recv1.at[d - 1],
            device_id=(me + d * plane, h),
            device_id_type=MESH_ID,
        )

    for d in range(1, depth + 1):
        @pl.when((z + d < n_z) & wanted(d))
        def _():
            down(d).start()

    def hop(idx, col, slot, to):
        return pltpu.make_async_remote_copy(
            src_ref=win.at[col, slot],
            dst_ref=win.at[col, slot],
            send_sem=send2.at[idx, slot],
            recv_sem=recv2.at[idx, slot],
            device_id=(z * plane + to, h),
            device_id_type=MESH_ID,
        )

    m_sc[...] = jnp.full(m_sc.shape, NEG_FILL, jnp.float32)
    l_sc[...] = jnp.zeros(l_sc.shape, jnp.float32)
    acc_sc[...] = jnp.zeros(acc_sc.shape, jnp.float32)
    first_shard = (r * rows + plane * rows * depth - (LONGEST - 1)) // rows
    last_shard = plane * depth + r

    def tile_step(j, carry, slot):
        half = j // 2
        qt = j % 2
        i0 = slot * plane + 2 * half

        @pl.when((i0 + 1 >= first_shard) & (i0 <= last_shard))
        def _():
            r0 = pl.multiple_of(qt * tq, tq)
            q = q_ref[pl.ds(r0, tq), :]
            qpos = qpos_ref[:, pl.ds(r0, tq)]
            lo = lo_ref[:, pl.ds(r0, tq)]
            k0 = win[2 * half, slot, :, pl.ds(0, HD)]
            k1 = win[2 * half + 1, slot, :, pl.ds(0, HD)]
            s = jnp.concatenate([
                lax.dot_general(k, q, (((1,), (1,)), ((), ())), preferred_element_type=jnp.float32)
                for k in (k0, k1)
            ], axis=0) * scale
            kpos = i0 * rows + lax.broadcasted_iota(jnp.int32, s.shape, 0)
            ok = (kpos >= lo) & (kpos <= qpos)
            s = jnp.where(ok, s, NEG_FILL)
            m_prev = m_sc[:, pl.ds(r0, tq)]
            m_new = jnp.maximum(m_prev, jnp.max(s, axis=0, keepdims=True))
            p = jnp.where(ok, jnp.exp(s - m_new), 0.0)
            fade = jnp.exp(m_prev - m_new)
            l_sc[:, pl.ds(r0, tq)] = l_sc[:, pl.ds(r0, tq)] * fade + jnp.sum(p, axis=0, keepdims=True)
            pb = p.astype(jnp.bfloat16)
            update = acc_sc[:, pl.ds(r0, tq)] * fade
            for piece in range(2):
                v = win[2 * half + piece, slot, :, pl.ds(HD, HD)]
                update = update + lax.dot_general(
                    v, pb[piece * rows:(piece + 1) * rows], (((0,), (0,)), ((), ())),
                    preferred_element_type=jnp.float32,
                )
            acc_sc[:, pl.ds(r0, tq)] = update
            m_sc[:, pl.ds(r0, tq)] = m_new

        return carry

    local.wait()
    hop(0, r, depth, mate).start()
    hop(1, r, depth, across).start()
    for slot in range(depth, -1, -1):
        d = depth - slot
        if d > 0:
            @pl.when((z - d >= 0) & wanted(d))
            def _():
                down(d).wait_recv()
                hop(0, r, slot, mate).start()
                hop(1, r, slot, across).start()

        @pl.when(has(slot, across))
        def _():
            hop(1, across, slot, across).wait_recv()
            hop(2, across, slot, mate).start()

        @pl.when(has(slot, mate))
        def _():
            hop(0, mate, slot, mate).wait_recv()

        @pl.when(has(slot, far))
        def _():
            hop(2, far, slot, mate).wait_recv()

        lax.fori_loop(0, plane, functools.partial(tile_step, slot=slot), 0)

    for d in range(1, depth + 1):
        @pl.when((z + d < n_z) & wanted(d))
        def _():
            down(d).wait_send()

    for slot in range(slots):
        @pl.when(has(slot, r))
        def _():
            hop(0, r, slot, mate).wait_send()
            hop(1, r, slot, across).wait_send()

        @pl.when(has(slot, across))
        def _():
            hop(2, across, slot, mate).wait_send()

    o_ref[...] = (acc_sc[...] / l_sc[...]).T.astype(o_ref.dtype)


def window_attend(kv_local, q_rows, qpos_rows, lo_rows, depth, plane, n_ctx, need_col):
    rows, width = kv_local.shape
    n_rows = q_rows.shape[0]
    vmem = pltpu.MemorySpace.VMEM if hasattr(pltpu, "MemorySpace") else pltpu.VMEM
    return pl.pallas_call(
        functools.partial(window_attend_kernel, depth, plane, n_ctx, need_col),
        out_shape=jax.ShapeDtypeStruct((n_rows, HD), jnp.bfloat16),
        in_specs=[pl.BlockSpec(memory_space=vmem)] * 4,
        out_specs=pl.BlockSpec(memory_space=vmem),
        scratch_shapes=[
            pltpu.VMEM((plane, depth + 1, rows, width), kv_local.dtype),
            pltpu.SemaphoreType.DMA((depth,)),
            pltpu.SemaphoreType.DMA((depth,)),
            pltpu.SemaphoreType.DMA((3, depth + 1)),
            pltpu.SemaphoreType.DMA((3, depth + 1)),
            pltpu.SemaphoreType.DMA(()),
            pltpu.VMEM((1, n_rows), jnp.float32),
            pltpu.VMEM((1, n_rows), jnp.float32),
            pltpu.VMEM((HD, n_rows), jnp.float32),
        ],
        compiler_params=pltpu.CompilerParams(collective_id=0, has_side_effects=True),
    )(kv_local, q_rows, qpos_rows, lo_rows)


def project_kernel(n_head, att_ref, w_ref, o_ref, send_buf, got, send_sem, recv_sem):
    me = lax.axis_index("head")
    row = lax.axis_index("ctx")
    cols = o_ref.shape[1]
    barrier = pltpu.get_barrier_semaphore()
    for d in range(1, n_head):
        pl.semaphore_signal(
            barrier, 1, device_id=(row, lax.rem(me + d, n_head)), device_id_type=MESH_ID
        )
    pl.semaphore_wait(barrier, n_head - 1)

    def part(dst):
        c0 = pl.multiple_of(dst * cols, cols)
        return jnp.dot(
            att_ref[...], w_ref[:, pl.ds(c0, cols)], preferred_element_type=jnp.float32
        ).astype(jnp.bfloat16)

    def send(d):
        dst = lax.rem(me + d, n_head)
        return pltpu.make_async_remote_copy(
            src_ref=send_buf.at[d - 1],
            dst_ref=got.at[me],
            send_sem=send_sem.at[d - 1],
            recv_sem=recv_sem.at[d - 1],
            device_id=(row, dst),
            device_id_type=MESH_ID,
        )

    def arrival(d):
        src = lax.rem(me + n_head - d, n_head)
        return pltpu.make_async_remote_copy(
            src_ref=send_buf.at[d - 1],
            dst_ref=got.at[src],
            send_sem=send_sem.at[d - 1],
            recv_sem=recv_sem.at[d - 1],
            device_id=(row, src),
            device_id_type=MESH_ID,
        )

    send_buf[0] = part(lax.rem(me + 1, n_head))
    for d in range(1, n_head):
        if d + 1 < n_head:
            send_buf[d] = part(lax.rem(me + d + 1, n_head))
        send(d).start()
    total = part(me).astype(jnp.float32)
    for d in range(1, n_head):
        send(d).wait_send()
        arrival(d).wait_recv()
        total = total + got[lax.rem(me + n_head - d, n_head)].astype(jnp.float32)
    o_ref[...] = total.astype(o_ref.dtype)


def project(att, out_weight, n_head):
    rows = att.shape[0]
    cols = out_weight.shape[1] // n_head
    vmem = pltpu.MemorySpace.VMEM if hasattr(pltpu, "MemorySpace") else pltpu.VMEM
    return pl.pallas_call(
        functools.partial(project_kernel, n_head),
        out_shape=jax.ShapeDtypeStruct((rows, cols), jnp.bfloat16),
        in_specs=[pl.BlockSpec(memory_space=vmem), pl.BlockSpec(memory_space=vmem)],
        out_specs=pl.BlockSpec(memory_space=vmem),
        scratch_shapes=[
            pltpu.VMEM((n_head - 1, rows, cols), jnp.bfloat16),
            pltpu.VMEM((n_head, rows, cols), jnp.bfloat16),
            pltpu.SemaphoreType.DMA((n_head - 1,)),
            pltpu.SemaphoreType.DMA((n_head - 1,)),
        ],
        compiler_params=pltpu.CompilerParams(collective_id=1, has_side_effects=True),
    )(att, out_weight)


def on_device(queries, key_rows, values, lengths, block_plan, inverse, mask_lo, out_weight):
    row_count, query_width = queries.shape
    group_size = query_width // HD
    here = lax.axis_index("ctx")
    first = here * row_count
    pos = first + jnp.arange(row_count, dtype=jnp.int32)
    doc_ends = jnp.cumsum(lengths).astype(jnp.int32)
    doc_start = jnp.max(jnp.where(doc_ends[None, :] <= pos[:, None], doc_ends[None, :], 0), axis=1)
    block_lo = lax.dynamic_slice_in_dim(mask_lo, here * (row_count // BLK), row_count // BLK)
    lo_tok = jnp.maximum(jnp.repeat(block_lo, BLK) * BLK, doc_start)
    qpos_rows = jnp.repeat(pos, group_size)[None, :]
    lo_rows = jnp.repeat(lo_tok, group_size)[None, :]
    tok_per_tile = TQ // group_size
    tile_lo = jnp.min(lo_tok.reshape(-1, tok_per_tile), axis=1)
    tile_hi = pos.reshape(-1, tok_per_tile)[:, -1]
    tile_lo_max = jnp.max(lo_tok.reshape(-1, tok_per_tile), axis=1)
    tile_hi_min = pos.reshape(-1, tok_per_tile)[:, 0]

    kv_local = jnp.concatenate([key_rows, values], axis=1)
    n_ctx = lax.axis_size("ctx")
    plane = PLANE
    depth = min(n_ctx // plane - 1, -(-(LONGEST - 1) // (plane * row_count)))
    need_col = max(0, -(-(plane * row_count * depth - (LONGEST - 1) - (row_count - 1)) // row_count))
    base = (here // plane - depth) * plane * row_count
    q_rows = queries.reshape(row_count * group_size, HD)
    att = window_attend(
        kv_local, q_rows, qpos_rows - base, lo_rows - base, depth, plane, n_ctx, need_col
    ).reshape(row_count, query_width)

    return project(att, out_weight, lax.axis_size("head"))


def solution(mesh):
    in_specs = (
        P("ctx", "head"),
        P("ctx", "head"),
        P("ctx", "head"),
        P(),
        P("ctx"),
        P(),
        P(),
        P("head", None),
    )
    out_specs = P("ctx", "head")
    return jax.shard_map(
        on_device, mesh=mesh, in_specs=in_specs, out_specs=out_specs, check_vma=False
    )
```

```python
import functools

import jax
import jax.numpy as jnp
from jax import lax
from jax.experimental import pallas as pl
from jax.experimental.pallas import tpu as pltpu
from jax.sharding import PartitionSpec as P

HD = 128
BLK = 8
TQ = 1024
TK = 512
SHARD = 256
NEG_FILL = -1e30
LONGEST = 4352
PLANE = 4


def attn_kernel(plane, slots, tiles_ref, q_ref, kv_ref, qpos_ref, lo_ref, o_ref, m_sc, l_sc, acc_sc):
    n_q = q_ref.shape[0] // TQ
    scale = HD ** (-0.5)

    def q_body(qi, carry):
        r0 = pl.multiple_of(qi * TQ, TQ)
        q = q_ref[pl.ds(r0, TQ), :]
        qpos = qpos_ref[:, pl.ds(r0, TQ)]
        lo = lo_ref[:, pl.ds(r0, TQ)]
        m_sc[...] = jnp.full(m_sc.shape, NEG_FILL, jnp.float32)
        l_sc[...] = jnp.zeros(l_sc.shape, jnp.float32)
        acc_sc[...] = jnp.zeros(acc_sc.shape, jnp.float32)

        def k_step(kj, masked):
            c0 = pl.multiple_of(kj * TK, TK)
            at = []
            for piece in range(TK // SHARD):
                i = kj * (TK // SHARD) + piece
                at.append(pl.multiple_of((lax.rem(i, plane) * slots + i // plane) * SHARD, SHARD))
            s = jnp.concatenate([
                lax.dot_general(
                    kv_ref[pl.ds(a, SHARD), pl.ds(0, HD)], q, (((1,), (1,)), ((), ())),
                    preferred_element_type=jnp.float32,
                )
                for a in at
            ], axis=0) * scale
            if masked:
                kpos = c0 + lax.broadcasted_iota(jnp.int32, (TK, TQ), 0)
                ok = (kpos >= lo) & (kpos <= qpos)
                s = jnp.where(ok, s, NEG_FILL)
            m_prev = m_sc[...]
            m_new = jnp.maximum(m_prev, jnp.max(s, axis=0, keepdims=True))
            p = jnp.exp(s - m_new)
            if masked:
                p = jnp.where(ok, p, 0.0)
            fade = jnp.exp(m_prev - m_new)
            l_sc[...] = l_sc[...] * fade + jnp.sum(p, axis=0, keepdims=True)
            pb = p.astype(jnp.bfloat16)
            update = acc_sc[...] * fade
            for piece, a in enumerate(at):
                update = update + lax.dot_general(
                    kv_ref[pl.ds(a, SHARD), pl.ds(HD, HD)], pb[piece * SHARD:(piece + 1) * SHARD],
                    (((0,), (0,)), ((), ())), preferred_element_type=jnp.float32,
                )
            acc_sc[...] = update
            m_sc[...] = m_new

        def masked_body(kj, c):
            k_step(kj, True)
            return c

        def open_body(kj, c):
            k_step(kj, False)
            return c

        lax.fori_loop(tiles_ref[qi, 0], tiles_ref[qi, 1], masked_body, 0)
        lax.fori_loop(tiles_ref[qi, 1], tiles_ref[qi, 2], open_body, 0)
        lax.fori_loop(tiles_ref[qi, 2], tiles_ref[qi, 3], masked_body, 0)
        o_ref[pl.ds(r0, TQ), :] = (acc_sc[...] / l_sc[...]).T.astype(o_ref.dtype)
        return carry

    lax.fori_loop(0, n_q, q_body, 0)


def attend(q_rows, kv_all, qpos_rows, lo_rows, tiles, plane, slots):
    rows = q_rows.shape[0]
    vmem = pltpu.MemorySpace.VMEM if hasattr(pltpu, "MemorySpace") else pltpu.VMEM
    return pl.pallas_call(
        functools.partial(attn_kernel, plane, slots),
        out_shape=jax.ShapeDtypeStruct((rows, HD), jnp.bfloat16),
        in_specs=[
            pl.BlockSpec(memory_space=pltpu.SMEM),
            pl.BlockSpec(memory_space=vmem),
            pl.BlockSpec(memory_space=vmem),
            pl.BlockSpec(memory_space=vmem),
            pl.BlockSpec(memory_space=vmem),
        ],
        out_specs=pl.BlockSpec(memory_space=vmem),
        scratch_shapes=[
            pltpu.VMEM((1, TQ), jnp.float32),
            pltpu.VMEM((1, TQ), jnp.float32),
            pltpu.VMEM((HD, TQ), jnp.float32),
        ],
    )(tiles, q_rows, kv_all, qpos_rows, lo_rows)


MESH_ID = pl.DeviceIdType.MESH


def window_kernel(depth, plane, n_ctx, need_col, kv_ref, zero_ref, win_ref, send1, recv1, send2, recv2, local_sem):
    del zero_ref
    me = lax.axis_index("ctx")
    h = lax.axis_index("head")
    z = me // plane
    r = me % plane
    n_z = n_ctx // plane
    mate = r + 1 - 2 * (r % 2)
    across = (r + 2) % plane
    far = across + 1 - 2 * (across % 2)
    barrier = pltpu.get_barrier_semaphore()

    @pl.when(z + 1 < n_z)
    def _():
        pl.semaphore_signal(barrier, 1, device_id=(me + plane, h), device_id_type=MESH_ID)

    @pl.when(z - 1 >= 0)
    def _():
        pl.semaphore_signal(barrier, 1, device_id=(me - plane, h), device_id_type=MESH_ID)

    for peer in (mate, across):
        pl.semaphore_signal(barrier, 1, device_id=(z * plane + peer, h), device_id_type=MESH_ID)
    pl.semaphore_wait(barrier, jnp.minimum(1, n_z - 1 - z) + jnp.minimum(1, z) + 2)
    local = pltpu.make_async_copy(kv_ref, win_ref.at[r, depth], local_sem)
    local.start()

    def wanted(d):
        return (d < depth) | (r >= need_col)

    def up(k):
        return pltpu.make_async_remote_copy(
            src_ref=kv_ref if k == 1 else win_ref.at[r, depth - k + 1],
            dst_ref=win_ref.at[r, depth - k],
            send_sem=send1.at[k - 1],
            recv_sem=recv1.at[k - 1],
            device_id=(me + plane, h),
            device_id_type=MESH_ID,
        )

    def sends(k):
        return (z + 1 < n_z) & (z - (k - 1) >= 0) & wanted(k)

    def gets(k):
        return (z - k >= 0) & wanted(k)

    @pl.when(sends(1))
    def _():
        up(1).start()

    def has(slot, col):
        return (z - (depth - slot) >= 0) & ((slot > 0) | (col >= need_col))

    def hop(idx, col, slot, to):
        return pltpu.make_async_remote_copy(
            src_ref=win_ref.at[col, slot],
            dst_ref=win_ref.at[col, slot],
            send_sem=send2.at[idx, slot],
            recv_sem=recv2.at[idx, slot],
            device_id=(z * plane + to, h),
            device_id_type=MESH_ID,
        )

    local.wait()
    hop(0, r, depth, mate).start()
    hop(1, r, depth, across).start()
    for k in range(1, depth + 1):
        @pl.when(gets(k))
        def _():
            up(k).wait_recv()
            hop(0, r, depth - k, mate).start()
            hop(1, r, depth - k, across).start()

        if k < depth:
            @pl.when(sends(k + 1))
            def _():
                up(k + 1).start()

    for k in range(1, depth + 1):
        @pl.when(sends(k))
        def _():
            up(k).wait_send()

    for slot in range(depth, -1, -1):
        @pl.when(has(slot, across))
        def _():
            hop(1, across, slot, across).wait_recv()
            hop(2, across, slot, mate).start()

    for slot in range(depth + 1):
        @pl.when(has(slot, r))
        def _():
            hop(0, r, slot, mate).wait_send()
            hop(1, r, slot, across).wait_send()

        @pl.when(has(slot, across))
        def _():
            hop(2, across, slot, mate).wait_send()

        @pl.when(has(slot, mate))
        def _():
            hop(0, mate, slot, mate).wait_recv()

        @pl.when(has(slot, far))
        def _():
            hop(2, far, slot, mate).wait_recv()


def gather_window(kv_local, depth, plane, n_ctx, need_col):
    rows, width = kv_local.shape
    zero = jnp.zeros((plane, depth + 1, rows, width), kv_local.dtype)
    return pl.pallas_call(
        functools.partial(window_kernel, depth, plane, n_ctx, need_col),
        out_shape=jax.ShapeDtypeStruct(zero.shape, zero.dtype),
        in_specs=[pl.BlockSpec(memory_space=pl.ANY), pl.BlockSpec(memory_space=pl.ANY)],
        out_specs=pl.BlockSpec(memory_space=pl.ANY),
        scratch_shapes=[
            pltpu.SemaphoreType.DMA((depth,)),
            pltpu.SemaphoreType.DMA((depth,)),
            pltpu.SemaphoreType.DMA((3, depth + 1)),
            pltpu.SemaphoreType.DMA((3, depth + 1)),
            pltpu.SemaphoreType.DMA(()),
        ],
        input_output_aliases={1: 0},
        compiler_params=pltpu.CompilerParams(collective_id=0, has_side_effects=True),
    )(kv_local, zero)


def project_kernel(n_head, att_ref, w_ref, o_ref, send_buf, got, send_sem, recv_sem):
    me = lax.axis_index("head")
    row = lax.axis_index("ctx")
    cols = o_ref.shape[1]
    barrier = pltpu.get_barrier_semaphore()
    for d in range(1, n_head):
        pl.semaphore_signal(
            barrier, 1, device_id=(row, lax.rem(me + d, n_head)), device_id_type=MESH_ID
        )
    pl.semaphore_wait(barrier, n_head - 1)

    def part(dst):
        c0 = pl.multiple_of(dst * cols, cols)
        return jnp.dot(
            att_ref[...], w_ref[:, pl.ds(c0, cols)], preferred_element_type=jnp.float32
        ).astype(jnp.bfloat16)

    def send(d):
        dst = lax.rem(me + d, n_head)
        return pltpu.make_async_remote_copy(
            src_ref=send_buf.at[d - 1],
            dst_ref=got.at[me],
            send_sem=send_sem.at[d - 1],
            recv_sem=recv_sem.at[d - 1],
            device_id=(row, dst),
            device_id_type=MESH_ID,
        )

    def arrival(d):
        src = lax.rem(me + n_head - d, n_head)
        return pltpu.make_async_remote_copy(
            src_ref=send_buf.at[d - 1],
            dst_ref=got.at[src],
            send_sem=send_sem.at[d - 1],
            recv_sem=recv_sem.at[d - 1],
            device_id=(row, src),
            device_id_type=MESH_ID,
        )

    send_buf[0] = part(lax.rem(me + 1, n_head))
    for d in range(1, n_head):
        if d + 1 < n_head:
            send_buf[d] = part(lax.rem(me + d + 1, n_head))
        send(d).start()
    total = part(me).astype(jnp.float32)
    for d in range(1, n_head):
        send(d).wait_send()
        arrival(d).wait_recv()
        total = total + got[lax.rem(me + n_head - d, n_head)].astype(jnp.float32)
    o_ref[...] = total.astype(o_ref.dtype)


def project(att, out_weight, n_head):
    rows = att.shape[0]
    cols = out_weight.shape[1] // n_head
    vmem = pltpu.MemorySpace.VMEM if hasattr(pltpu, "MemorySpace") else pltpu.VMEM
    return pl.pallas_call(
        functools.partial(project_kernel, n_head),
        out_shape=jax.ShapeDtypeStruct((rows, cols), jnp.bfloat16),
        in_specs=[pl.BlockSpec(memory_space=vmem), pl.BlockSpec(memory_space=vmem)],
        out_specs=pl.BlockSpec(memory_space=vmem),
        scratch_shapes=[
            pltpu.VMEM((n_head - 1, rows, cols), jnp.bfloat16),
            pltpu.VMEM((n_head, rows, cols), jnp.bfloat16),
            pltpu.SemaphoreType.DMA((n_head - 1,)),
            pltpu.SemaphoreType.DMA((n_head - 1,)),
        ],
        compiler_params=pltpu.CompilerParams(collective_id=1, has_side_effects=True),
    )(att, out_weight)


def on_device(queries, key_rows, values, lengths, block_plan, inverse, mask_lo, out_weight):
    row_count, query_width = queries.shape
    group_size = query_width // HD
    here = lax.axis_index("ctx")
    first = here * row_count
    pos = first + jnp.arange(row_count, dtype=jnp.int32)
    doc_ends = jnp.cumsum(lengths).astype(jnp.int32)
    doc_start = jnp.max(jnp.where(doc_ends[None, :] <= pos[:, None], doc_ends[None, :], 0), axis=1)
    block_lo = lax.dynamic_slice_in_dim(mask_lo, here * (row_count // BLK), row_count // BLK)
    lo_tok = jnp.maximum(jnp.repeat(block_lo, BLK) * BLK, doc_start)
    qpos_rows = jnp.repeat(pos, group_size)[None, :]
    lo_rows = jnp.repeat(lo_tok, group_size)[None, :]
    tok_per_tile = TQ // group_size
    tile_lo = jnp.min(lo_tok.reshape(-1, tok_per_tile), axis=1)
    tile_hi = pos.reshape(-1, tok_per_tile)[:, -1]
    tile_lo_max = jnp.max(lo_tok.reshape(-1, tok_per_tile), axis=1)
    tile_hi_min = pos.reshape(-1, tok_per_tile)[:, 0]

    kv_local = jnp.concatenate([key_rows, values], axis=1)
    n_ctx = lax.axis_size("ctx")
    plane = PLANE
    depth = min(n_ctx // plane - 1, -(-(LONGEST - 1) // (plane * row_count)))
    need_col = max(0, -(-(plane * row_count * depth - (LONGEST - 1) - (row_count - 1)) // row_count))
    kv_win = gather_window(kv_local, depth, plane, n_ctx, need_col)
    kv_win = kv_win.reshape(-1, kv_win.shape[-1])
    base = (here // plane - depth) * plane * row_count
    span = kv_win.shape[0]
    t0 = (tile_lo - base) // TK
    t3 = jnp.minimum((tile_hi - base) // TK + 1, span // TK)
    t1 = jnp.clip((tile_lo_max - base + TK - 1) // TK, t0, t3)
    t2 = jnp.clip((tile_hi_min - base + 1) // TK, t1, t3)
    tiles = jnp.stack([t0, t1, t2, t3], axis=1).astype(jnp.int32)
    q_rows = queries.reshape(row_count * group_size, HD)
    att = attend(q_rows, kv_win, qpos_rows - base, lo_rows - base, tiles, plane, depth + 1).reshape(row_count, query_width)

    return project(att, out_weight, lax.axis_size("head"))


def solution(mesh):
    in_specs = (
        P("ctx", "head"),
        P("ctx", "head"),
        P("ctx", "head"),
        P(),
        P("ctx"),
        P(),
        P(),
        P("head", None),
    )
    out_specs = P("ctx", "head")
    return jax.shard_map(
        on_device, mesh=mesh, in_specs=in_specs, out_specs=out_specs, check_vma=False
    )
```

```python
import functools

import jax
import jax.numpy as jnp
from jax import lax
from jax.experimental import pallas as pl
from jax.experimental.pallas import tpu as pltpu
from jax.sharding import PartitionSpec as P

HD = 128
BLK = 8
TQ = 1024
TK = 512
SHARD = 256
NEG_FILL = -1e30
LONGEST = 4352
PLANE = 4


def attn_kernel(plane, slots, tiles_ref, q_ref, kv_ref, qpos_ref, lo_ref, o_ref, m_sc, l_sc, acc_sc):
    n_q = q_ref.shape[0] // TQ
    scale = HD ** (-0.5)

    def q_body(qi, carry):
        r0 = pl.multiple_of(qi * TQ, TQ)
        q = q_ref[pl.ds(r0, TQ), :]
        qpos = qpos_ref[:, pl.ds(r0, TQ)]
        lo = lo_ref[:, pl.ds(r0, TQ)]
        m_sc[...] = jnp.full(m_sc.shape, NEG_FILL, jnp.float32)
        l_sc[...] = jnp.zeros(l_sc.shape, jnp.float32)
        acc_sc[...] = jnp.zeros(acc_sc.shape, jnp.float32)

        def k_step(kj, masked):
            c0 = pl.multiple_of(kj * TK, TK)
            at = []
            for piece in range(TK // SHARD):
                i = kj * (TK // SHARD) + piece
                at.append(pl.multiple_of((lax.rem(i, plane) * slots + i // plane) * SHARD, SHARD))
            s = jnp.concatenate([
                lax.dot_general(
                    kv_ref[pl.ds(a, SHARD), pl.ds(0, HD)], q, (((1,), (1,)), ((), ())),
                    preferred_element_type=jnp.float32,
                )
                for a in at
            ], axis=0) * scale
            if masked:
                kpos = c0 + lax.broadcasted_iota(jnp.int32, (TK, TQ), 0)
                ok = (kpos >= lo) & (kpos <= qpos)
                s = jnp.where(ok, s, NEG_FILL)
            m_prev = m_sc[...]
            m_new = jnp.maximum(m_prev, jnp.max(s, axis=0, keepdims=True))
            p = jnp.exp(s - m_new)
            if masked:
                p = jnp.where(ok, p, 0.0)
            fade = jnp.exp(m_prev - m_new)
            l_sc[...] = l_sc[...] * fade + jnp.sum(p, axis=0, keepdims=True)
            pb = p.astype(jnp.bfloat16)
            update = acc_sc[...] * fade
            for piece, a in enumerate(at):
                update = update + lax.dot_general(
                    kv_ref[pl.ds(a, SHARD), pl.ds(HD, HD)], pb[piece * SHARD:(piece + 1) * SHARD],
                    (((0,), (0,)), ((), ())), preferred_element_type=jnp.float32,
                )
            acc_sc[...] = update
            m_sc[...] = m_new

        def masked_body(kj, c):
            k_step(kj, True)
            return c

        def open_body(kj, c):
            k_step(kj, False)
            return c

        lax.fori_loop(tiles_ref[qi, 0], tiles_ref[qi, 1], masked_body, 0)
        lax.fori_loop(tiles_ref[qi, 1], tiles_ref[qi, 2], open_body, 0)
        lax.fori_loop(tiles_ref[qi, 2], tiles_ref[qi, 3], masked_body, 0)
        o_ref[pl.ds(r0, TQ), :] = (acc_sc[...] / l_sc[...]).T.astype(o_ref.dtype)
        return carry

    lax.fori_loop(0, n_q, q_body, 0)


def attend(q_rows, kv_all, qpos_rows, lo_rows, tiles, plane, slots):
    rows = q_rows.shape[0]
    vmem = pltpu.MemorySpace.VMEM if hasattr(pltpu, "MemorySpace") else pltpu.VMEM
    return pl.pallas_call(
        functools.partial(attn_kernel, plane, slots),
        out_shape=jax.ShapeDtypeStruct((rows, HD), jnp.bfloat16),
        in_specs=[
            pl.BlockSpec(memory_space=pltpu.SMEM),
            pl.BlockSpec(memory_space=vmem),
            pl.BlockSpec(memory_space=vmem),
            pl.BlockSpec(memory_space=vmem),
            pl.BlockSpec(memory_space=vmem),
        ],
        out_specs=pl.BlockSpec(memory_space=vmem),
        scratch_shapes=[
            pltpu.VMEM((1, TQ), jnp.float32),
            pltpu.VMEM((1, TQ), jnp.float32),
            pltpu.VMEM((HD, TQ), jnp.float32),
        ],
    )(tiles, q_rows, kv_all, qpos_rows, lo_rows)


MESH_ID = pl.DeviceIdType.MESH


def window_kernel(depth, plane, n_ctx, need_col, kv_ref, win_ref, send1, recv1, send2, recv2, local_sem):
    me = lax.axis_index("ctx")
    h = lax.axis_index("head")
    z = me // plane
    r = me % plane
    n_z = n_ctx // plane
    mate = r + 1 - 2 * (r % 2)
    across = (r + 2) % plane
    far = across + 1 - 2 * (across % 2)
    barrier = pltpu.get_barrier_semaphore()

    @pl.when(z + 1 < n_z)
    def _():
        pl.semaphore_signal(barrier, 1, device_id=(me + plane, h), device_id_type=MESH_ID)

    @pl.when(z - 1 >= 0)
    def _():
        pl.semaphore_signal(barrier, 1, device_id=(me - plane, h), device_id_type=MESH_ID)

    for peer in (mate, across):
        pl.semaphore_signal(barrier, 1, device_id=(z * plane + peer, h), device_id_type=MESH_ID)
    pl.semaphore_wait(barrier, jnp.minimum(1, n_z - 1 - z) + jnp.minimum(1, z) + 2)
    local = pltpu.make_async_copy(kv_ref, win_ref.at[r, depth], local_sem)
    local.start()

    def wanted(d):
        return (d < depth) | (r >= need_col)

    def up(k):
        return pltpu.make_async_remote_copy(
            src_ref=kv_ref if k == 1 else win_ref.at[r, depth - k + 1],
            dst_ref=win_ref.at[r, depth - k],
            send_sem=send1.at[k - 1],
            recv_sem=recv1.at[k - 1],
            device_id=(me + plane, h),
            device_id_type=MESH_ID,
        )

    def sends(k):
        return (z + 1 < n_z) & (z - (k - 1) >= 0) & wanted(k)

    def gets(k):
        return (z - k >= 0) & wanted(k)

    @pl.when(sends(1))
    def _():
        up(1).start()

    def has(slot, col):
        return (z - (depth - slot) >= 0) & ((slot > 0) | (col >= need_col))

    def hop(idx, col, slot, to):
        return pltpu.make_async_remote_copy(
            src_ref=win_ref.at[col, slot],
            dst_ref=win_ref.at[col, slot],
            send_sem=send2.at[idx, slot],
            recv_sem=recv2.at[idx, slot],
            device_id=(z * plane + to, h),
            device_id_type=MESH_ID,
        )

    local.wait()
    hop(0, r, depth, mate).start()
    hop(1, r, depth, across).start()
    for k in range(1, depth + 1):
        @pl.when(gets(k))
        def _():
            up(k).wait_recv()
            hop(0, r, depth - k, mate).start()
            hop(1, r, depth - k, across).start()

        if k < depth:
            @pl.when(sends(k + 1))
            def _():
                up(k + 1).start()

    for k in range(1, depth + 1):
        @pl.when(sends(k))
        def _():
            up(k).wait_send()

    for slot in range(depth, -1, -1):
        @pl.when(has(slot, across))
        def _():
            hop(1, across, slot, across).wait_recv()
            hop(2, across, slot, mate).start()

    for slot in range(depth + 1):
        @pl.when(has(slot, r))
        def _():
            hop(0, r, slot, mate).wait_send()
            hop(1, r, slot, across).wait_send()

        @pl.when(has(slot, across))
        def _():
            hop(2, across, slot, mate).wait_send()

        @pl.when(has(slot, mate))
        def _():
            hop(0, mate, slot, mate).wait_recv()

        @pl.when(has(slot, far))
        def _():
            hop(2, far, slot, mate).wait_recv()


def gather_window(kv_local, depth, plane, n_ctx, need_col):
    rows, width = kv_local.shape
    return pl.pallas_call(
        functools.partial(window_kernel, depth, plane, n_ctx, need_col),
        out_shape=jax.ShapeDtypeStruct((plane, depth + 1, rows, width), kv_local.dtype),
        in_specs=[pl.BlockSpec(memory_space=pl.ANY)],
        out_specs=pl.BlockSpec(memory_space=pl.ANY),
        scratch_shapes=[
            pltpu.SemaphoreType.DMA((depth,)),
            pltpu.SemaphoreType.DMA((depth,)),
            pltpu.SemaphoreType.DMA((3, depth + 1)),
            pltpu.SemaphoreType.DMA((3, depth + 1)),
            pltpu.SemaphoreType.DMA(()),
        ],
        compiler_params=pltpu.CompilerParams(collective_id=0, has_side_effects=True),
    )(kv_local)


def project_kernel(ny, att_ref, w_ref, o_ref, sbuf, got1, tot, s2buf, got2, send1, recv1, send2, recv2):
    me = lax.axis_index("head")
    row = lax.axis_index("ctx")
    y = me // 2
    xl = me % 2
    other = 1 - xl
    cols = o_ref.shape[1]
    wide = 2 * cols
    barrier = pltpu.get_barrier_semaphore()
    for e in range(1, ny):
        pl.semaphore_signal(
            barrier, 1, device_id=(row, lax.rem(y + e, ny) * 2 + xl), device_id_type=MESH_ID
        )
    pl.semaphore_signal(barrier, 1, device_id=(row, y * 2 + other), device_id_type=MESH_ID)
    pl.semaphore_wait(barrier, ny)

    def part(yy):
        c0 = pl.multiple_of(yy * wide, wide)
        return jnp.dot(
            att_ref[...], w_ref[:, pl.ds(c0, wide)], preferred_element_type=jnp.float32
        ).astype(jnp.bfloat16)

    def send(e):
        return pltpu.make_async_remote_copy(
            src_ref=sbuf.at[e - 1],
            dst_ref=got1.at[y],
            send_sem=send1.at[e - 1],
            recv_sem=recv1.at[e - 1],
            device_id=(row, lax.rem(y + e, ny) * 2 + xl),
            device_id_type=MESH_ID,
        )

    def arrival(e):
        src = lax.rem(y + ny - e, ny)
        return pltpu.make_async_remote_copy(
            src_ref=sbuf.at[e - 1],
            dst_ref=got1.at[src],
            send_sem=send1.at[e - 1],
            recv_sem=recv1.at[e - 1],
            device_id=(row, src * 2 + xl),
            device_id_type=MESH_ID,
        )

    sbuf[0] = part(lax.rem(y + 1, ny))
    for e in range(1, ny):
        if e + 1 < ny:
            sbuf[e] = part(lax.rem(y + e + 1, ny))
        send(e).start()
    total = part(y).astype(jnp.float32)
    for e in range(1, ny):
        send(e).wait_send()
        arrival(e).wait_recv()
        total = total + got1[lax.rem(y + ny - e, ny)].astype(jnp.float32)
    tot[...] = total
    s2buf[...] = tot[:, pl.ds(pl.multiple_of(other * cols, cols), cols)]
    cross = pltpu.make_async_remote_copy(
        src_ref=s2buf,
        dst_ref=got2,
        send_sem=send2,
        recv_sem=recv2,
        device_id=(row, y * 2 + other),
        device_id_type=MESH_ID,
    )
    cross.start()
    cross.wait_send()
    cross.wait_recv()
    o_ref[...] = (
        tot[:, pl.ds(pl.multiple_of(xl * cols, cols), cols)] + got2[...]
    ).astype(o_ref.dtype)


def project(att, out_weight, n_head):
    rows = att.shape[0]
    cols = out_weight.shape[1] // n_head
    ny = n_head // 2
    vmem = pltpu.MemorySpace.VMEM if hasattr(pltpu, "MemorySpace") else pltpu.VMEM
    return pl.pallas_call(
        functools.partial(project_kernel, ny),
        out_shape=jax.ShapeDtypeStruct((rows, cols), jnp.bfloat16),
        in_specs=[pl.BlockSpec(memory_space=vmem), pl.BlockSpec(memory_space=vmem)],
        out_specs=pl.BlockSpec(memory_space=vmem),
        scratch_shapes=[
            pltpu.VMEM((ny - 1, rows, 2 * cols), jnp.bfloat16),
            pltpu.VMEM((ny, rows, 2 * cols), jnp.bfloat16),
            pltpu.VMEM((rows, 2 * cols), jnp.float32),
            pltpu.VMEM((rows, cols), jnp.float32),
            pltpu.VMEM((rows, cols), jnp.float32),
            pltpu.SemaphoreType.DMA((ny - 1,)),
            pltpu.SemaphoreType.DMA((ny - 1,)),
            pltpu.SemaphoreType.DMA(()),
            pltpu.SemaphoreType.DMA(()),
        ],
        compiler_params=pltpu.CompilerParams(collective_id=1, has_side_effects=True),
    )(att, out_weight)


def on_device(queries, key_rows, values, lengths, block_plan, inverse, mask_lo, out_weight):
    row_count, query_width = queries.shape
    group_size = query_width // HD
    here = lax.axis_index("ctx")
    first = here * row_count
    pos = first + jnp.arange(row_count, dtype=jnp.int32)
    doc_ends = jnp.cumsum(lengths).astype(jnp.int32)
    doc_start = jnp.max(jnp.where(doc_ends[None, :] <= pos[:, None], doc_ends[None, :], 0), axis=1)
    block_lo = lax.dynamic_slice_in_dim(mask_lo, here * (row_count // BLK), row_count // BLK)
    lo_tok = jnp.maximum(jnp.repeat(block_lo, BLK) * BLK, doc_start)
    qpos_rows = jnp.repeat(pos, group_size)[None, :]
    lo_rows = jnp.repeat(lo_tok, group_size)[None, :]
    tok_per_tile = TQ // group_size
    tile_lo = jnp.min(lo_tok.reshape(-1, tok_per_tile), axis=1)
    tile_hi = pos.reshape(-1, tok_per_tile)[:, -1]
    tile_lo_max = jnp.max(lo_tok.reshape(-1, tok_per_tile), axis=1)
    tile_hi_min = pos.reshape(-1, tok_per_tile)[:, 0]

    kv_local = jnp.concatenate([key_rows, values], axis=1)
    n_ctx = lax.axis_size("ctx")
    plane = PLANE
    depth = min(n_ctx // plane - 1, -(-(LONGEST - 1) // (plane * row_count)))
    need_col = max(0, -(-(plane * row_count * depth - (LONGEST - 1) - (row_count - 1)) // row_count))
    need_col = need_col // (TK // SHARD) * (TK // SHARD)
    kv_win = gather_window(kv_local, depth, plane, n_ctx, need_col)
    kv_win = kv_win.reshape(-1, kv_win.shape[-1])
    base = (here // plane - depth) * plane * row_count
    span = kv_win.shape[0]
    t0 = (tile_lo - base) // TK
    t3 = jnp.minimum((tile_hi - base) // TK + 1, span // TK)
    t1 = jnp.clip((tile_lo_max - base + TK - 1) // TK, t0, t3)
    t2 = jnp.clip((tile_hi_min - base + 1) // TK, t1, t3)
    tiles = jnp.stack([t0, t1, t2, t3], axis=1).astype(jnp.int32)
    q_rows = queries.reshape(row_count * group_size, HD)
    att = attend(q_rows, kv_win, qpos_rows - base, lo_rows - base, tiles, plane, depth + 1).reshape(row_count, query_width)

    return project(att, out_weight, lax.axis_size("head"))


def solution(mesh):
    in_specs = (
        P("ctx", "head"),
        P("ctx", "head"),
        P("ctx", "head"),
        P(),
        P("ctx"),
        P(),
        P(),
        P("head", None),
    )
    out_specs = P("ctx", "head")
    return jax.shard_map(
        on_device, mesh=mesh, in_specs=in_specs, out_specs=out_specs, check_vma=False
    )
```

```python
import functools

import jax
import jax.numpy as jnp
from jax import lax
from jax.experimental import pallas as pl
from jax.experimental.pallas import tpu as pltpu
from jax.sharding import PartitionSpec as P

HD = 128
BLK = 8
TQ = 1024
TK = 512
SHARD = 256
NEG_FILL = -1e30
LONGEST = 4352
PLANE = 4


def attn_kernel(plane, slots, tiles_ref, q_ref, kv_ref, qpos_ref, lo_ref, o_ref, m_sc, l_sc, acc_sc):
    n_q = q_ref.shape[0] * q_ref.shape[1] // (HD * TQ)
    scale = HD ** (-0.5)

    def q_body(qi, carry):
        r0 = pl.multiple_of(qi * TQ, TQ)
        heads = TQ // q_ref.shape[0]
        q = jnp.concatenate([
            q_ref[:, pl.ds(pl.multiple_of((qi * heads + g) * HD, HD), HD)] for g in range(heads)
        ], axis=0)
        qpos = qpos_ref[:, pl.ds(r0, TQ)]
        lo = lo_ref[:, pl.ds(r0, TQ)]
        m_sc[...] = jnp.full(m_sc.shape, NEG_FILL, jnp.float32)
        l_sc[...] = jnp.zeros(l_sc.shape, jnp.float32)
        acc_sc[...] = jnp.zeros(acc_sc.shape, jnp.float32)

        def k_step(kj, masked):
            c0 = pl.multiple_of(kj * TK, TK)
            at = []
            for piece in range(TK // SHARD):
                i = kj * (TK // SHARD) + piece
                at.append(pl.multiple_of((lax.rem(i, plane) * slots + i // plane) * SHARD, SHARD))
            s = jnp.concatenate([
                lax.dot_general(
                    kv_ref[pl.ds(a, SHARD), pl.ds(0, HD)], q, (((1,), (1,)), ((), ())),
                    preferred_element_type=jnp.float32,
                )
                for a in at
            ], axis=0) * scale
            if masked:
                kpos = c0 + lax.broadcasted_iota(jnp.int32, (TK, TQ), 0)
                ok = (kpos >= lo) & (kpos <= qpos)
                s = jnp.where(ok, s, NEG_FILL)
            m_prev = m_sc[...]
            m_new = jnp.maximum(m_prev, jnp.max(s, axis=0, keepdims=True))
            p = jnp.exp(s - m_new)
            if masked:
                p = jnp.where(ok, p, 0.0)
            fade = jnp.exp(m_prev - m_new)
            l_sc[...] = l_sc[...] * fade + jnp.sum(p, axis=0, keepdims=True)
            pb = p.astype(jnp.bfloat16)
            update = acc_sc[...] * fade
            for piece, a in enumerate(at):
                update = update + lax.dot_general(
                    kv_ref[pl.ds(a, SHARD), pl.ds(HD, HD)], pb[piece * SHARD:(piece + 1) * SHARD],
                    (((0,), (0,)), ((), ())), preferred_element_type=jnp.float32,
                )
            acc_sc[...] = update
            m_sc[...] = m_new

        def masked_body(kj, c):
            k_step(kj, True)
            return c

        def open_body(kj, c):
            k_step(kj, False)
            return c

        lax.fori_loop(tiles_ref[qi, 0], tiles_ref[qi, 1], masked_body, 0)
        lax.fori_loop(tiles_ref[qi, 1], tiles_ref[qi, 2], open_body, 0)
        lax.fori_loop(tiles_ref[qi, 2], tiles_ref[qi, 3], masked_body, 0)
        out = (acc_sc[...] / l_sc[...]).T.astype(o_ref.dtype)
        tokens = q_ref.shape[0]
        for g in range(heads):
            o_ref[:, pl.ds(pl.multiple_of((qi * heads + g) * HD, HD), HD)] = out[g * tokens:(g + 1) * tokens]
        return carry

    lax.fori_loop(0, n_q, q_body, 0)


def attend(q_rows, kv_all, qpos_rows, lo_rows, tiles, plane, slots):
    vmem = pltpu.MemorySpace.VMEM if hasattr(pltpu, "MemorySpace") else pltpu.VMEM
    return pl.pallas_call(
        functools.partial(attn_kernel, plane, slots),
        out_shape=jax.ShapeDtypeStruct(q_rows.shape, jnp.bfloat16),
        in_specs=[
            pl.BlockSpec(memory_space=pltpu.SMEM),
            pl.BlockSpec(memory_space=vmem),
            pl.BlockSpec(memory_space=vmem),
            pl.BlockSpec(memory_space=vmem),
            pl.BlockSpec(memory_space=vmem),
        ],
        out_specs=pl.BlockSpec(memory_space=vmem),
        scratch_shapes=[
            pltpu.VMEM((1, TQ), jnp.float32),
            pltpu.VMEM((1, TQ), jnp.float32),
            pltpu.VMEM((HD, TQ), jnp.float32),
        ],
    )(tiles, q_rows, kv_all, qpos_rows, lo_rows)


MESH_ID = pl.DeviceIdType.MESH


def window_kernel(depth, plane, n_ctx, need_col, kv_ref, zero_ref, win_ref, send1, recv1, send2, recv2, local_sem):
    del zero_ref
    me = lax.axis_index("ctx")
    h = lax.axis_index("head")
    z = me // plane
    r = me % plane
    n_z = n_ctx // plane
    mate = r + 1 - 2 * (r % 2)
    across = (r + 2) % plane
    far = across + 1 - 2 * (across % 2)
    barrier = pltpu.get_barrier_semaphore()

    @pl.when(z + 1 < n_z)
    def _():
        pl.semaphore_signal(barrier, 1, device_id=(me + plane, h), device_id_type=MESH_ID)

    @pl.when(z - 1 >= 0)
    def _():
        pl.semaphore_signal(barrier, 1, device_id=(me - plane, h), device_id_type=MESH_ID)

    for peer in (mate, across):
        pl.semaphore_signal(barrier, 1, device_id=(z * plane + peer, h), device_id_type=MESH_ID)
    pl.semaphore_wait(barrier, jnp.minimum(1, n_z - 1 - z) + jnp.minimum(1, z) + 2)
    local = pltpu.make_async_copy(kv_ref, win_ref.at[r, depth], local_sem)
    local.start()

    def wanted(d):
        return (d < depth) | (r >= need_col)

    def up(k):
        return pltpu.make_async_remote_copy(
            src_ref=kv_ref if k == 1 else win_ref.at[r, depth - k + 1],
            dst_ref=win_ref.at[r, depth - k],
            send_sem=send1.at[k - 1],
            recv_sem=recv1.at[k - 1],
            device_id=(me + plane, h),
            device_id_type=MESH_ID,
        )

    def sends(k):
        return (z + 1 < n_z) & (z - (k - 1) >= 0) & wanted(k)

    def gets(k):
        return (z - k >= 0) & wanted(k)

    @pl.when(sends(1))
    def _():
        up(1).start()

    def has(slot, col):
        return (z - (depth - slot) >= 0) & ((slot > 0) | (col >= need_col))

    def hop(idx, col, slot, to):
        return pltpu.make_async_remote_copy(
            src_ref=win_ref.at[col, slot],
            dst_ref=win_ref.at[col, slot],
            send_sem=send2.at[idx, slot],
            recv_sem=recv2.at[idx, slot],
            device_id=(z * plane + to, h),
            device_id_type=MESH_ID,
        )

    local.wait()
    hop(0, r, depth, mate).start()
    hop(1, r, depth, across).start()
    for k in range(1, depth + 1):
        @pl.when(gets(k))
        def _():
            up(k).wait_recv()
            hop(0, r, depth - k, mate).start()
            hop(1, r, depth - k, across).start()

        if k < depth:
            @pl.when(sends(k + 1))
            def _():
                up(k + 1).start()

    for k in range(1, depth + 1):
        @pl.when(sends(k))
        def _():
            up(k).wait_send()

    for slot in range(depth, -1, -1):
        @pl.when(has(slot, across))
        def _():
            hop(1, across, slot, across).wait_recv()
            hop(2, across, slot, mate).start()

    for slot in range(depth + 1):
        @pl.when(has(slot, r))
        def _():
            hop(0, r, slot, mate).wait_send()
            hop(1, r, slot, across).wait_send()

        @pl.when(has(slot, across))
        def _():
            hop(2, across, slot, mate).wait_send()

        @pl.when(has(slot, mate))
        def _():
            hop(0, mate, slot, mate).wait_recv()

        @pl.when(has(slot, far))
        def _():
            hop(2, far, slot, mate).wait_recv()


def gather_window(kv_local, depth, plane, n_ctx, need_col):
    rows, width = kv_local.shape
    zero = jnp.zeros((plane, depth + 1, rows, width), kv_local.dtype)
    return pl.pallas_call(
        functools.partial(window_kernel, depth, plane, n_ctx, need_col),
        out_shape=jax.ShapeDtypeStruct(zero.shape, zero.dtype),
        in_specs=[pl.BlockSpec(memory_space=pl.ANY), pl.BlockSpec(memory_space=pl.ANY)],
        out_specs=pl.BlockSpec(memory_space=pl.ANY),
        scratch_shapes=[
            pltpu.SemaphoreType.DMA((depth,)),
            pltpu.SemaphoreType.DMA((depth,)),
            pltpu.SemaphoreType.DMA((3, depth + 1)),
            pltpu.SemaphoreType.DMA((3, depth + 1)),
            pltpu.SemaphoreType.DMA(()),
        ],
        input_output_aliases={1: 0},
        compiler_params=pltpu.CompilerParams(collective_id=0, has_side_effects=True),
    )(kv_local, zero)


def project_kernel(n_head, att_ref, w_ref, o_ref, send_buf, got, send_sem, recv_sem):
    me = lax.axis_index("head")
    row = lax.axis_index("ctx")
    cols = o_ref.shape[1]
    barrier = pltpu.get_barrier_semaphore()
    for d in range(1, n_head):
        pl.semaphore_signal(
            barrier, 1, device_id=(row, lax.rem(me + d, n_head)), device_id_type=MESH_ID
        )
    pl.semaphore_wait(barrier, n_head - 1)

    def part(dst):
        c0 = pl.multiple_of(dst * cols, cols)
        return jnp.dot(
            att_ref[...], w_ref[:, pl.ds(c0, cols)], preferred_element_type=jnp.float32
        ).astype(jnp.bfloat16)

    def send(d):
        dst = lax.rem(me + d, n_head)
        return pltpu.make_async_remote_copy(
            src_ref=send_buf.at[d - 1],
            dst_ref=got.at[me],
            send_sem=send_sem.at[d - 1],
            recv_sem=recv_sem.at[d - 1],
            device_id=(row, dst),
            device_id_type=MESH_ID,
        )

    def arrival(d):
        src = lax.rem(me + n_head - d, n_head)
        return pltpu.make_async_remote_copy(
            src_ref=send_buf.at[d - 1],
            dst_ref=got.at[src],
            send_sem=send_sem.at[d - 1],
            recv_sem=recv_sem.at[d - 1],
            device_id=(row, src),
            device_id_type=MESH_ID,
        )

    send_buf[0] = part(lax.rem(me + 1, n_head))
    for d in range(1, n_head):
        if d + 1 < n_head:
            send_buf[d] = part(lax.rem(me + d + 1, n_head))
        send(d).start()
    total = part(me).astype(jnp.float32)
    for d in range(1, n_head):
        send(d).wait_send()
        arrival(d).wait_recv()
        total = total + got[lax.rem(me + n_head - d, n_head)].astype(jnp.float32)
    o_ref[...] = total.astype(o_ref.dtype)


def project(att, out_weight, n_head):
    rows = att.shape[0]
    cols = out_weight.shape[1] // n_head
    vmem = pltpu.MemorySpace.VMEM if hasattr(pltpu, "MemorySpace") else pltpu.VMEM
    return pl.pallas_call(
        functools.partial(project_kernel, n_head),
        out_shape=jax.ShapeDtypeStruct((rows, cols), jnp.bfloat16),
        in_specs=[pl.BlockSpec(memory_space=vmem), pl.BlockSpec(memory_space=vmem)],
        out_specs=pl.BlockSpec(memory_space=vmem),
        scratch_shapes=[
            pltpu.VMEM((n_head - 1, rows, cols), jnp.bfloat16),
            pltpu.VMEM((n_head, rows, cols), jnp.bfloat16),
            pltpu.SemaphoreType.DMA((n_head - 1,)),
            pltpu.SemaphoreType.DMA((n_head - 1,)),
        ],
        compiler_params=pltpu.CompilerParams(collective_id=1, has_side_effects=True),
    )(att, out_weight)


def on_device(queries, key_rows, values, lengths, block_plan, inverse, mask_lo, out_weight):
    row_count, query_width = queries.shape
    group_size = query_width // HD
    here = lax.axis_index("ctx")
    first = here * row_count
    pos = first + jnp.arange(row_count, dtype=jnp.int32)
    doc_ends = jnp.cumsum(lengths).astype(jnp.int32)
    doc_start = jnp.max(jnp.where(doc_ends[None, :] <= pos[:, None], doc_ends[None, :], 0), axis=1)
    block_lo = lax.dynamic_slice_in_dim(mask_lo, here * (row_count // BLK), row_count // BLK)
    lo_tok = jnp.maximum(jnp.repeat(block_lo, BLK) * BLK, doc_start)
    qpos_rows = jnp.tile(pos, group_size)[None, :]
    lo_rows = jnp.tile(lo_tok, group_size)[None, :]
    n_q = row_count * group_size // TQ
    tile_lo = jnp.full((n_q,), jnp.min(lo_tok))
    tile_hi = jnp.full((n_q,), pos[-1])
    tile_lo_max = jnp.full((n_q,), jnp.max(lo_tok))
    tile_hi_min = jnp.full((n_q,), pos[0])

    kv_local = jnp.concatenate([key_rows, values], axis=1)
    n_ctx = lax.axis_size("ctx")
    plane = PLANE
    depth = min(n_ctx // plane - 1, -(-(LONGEST - 1) // (plane * row_count)))
    need_col = max(0, -(-(plane * row_count * depth - (LONGEST - 1) - (row_count - 1)) // row_count))
    kv_win = gather_window(kv_local, depth, plane, n_ctx, need_col)
    kv_win = kv_win.reshape(-1, kv_win.shape[-1])
    base = (here // plane - depth) * plane * row_count
    span = kv_win.shape[0]
    t0 = (tile_lo - base) // TK
    t3 = jnp.minimum((tile_hi - base) // TK + 1, span // TK)
    t1 = jnp.clip((tile_lo_max - base + TK - 1) // TK, t0, t3)
    t2 = jnp.clip((tile_hi_min - base + 1) // TK, t1, t3)
    tiles = jnp.stack([t0, t1, t2, t3], axis=1).astype(jnp.int32)
    att = attend(queries, kv_win, qpos_rows - base, lo_rows - base, tiles, plane, depth + 1)

    return project(att, out_weight, lax.axis_size("head"))


def solution(mesh):
    in_specs = (
        P("ctx", "head"),
        P("ctx", "head"),
        P("ctx", "head"),
        P(),
        P("ctx"),
        P(),
        P(),
        P("head", None),
    )
    out_specs = P("ctx", "head")
    return jax.shard_map(
        on_device, mesh=mesh, in_specs=in_specs, out_specs=out_specs, check_vma=False
    )
```

```python
import functools

import jax
import jax.numpy as jnp
from jax import lax
from jax.experimental import pallas as pl
from jax.experimental.pallas import tpu as pltpu
from jax.sharding import PartitionSpec as P

HD = 128
BLK = 8
TQ = 1024
TK = 512
SHARD = 256
NEG_FILL = -1e30
LONGEST = 4352
PLANE = 4


def attn_kernel(plane, slots, tiles_ref, q_ref, kv_ref, qpos_ref, lo_ref, o_ref, m_sc, l_sc, acc_sc):
    n_q = q_ref.shape[0] * q_ref.shape[1] // (HD * TQ)
    scale = HD ** (-0.5)

    def q_body(qi, carry):
        r0 = pl.multiple_of(qi * TQ, TQ)
        heads = TQ // q_ref.shape[0]
        q = jnp.concatenate([
            q_ref[:, pl.ds(pl.multiple_of((qi * heads + g) * HD, HD), HD)] for g in range(heads)
        ], axis=0)
        qpos = qpos_ref[:, pl.ds(r0, TQ)]
        lo = lo_ref[:, pl.ds(r0, TQ)]
        m_sc[...] = jnp.full(m_sc.shape, NEG_FILL, jnp.float32)
        l_sc[...] = jnp.zeros(l_sc.shape, jnp.float32)
        acc_sc[...] = jnp.zeros(acc_sc.shape, jnp.float32)

        def k_step(kj, masked):
            c0 = pl.multiple_of(kj * TK, TK)
            at = []
            for piece in range(TK // SHARD):
                i = kj * (TK // SHARD) + piece
                at.append(pl.multiple_of((lax.rem(i, plane) * slots + i // plane) * SHARD, SHARD))
            s = jnp.concatenate([
                lax.dot_general(
                    kv_ref[pl.ds(a, SHARD), pl.ds(0, HD)], q, (((1,), (1,)), ((), ())),
                    preferred_element_type=jnp.float32,
                )
                for a in at
            ], axis=0) * scale
            if masked:
                kpos = c0 + lax.broadcasted_iota(jnp.int32, (TK, TQ), 0)
                ok = (kpos >= lo) & (kpos <= qpos)
                s = jnp.where(ok, s, NEG_FILL)
            m_prev = m_sc[...]
            m_new = jnp.maximum(m_prev, jnp.max(s, axis=0, keepdims=True))
            p = jnp.exp(s - m_new)
            if masked:
                p = jnp.where(ok, p, 0.0)
            fade = jnp.exp(m_prev - m_new)
            l_sc[...] = l_sc[...] * fade + jnp.sum(p, axis=0, keepdims=True)
            pb = p.astype(jnp.bfloat16)
            update = acc_sc[...] * fade
            for piece, a in enumerate(at):
                update = update + lax.dot_general(
                    kv_ref[pl.ds(a, SHARD), pl.ds(HD, HD)], pb[piece * SHARD:(piece + 1) * SHARD],
                    (((0,), (0,)), ((), ())), preferred_element_type=jnp.float32,
                )
            acc_sc[...] = update
            m_sc[...] = m_new

        def masked_body(kj, c):
            k_step(kj, True)
            return c

        def open_body(kj, c):
            k_step(kj, False)
            return c

        lax.fori_loop(tiles_ref[qi, 0], tiles_ref[qi, 1], masked_body, 0)
        lax.fori_loop(tiles_ref[qi, 1], tiles_ref[qi, 2], open_body, 0)
        lax.fori_loop(tiles_ref[qi, 2], tiles_ref[qi, 3], masked_body, 0)
        out = (acc_sc[...] / l_sc[...]).T.astype(o_ref.dtype)
        tokens = q_ref.shape[0]
        for g in range(heads):
            o_ref[:, pl.ds(pl.multiple_of((qi * heads + g) * HD, HD), HD)] = out[g * tokens:(g + 1) * tokens]
        return carry

    lax.fori_loop(0, n_q, q_body, 0)


def attend(q_rows, kv_all, qpos_rows, lo_rows, tiles, plane, slots):
    vmem = pltpu.MemorySpace.VMEM if hasattr(pltpu, "MemorySpace") else pltpu.VMEM
    return pl.pallas_call(
        functools.partial(attn_kernel, plane, slots),
        out_shape=jax.ShapeDtypeStruct(q_rows.shape, jnp.bfloat16),
        in_specs=[
            pl.BlockSpec(memory_space=pltpu.SMEM),
            pl.BlockSpec(memory_space=vmem),
            pl.BlockSpec(memory_space=vmem),
            pl.BlockSpec(memory_space=vmem),
            pl.BlockSpec(memory_space=vmem),
        ],
        out_specs=pl.BlockSpec(memory_space=vmem),
        scratch_shapes=[
            pltpu.VMEM((1, TQ), jnp.float32),
            pltpu.VMEM((1, TQ), jnp.float32),
            pltpu.VMEM((HD, TQ), jnp.float32),
        ],
    )(tiles, q_rows, kv_all, qpos_rows, lo_rows)


MESH_ID = pl.DeviceIdType.MESH


def window_kernel(depth, plane, n_ctx, need_col, kv_ref, win_ref, send1, recv1, send2, recv2, local_sem):
    me = lax.axis_index("ctx")
    h = lax.axis_index("head")
    z = me // plane
    r = me % plane
    n_z = n_ctx // plane
    mate = r + 1 - 2 * (r % 2)
    across = (r + 2) % plane
    far = across + 1 - 2 * (across % 2)
    barrier = pltpu.get_barrier_semaphore()

    @pl.when(z + 1 < n_z)
    def _():
        pl.semaphore_signal(barrier, 1, device_id=(me + plane, h), device_id_type=MESH_ID)

    @pl.when(z - 1 >= 0)
    def _():
        pl.semaphore_signal(barrier, 1, device_id=(me - plane, h), device_id_type=MESH_ID)

    for peer in (mate, across):
        pl.semaphore_signal(barrier, 1, device_id=(z * plane + peer, h), device_id_type=MESH_ID)
    pl.semaphore_wait(barrier, jnp.minimum(1, n_z - 1 - z) + jnp.minimum(1, z) + 2)
    local = pltpu.make_async_copy(kv_ref, win_ref.at[r, depth], local_sem)
    local.start()

    def wanted(d):
        return (d < depth) | (r >= need_col)

    def up(k):
        return pltpu.make_async_remote_copy(
            src_ref=kv_ref if k == 1 else win_ref.at[r, depth - k + 1],
            dst_ref=win_ref.at[r, depth - k],
            send_sem=send1.at[k - 1],
            recv_sem=recv1.at[k - 1],
            device_id=(me + plane, h),
            device_id_type=MESH_ID,
        )

    def sends(k):
        return (z + 1 < n_z) & (z - (k - 1) >= 0) & wanted(k)

    def gets(k):
        return (z - k >= 0) & wanted(k)

    @pl.when(sends(1))
    def _():
        up(1).start()

    def has(slot, col):
        return (z - (depth - slot) >= 0) & ((slot > 0) | (col >= need_col))

    def hop(idx, col, slot, to):
        return pltpu.make_async_remote_copy(
            src_ref=win_ref.at[col, slot],
            dst_ref=win_ref.at[col, slot],
            send_sem=send2.at[idx, slot],
            recv_sem=recv2.at[idx, slot],
            device_id=(z * plane + to, h),
            device_id_type=MESH_ID,
        )

    local.wait()
    hop(0, r, depth, mate).start()
    hop(1, r, depth, across).start()
    for k in range(1, depth + 1):
        @pl.when(gets(k))
        def _():
            up(k).wait_recv()
            hop(0, r, depth - k, mate).start()
            hop(1, r, depth - k, across).start()

        if k < depth:
            @pl.when(sends(k + 1))
            def _():
                up(k + 1).start()

    for k in range(1, depth + 1):
        @pl.when(sends(k))
        def _():
            up(k).wait_send()

    for slot in range(depth, -1, -1):
        @pl.when(has(slot, across))
        def _():
            hop(1, across, slot, across).wait_recv()
            hop(2, across, slot, mate).start()

    for slot in range(depth + 1):
        @pl.when(has(slot, r))
        def _():
            hop(0, r, slot, mate).wait_send()
            hop(1, r, slot, across).wait_send()

        @pl.when(has(slot, across))
        def _():
            hop(2, across, slot, mate).wait_send()

        @pl.when(has(slot, mate))
        def _():
            hop(0, mate, slot, mate).wait_recv()

        @pl.when(has(slot, far))
        def _():
            hop(2, far, slot, mate).wait_recv()


def gather_window(kv_local, depth, plane, n_ctx, need_col):
    rows, width = kv_local.shape
    return pl.pallas_call(
        functools.partial(window_kernel, depth, plane, n_ctx, need_col),
        out_shape=jax.ShapeDtypeStruct((plane, depth + 1, rows, width), kv_local.dtype),
        in_specs=[pl.BlockSpec(memory_space=pl.ANY)],
        out_specs=pl.BlockSpec(memory_space=pl.ANY),
        scratch_shapes=[
            pltpu.SemaphoreType.DMA((depth,)),
            pltpu.SemaphoreType.DMA((depth,)),
            pltpu.SemaphoreType.DMA((3, depth + 1)),
            pltpu.SemaphoreType.DMA((3, depth + 1)),
            pltpu.SemaphoreType.DMA(()),
        ],
        compiler_params=pltpu.CompilerParams(collective_id=0, has_side_effects=True),
    )(kv_local)


def project_kernel(n_head, att_ref, w_ref, o_ref, send_buf, got, send_sem, recv_sem):
    me = lax.axis_index("head")
    row = lax.axis_index("ctx")
    cols = o_ref.shape[1]
    barrier = pltpu.get_barrier_semaphore()
    for d in range(1, n_head):
        pl.semaphore_signal(
            barrier, 1, device_id=(row, lax.rem(me + d, n_head)), device_id_type=MESH_ID
        )
    pl.semaphore_wait(barrier, n_head - 1)

    def part(dst):
        c0 = pl.multiple_of(dst * cols, cols)
        return jnp.dot(
            att_ref[...], w_ref[:, pl.ds(c0, cols)], preferred_element_type=jnp.float32
        ).astype(jnp.bfloat16)

    def send(d):
        dst = lax.rem(me + d, n_head)
        return pltpu.make_async_remote_copy(
            src_ref=send_buf.at[d - 1],
            dst_ref=got.at[me],
            send_sem=send_sem.at[d - 1],
            recv_sem=recv_sem.at[d - 1],
            device_id=(row, dst),
            device_id_type=MESH_ID,
        )

    def arrival(d):
        src = lax.rem(me + n_head - d, n_head)
        return pltpu.make_async_remote_copy(
            src_ref=send_buf.at[d - 1],
            dst_ref=got.at[src],
            send_sem=send_sem.at[d - 1],
            recv_sem=recv_sem.at[d - 1],
            device_id=(row, src),
            device_id_type=MESH_ID,
        )

    send_buf[0] = part(lax.rem(me + 1, n_head))
    for d in range(1, n_head):
        if d + 1 < n_head:
            send_buf[d] = part(lax.rem(me + d + 1, n_head))
        send(d).start()
    total = part(me).astype(jnp.float32)
    for d in range(1, n_head):
        send(d).wait_send()
        arrival(d).wait_recv()
        total = total + got[lax.rem(me + n_head - d, n_head)].astype(jnp.float32)
    o_ref[...] = total.astype(o_ref.dtype)


def project(att, out_weight, n_head):
    rows = att.shape[0]
    cols = out_weight.shape[1] // n_head
    vmem = pltpu.MemorySpace.VMEM if hasattr(pltpu, "MemorySpace") else pltpu.VMEM
    return pl.pallas_call(
        functools.partial(project_kernel, n_head),
        out_shape=jax.ShapeDtypeStruct((rows, cols), jnp.bfloat16),
        in_specs=[pl.BlockSpec(memory_space=vmem), pl.BlockSpec(memory_space=vmem)],
        out_specs=pl.BlockSpec(memory_space=vmem),
        scratch_shapes=[
            pltpu.VMEM((n_head - 1, rows, cols), jnp.bfloat16),
            pltpu.VMEM((n_head, rows, cols), jnp.bfloat16),
            pltpu.SemaphoreType.DMA((n_head - 1,)),
            pltpu.SemaphoreType.DMA((n_head - 1,)),
        ],
        compiler_params=pltpu.CompilerParams(collective_id=1, has_side_effects=True),
    )(att, out_weight)


def on_device(queries, key_rows, values, lengths, block_plan, inverse, mask_lo, out_weight):
    row_count, query_width = queries.shape
    group_size = query_width // HD
    here = lax.axis_index("ctx")
    first = here * row_count
    pos = first + jnp.arange(row_count, dtype=jnp.int32)
    doc_ends = jnp.cumsum(lengths).astype(jnp.int32)
    doc_start = jnp.max(jnp.where(doc_ends[None, :] <= pos[:, None], doc_ends[None, :], 0), axis=1)
    block_lo = lax.dynamic_slice_in_dim(mask_lo, here * (row_count // BLK), row_count // BLK)
    lo_tok = jnp.maximum(jnp.repeat(block_lo, BLK) * BLK, doc_start)
    qpos_rows = jnp.tile(pos, group_size)[None, :]
    lo_rows = jnp.tile(lo_tok, group_size)[None, :]
    n_q = row_count * group_size // TQ
    tile_lo = jnp.full((n_q,), jnp.min(lo_tok))
    tile_hi = jnp.full((n_q,), pos[-1])
    tile_lo_max = jnp.full((n_q,), jnp.max(lo_tok))
    tile_hi_min = jnp.full((n_q,), pos[0])

    kv_local = jnp.concatenate([key_rows, values], axis=1)
    n_ctx = lax.axis_size("ctx")
    plane = PLANE
    depth = min(n_ctx // plane - 1, -(-(LONGEST - 1) // (plane * row_count)))
    need_col = max(0, -(-(plane * row_count * depth - (LONGEST - 1) - (row_count - 1)) // row_count))
    need_col = need_col // (TK // SHARD) * (TK // SHARD)
    kv_win = gather_window(kv_local, depth, plane, n_ctx, need_col)
    kv_win = kv_win.reshape(-1, kv_win.shape[-1])
    base = (here // plane - depth) * plane * row_count
    span = kv_win.shape[0]
    t0 = (tile_lo - base) // TK
    t3 = jnp.minimum((tile_hi - base) // TK + 1, span // TK)
    t1 = jnp.clip((tile_lo_max - base + TK - 1) // TK, t0, t3)
    t2 = jnp.clip((tile_hi_min - base + 1) // TK, t1, t3)
    tiles = jnp.stack([t0, t1, t2, t3], axis=1).astype(jnp.int32)
    att = attend(queries, kv_win, qpos_rows - base, lo_rows - base, tiles, plane, depth + 1)

    return project(att, out_weight, lax.axis_size("head"))


def solution(mesh):
    in_specs = (
        P("ctx", "head"),
        P("ctx", "head"),
        P("ctx", "head"),
        P(),
        P("ctx"),
        P(),
        P(),
        P("head", None),
    )
    out_specs = P("ctx", "head")
    return jax.shard_map(
        on_device, mesh=mesh, in_specs=in_specs, out_specs=out_specs, check_vma=False
    )
```

```python
import functools

import jax
import jax.numpy as jnp
from jax import lax
from jax.experimental import pallas as pl
from jax.experimental.pallas import tpu as pltpu
from jax.sharding import PartitionSpec as P

HD = 128
BLK = 8
TQ = 1024
TK = 512
SHARD = 256
NEG_FILL = -1e30
LONGEST = 4352
PLANE = 4


def attn_kernel(plane, slots, tiles_ref, q_ref, kv_ref, qpos_ref, lo_ref, o_ref, m_sc, l_sc, acc_sc):
    n_q = q_ref.shape[0] * q_ref.shape[1] // (HD * TQ)
    scale = HD ** (-0.5)

    def q_body(qi, carry):
        r0 = pl.multiple_of(qi * TQ, TQ)
        heads = TQ // q_ref.shape[0]
        q = jnp.concatenate([
            q_ref[:, pl.ds(pl.multiple_of((qi * heads + g) * HD, HD), HD)] for g in range(heads)
        ], axis=0)
        qpos = qpos_ref[:, pl.ds(r0, TQ)]
        lo = lo_ref[:, pl.ds(r0, TQ)]
        m_sc[...] = jnp.full(m_sc.shape, NEG_FILL, jnp.float32)
        l_sc[...] = jnp.zeros(l_sc.shape, jnp.float32)
        acc_sc[...] = jnp.zeros(acc_sc.shape, jnp.float32)

        def k_step(kj, masked):
            c0 = pl.multiple_of(kj * TK, TK)
            at = []
            for piece in range(TK // SHARD):
                i = kj * (TK // SHARD) + piece
                at.append(pl.multiple_of((lax.rem(i, plane) * slots + i // plane) * SHARD, SHARD))
            s = jnp.concatenate([
                lax.dot_general(
                    kv_ref[pl.ds(a, SHARD), pl.ds(0, HD)], q, (((1,), (1,)), ((), ())),
                    preferred_element_type=jnp.float32,
                )
                for a in at
            ], axis=0) * scale
            if masked:
                kpos = c0 + lax.broadcasted_iota(jnp.int32, (TK, TQ), 0)
                ok = (kpos >= lo) & (kpos <= qpos)
                s = jnp.where(ok, s, NEG_FILL)
            m_prev = m_sc[...]
            m_new = jnp.maximum(m_prev, jnp.max(s, axis=0, keepdims=True))
            p = jnp.exp(s - m_new)
            if masked:
                p = jnp.where(ok, p, 0.0)
            fade = jnp.exp(m_prev - m_new)
            l_sc[...] = l_sc[...] * fade + jnp.sum(p, axis=0, keepdims=True)
            pb = p.astype(jnp.bfloat16)
            update = acc_sc[...] * fade
            for piece, a in enumerate(at):
                update = update + lax.dot_general(
                    kv_ref[pl.ds(a, SHARD), pl.ds(HD, HD)], pb[piece * SHARD:(piece + 1) * SHARD],
                    (((0,), (0,)), ((), ())), preferred_element_type=jnp.float32,
                )
            acc_sc[...] = update
            m_sc[...] = m_new

        def masked_body(kj, c):
            k_step(kj, True)
            return c

        def open_body(kj, c):
            k_step(kj, False)
            return c

        lax.fori_loop(tiles_ref[qi, 0], tiles_ref[qi, 1], masked_body, 0)
        lax.fori_loop(tiles_ref[qi, 1], tiles_ref[qi, 2], open_body, 0)
        lax.fori_loop(tiles_ref[qi, 2], tiles_ref[qi, 3], masked_body, 0)
        out = (acc_sc[...] / l_sc[...]).T.astype(o_ref.dtype)
        tokens = q_ref.shape[0]
        for g in range(heads):
            o_ref[:, pl.ds(pl.multiple_of((qi * heads + g) * HD, HD), HD)] = out[g * tokens:(g + 1) * tokens]
        return carry

    lax.fori_loop(0, n_q, q_body, 0)


def attend(q_rows, kv_all, qpos_rows, lo_rows, tiles, plane, slots):
    vmem = pltpu.MemorySpace.VMEM if hasattr(pltpu, "MemorySpace") else pltpu.VMEM
    return pl.pallas_call(
        functools.partial(attn_kernel, plane, slots),
        out_shape=jax.ShapeDtypeStruct(q_rows.shape, jnp.bfloat16),
        in_specs=[
            pl.BlockSpec(memory_space=pltpu.SMEM),
            pl.BlockSpec(memory_space=vmem),
            pl.BlockSpec(memory_space=vmem),
            pl.BlockSpec(memory_space=vmem),
            pl.BlockSpec(memory_space=vmem),
        ],
        out_specs=pl.BlockSpec(memory_space=vmem),
        scratch_shapes=[
            pltpu.VMEM((1, TQ), jnp.float32),
            pltpu.VMEM((1, TQ), jnp.float32),
            pltpu.VMEM((HD, TQ), jnp.float32),
        ],
    )(tiles, q_rows, kv_all, qpos_rows, lo_rows)


MESH_ID = pl.DeviceIdType.MESH


def window_kernel(depth, plane, n_ctx, need_col, kv_ref, win_ref, send1, recv1, send2, recv2, local_sem):
    me = lax.axis_index("ctx")
    h = lax.axis_index("head")
    z = me // plane
    r = me % plane
    n_z = n_ctx // plane
    mate = r + 1 - 2 * (r % 2)
    across = (r + 2) % plane
    far = across + 1 - 2 * (across % 2)
    barrier = pltpu.get_barrier_semaphore()

    for step in (1, 2):
        @pl.when(z + step < n_z)
        def _():
            pl.semaphore_signal(barrier, 1, device_id=(me + step * plane, h), device_id_type=MESH_ID)

        @pl.when(z - step >= 0)
        def _():
            pl.semaphore_signal(barrier, 1, device_id=(me - step * plane, h), device_id_type=MESH_ID)

    for peer in (mate, across):
        pl.semaphore_signal(barrier, 1, device_id=(z * plane + peer, h), device_id_type=MESH_ID)
    pl.semaphore_wait(barrier, jnp.minimum(2, n_z - 1 - z) + jnp.minimum(2, z) + 2)
    local = pltpu.make_async_copy(kv_ref, win_ref.at[r, depth], local_sem)
    local.start()

    def wanted(d):
        return (d < depth) | (r >= need_col)

    def stride(d):
        return 1 if d == 1 else 2

    def up(d):
        return pltpu.make_async_remote_copy(
            src_ref=kv_ref if d <= 2 else win_ref.at[r, depth - d + 2],
            dst_ref=win_ref.at[r, depth - d],
            send_sem=send1.at[d - 1],
            recv_sem=recv1.at[d - 1],
            device_id=(me + stride(d) * plane, h),
            device_id_type=MESH_ID,
        )

    def sends(d):
        return (z + stride(d) < n_z) & (z - (d - stride(d)) >= 0) & wanted(d)

    def gets(d):
        return (z - d >= 0) & wanted(d)

    for d in range(1, min(2, depth) + 1):
        @pl.when(sends(d))
        def _():
            up(d).start()

    def has(slot, col):
        return (z - (depth - slot) >= 0) & ((slot > 0) | (col >= need_col))

    def hop(idx, col, slot, to):
        return pltpu.make_async_remote_copy(
            src_ref=win_ref.at[col, slot],
            dst_ref=win_ref.at[col, slot],
            send_sem=send2.at[idx, slot],
            recv_sem=recv2.at[idx, slot],
            device_id=(z * plane + to, h),
            device_id_type=MESH_ID,
        )

    local.wait()
    hop(0, r, depth, mate).start()
    hop(1, r, depth, across).start()
    for k in range(1, depth + 1):
        @pl.when(gets(k))
        def _():
            up(k).wait_recv()
            hop(0, r, depth - k, mate).start()
            hop(1, r, depth - k, across).start()

        if k + 2 <= depth:
            @pl.when(sends(k + 2))
            def _():
                up(k + 2).start()

    for k in range(1, depth + 1):
        @pl.when(sends(k))
        def _():
            up(k).wait_send()

    for slot in range(depth, -1, -1):
        @pl.when(has(slot, across))
        def _():
            hop(1, across, slot, across).wait_recv()
            hop(2, across, slot, mate).start()

    for slot in range(depth + 1):
        @pl.when(has(slot, r))
        def _():
            hop(0, r, slot, mate).wait_send()
            hop(1, r, slot, across).wait_send()

        @pl.when(has(slot, across))
        def _():
            hop(2, across, slot, mate).wait_send()

        @pl.when(has(slot, mate))
        def _():
            hop(0, mate, slot, mate).wait_recv()

        @pl.when(has(slot, far))
        def _():
            hop(2, far, slot, mate).wait_recv()


def gather_window(kv_local, depth, plane, n_ctx, need_col):
    rows, width = kv_local.shape
    return pl.pallas_call(
        functools.partial(window_kernel, depth, plane, n_ctx, need_col),
        out_shape=jax.ShapeDtypeStruct((plane, depth + 1, rows, width), kv_local.dtype),
        in_specs=[pl.BlockSpec(memory_space=pl.ANY)],
        out_specs=pl.BlockSpec(memory_space=pl.ANY),
        scratch_shapes=[
            pltpu.SemaphoreType.DMA((depth,)),
            pltpu.SemaphoreType.DMA((depth,)),
            pltpu.SemaphoreType.DMA((3, depth + 1)),
            pltpu.SemaphoreType.DMA((3, depth + 1)),
            pltpu.SemaphoreType.DMA(()),
        ],
        compiler_params=pltpu.CompilerParams(collective_id=0, has_side_effects=True),
    )(kv_local)


def project_kernel(n_head, att_ref, w_ref, o_ref, send_buf, got, send_sem, recv_sem):
    me = lax.axis_index("head")
    row = lax.axis_index("ctx")
    cols = o_ref.shape[1]
    barrier = pltpu.get_barrier_semaphore()
    for d in range(1, n_head):
        pl.semaphore_signal(
            barrier, 1, device_id=(row, lax.rem(me + d, n_head)), device_id_type=MESH_ID
        )
    pl.semaphore_wait(barrier, n_head - 1)

    def part(dst):
        c0 = pl.multiple_of(dst * cols, cols)
        return jnp.dot(
            att_ref[...], w_ref[:, pl.ds(c0, cols)], preferred_element_type=jnp.float32
        ).astype(jnp.bfloat16)

    def send(d):
        dst = lax.rem(me + d, n_head)
        return pltpu.make_async_remote_copy(
            src_ref=send_buf.at[d - 1],
            dst_ref=got.at[me],
            send_sem=send_sem.at[d - 1],
            recv_sem=recv_sem.at[d - 1],
            device_id=(row, dst),
            device_id_type=MESH_ID,
        )

    def arrival(d):
        src = lax.rem(me + n_head - d, n_head)
        return pltpu.make_async_remote_copy(
            src_ref=send_buf.at[d - 1],
            dst_ref=got.at[src],
            send_sem=send_sem.at[d - 1],
            recv_sem=recv_sem.at[d - 1],
            device_id=(row, src),
            device_id_type=MESH_ID,
        )

    send_buf[0] = part(lax.rem(me + 1, n_head))
    for d in range(1, n_head):
        if d + 1 < n_head:
            send_buf[d] = part(lax.rem(me + d + 1, n_head))
        send(d).start()
    total = part(me).astype(jnp.float32)
    for d in range(1, n_head):
        send(d).wait_send()
        arrival(d).wait_recv()
        total = total + got[lax.rem(me + n_head - d, n_head)].astype(jnp.float32)
    o_ref[...] = total.astype(o_ref.dtype)


def project(att, out_weight, n_head):
    rows = att.shape[0]
    cols = out_weight.shape[1] // n_head
    vmem = pltpu.MemorySpace.VMEM if hasattr(pltpu, "MemorySpace") else pltpu.VMEM
    return pl.pallas_call(
        functools.partial(project_kernel, n_head),
        out_shape=jax.ShapeDtypeStruct((rows, cols), jnp.bfloat16),
        in_specs=[pl.BlockSpec(memory_space=vmem), pl.BlockSpec(memory_space=vmem)],
        out_specs=pl.BlockSpec(memory_space=vmem),
        scratch_shapes=[
            pltpu.VMEM((n_head - 1, rows, cols), jnp.bfloat16),
            pltpu.VMEM((n_head, rows, cols), jnp.bfloat16),
            pltpu.SemaphoreType.DMA((n_head - 1,)),
            pltpu.SemaphoreType.DMA((n_head - 1,)),
        ],
        compiler_params=pltpu.CompilerParams(collective_id=1, has_side_effects=True),
    )(att, out_weight)


def on_device(queries, key_rows, values, lengths, block_plan, inverse, mask_lo, out_weight):
    row_count, query_width = queries.shape
    group_size = query_width // HD
    here = lax.axis_index("ctx")
    first = here * row_count
    pos = first + jnp.arange(row_count, dtype=jnp.int32)
    doc_ends = jnp.cumsum(lengths).astype(jnp.int32)
    doc_start = jnp.max(jnp.where(doc_ends[None, :] <= pos[:, None], doc_ends[None, :], 0), axis=1)
    block_lo = lax.dynamic_slice_in_dim(mask_lo, here * (row_count // BLK), row_count // BLK)
    lo_tok = jnp.maximum(jnp.repeat(block_lo, BLK) * BLK, doc_start)
    qpos_rows = jnp.tile(pos, group_size)[None, :]
    lo_rows = jnp.tile(lo_tok, group_size)[None, :]
    n_q = row_count * group_size // TQ
    tile_lo = jnp.full((n_q,), jnp.min(lo_tok))
    tile_hi = jnp.full((n_q,), pos[-1])
    tile_lo_max = jnp.full((n_q,), jnp.max(lo_tok))
    tile_hi_min = jnp.full((n_q,), pos[0])

    kv_local = jnp.concatenate([key_rows, values], axis=1)
    n_ctx = lax.axis_size("ctx")
    plane = PLANE
    depth = min(n_ctx // plane - 1, -(-(LONGEST - 1) // (plane * row_count)))
    need_col = max(0, -(-(plane * row_count * depth - (LONGEST - 1) - (row_count - 1)) // row_count))
    need_col = need_col // (TK // SHARD) * (TK // SHARD)
    kv_win = gather_window(kv_local, depth, plane, n_ctx, need_col)
    kv_win = kv_win.reshape(-1, kv_win.shape[-1])
    base = (here // plane - depth) * plane * row_count
    span = kv_win.shape[0]
    t0 = (tile_lo - base) // TK
    t3 = jnp.minimum((tile_hi - base) // TK + 1, span // TK)
    t1 = jnp.clip((tile_lo_max - base + TK - 1) // TK, t0, t3)
    t2 = jnp.clip((tile_hi_min - base + 1) // TK, t1, t3)
    tiles = jnp.stack([t0, t1, t2, t3], axis=1).astype(jnp.int32)
    att = attend(queries, kv_win, qpos_rows - base, lo_rows - base, tiles, plane, depth + 1)

    return project(att, out_weight, lax.axis_size("head"))


def solution(mesh):
    in_specs = (
        P("ctx", "head"),
        P("ctx", "head"),
        P("ctx", "head"),
        P(),
        P("ctx"),
        P(),
        P(),
        P("head", None),
    )
    out_specs = P("ctx", "head")
    return jax.shard_map(
        on_device, mesh=mesh, in_specs=in_specs, out_specs=out_specs, check_vma=False
    )
```

```python
import functools

import jax
import jax.numpy as jnp
from jax import lax
from jax.experimental import pallas as pl
from jax.experimental.pallas import tpu as pltpu
from jax.sharding import PartitionSpec as P

HD = 128
BLK = 8
TQ = 1024
TK = 512
SHARD = 256
NEG_FILL = -1e30
LONGEST = 4352
PLANE = 4


def attn_kernel(plane, slots, tiles_ref, q_ref, kv_ref, qpos_ref, lo_ref, o_ref, m_sc, l_sc, acc_sc):
    n_q = q_ref.shape[0] * q_ref.shape[1] // (HD * TQ)
    scale = HD ** (-0.5)

    def q_body(qi, carry):
        r0 = pl.multiple_of(qi * TQ, TQ)
        heads = TQ // q_ref.shape[0]
        q = jnp.concatenate([
            q_ref[:, pl.ds(pl.multiple_of((qi * heads + g) * HD, HD), HD)] for g in range(heads)
        ], axis=0)
        qpos = qpos_ref[:, pl.ds(r0, TQ)]
        lo = lo_ref[:, pl.ds(r0, TQ)]
        m_sc[...] = jnp.full(m_sc.shape, NEG_FILL, jnp.float32)
        l_sc[...] = jnp.zeros(l_sc.shape, jnp.float32)
        acc_sc[...] = jnp.zeros(acc_sc.shape, jnp.float32)

        def k_step(kj, masked):
            c0 = pl.multiple_of(kj * TK, TK)
            at = []
            for piece in range(TK // SHARD):
                i = kj * (TK // SHARD) + piece
                at.append(pl.multiple_of((lax.rem(i, plane) * slots + i // plane) * SHARD, SHARD))
            s = jnp.concatenate([
                lax.dot_general(
                    kv_ref[pl.ds(a, SHARD), pl.ds(0, HD)], q, (((1,), (1,)), ((), ())),
                    preferred_element_type=jnp.float32,
                )
                for a in at
            ], axis=0) * scale
            if masked:
                kpos = c0 + lax.broadcasted_iota(jnp.int32, (TK, TQ), 0)
                ok = (kpos >= lo) & (kpos <= qpos)
                s = jnp.where(ok, s, NEG_FILL)
            m_prev = m_sc[...]
            m_new = jnp.maximum(m_prev, jnp.max(s, axis=0, keepdims=True))
            p = jnp.exp(s - m_new)
            if masked:
                p = jnp.where(ok, p, 0.0)
            fade = jnp.exp(m_prev - m_new)
            l_sc[...] = l_sc[...] * fade + jnp.sum(p, axis=0, keepdims=True)
            pb = p.astype(jnp.bfloat16)
            update = acc_sc[...] * fade
            for piece, a in enumerate(at):
                update = update + lax.dot_general(
                    kv_ref[pl.ds(a, SHARD), pl.ds(HD, HD)], pb[piece * SHARD:(piece + 1) * SHARD],
                    (((0,), (0,)), ((), ())), preferred_element_type=jnp.float32,
                )
            acc_sc[...] = update
            m_sc[...] = m_new

        def masked_body(kj, c):
            k_step(kj, True)
            return c

        def open_body(kj, c):
            k_step(kj, False)
            return c

        lax.fori_loop(tiles_ref[qi, 0], tiles_ref[qi, 1], masked_body, 0)
        lax.fori_loop(tiles_ref[qi, 1], tiles_ref[qi, 2], open_body, 0)
        lax.fori_loop(tiles_ref[qi, 2], tiles_ref[qi, 3], masked_body, 0)
        out = (acc_sc[...] / l_sc[...]).T.astype(o_ref.dtype)
        tokens = q_ref.shape[0]
        for g in range(heads):
            o_ref[:, pl.ds(pl.multiple_of((qi * heads + g) * HD, HD), HD)] = out[g * tokens:(g + 1) * tokens]
        return carry

    lax.fori_loop(0, n_q, q_body, 0)


def attend(q_rows, kv_all, qpos_rows, lo_rows, tiles, plane, slots):
    vmem = pltpu.MemorySpace.VMEM if hasattr(pltpu, "MemorySpace") else pltpu.VMEM
    return pl.pallas_call(
        functools.partial(attn_kernel, plane, slots),
        out_shape=jax.ShapeDtypeStruct(q_rows.shape, jnp.bfloat16),
        in_specs=[
            pl.BlockSpec(memory_space=pltpu.SMEM),
            pl.BlockSpec(memory_space=vmem),
            pl.BlockSpec(memory_space=vmem),
            pl.BlockSpec(memory_space=vmem),
            pl.BlockSpec(memory_space=vmem),
        ],
        out_specs=pl.BlockSpec(memory_space=vmem),
        scratch_shapes=[
            pltpu.VMEM((1, TQ), jnp.float32),
            pltpu.VMEM((1, TQ), jnp.float32),
            pltpu.VMEM((HD, TQ), jnp.float32),
        ],
    )(tiles, q_rows, kv_all, qpos_rows, lo_rows)


MESH_ID = pl.DeviceIdType.MESH


def window_kernel(depth, plane, n_ctx, need_col, kv_ref, win_ref, send1, recv1, send2, recv2, local_sem):
    me = lax.axis_index("ctx")
    h = lax.axis_index("head")
    z = me // plane
    r = me % plane
    n_z = n_ctx // plane
    mate = r + 1 - 2 * (r % 2)
    across = (r + 2) % plane
    far = across + 1 - 2 * (across % 2)
    barrier = pltpu.get_barrier_semaphore()

    @pl.when(z + 1 < n_z)
    def _():
        pl.semaphore_signal(barrier, 1, device_id=(me + plane, h), device_id_type=MESH_ID)

    @pl.when(z - 1 >= 0)
    def _():
        pl.semaphore_signal(barrier, 1, device_id=(me - plane, h), device_id_type=MESH_ID)

    for peer in (mate, across):
        pl.semaphore_signal(barrier, 1, device_id=(z * plane + peer, h), device_id_type=MESH_ID)
    pl.semaphore_wait(barrier, jnp.minimum(1, n_z - 1 - z) + jnp.minimum(1, z) + 2)
    local = pltpu.make_async_copy(kv_ref, win_ref.at[r, depth], local_sem)
    local.start()

    def wanted(d):
        return (d < depth) | (r >= need_col)

    def up(k):
        return pltpu.make_async_remote_copy(
            src_ref=kv_ref if k == 1 else win_ref.at[r, depth - k + 1],
            dst_ref=win_ref.at[r, depth - k],
            send_sem=send1.at[k - 1],
            recv_sem=recv1.at[k - 1],
            device_id=(me + plane, h),
            device_id_type=MESH_ID,
        )

    def sends(k):
        return (z + 1 < n_z) & (z - (k - 1) >= 0) & wanted(k)

    def gets(k):
        return (z - k >= 0) & wanted(k)

    @pl.when(sends(1))
    def _():
        up(1).start()

    def has(slot, col):
        return (z - (depth - slot) >= 0) & ((slot > 0) | (col >= need_col))

    def hop(idx, col, slot, to):
        return pltpu.make_async_remote_copy(
            src_ref=win_ref.at[col, slot],
            dst_ref=win_ref.at[col, slot],
            send_sem=send2.at[idx, slot],
            recv_sem=recv2.at[idx, slot],
            device_id=(z * plane + to, h),
            device_id_type=MESH_ID,
        )

    local.wait()
    hop(0, r, depth, mate).start()
    hop(1, r, depth, across).start()
    for k in range(1, depth + 1):
        @pl.when(gets(k))
        def _():
            up(k).wait_recv()
            hop(0, r, depth - k, mate).start()
            hop(1, r, depth - k, across).start()

        if k < depth:
            @pl.when(sends(k + 1))
            def _():
                up(k + 1).start()

    for k in range(1, depth + 1):
        @pl.when(sends(k))
        def _():
            up(k).wait_send()

    for slot in range(depth, -1, -1):
        @pl.when(has(slot, across))
        def _():
            hop(1, across, slot, across).wait_recv()
            hop(2, across, slot, mate).start()

    for slot in range(depth + 1):
        @pl.when(has(slot, r))
        def _():
            hop(0, r, slot, mate).wait_send()
            hop(1, r, slot, across).wait_send()

        @pl.when(has(slot, across))
        def _():
            hop(2, across, slot, mate).wait_send()

        @pl.when(has(slot, mate))
        def _():
            hop(0, mate, slot, mate).wait_recv()

        @pl.when(has(slot, far))
        def _():
            hop(2, far, slot, mate).wait_recv()


def gather_window(kv_local, depth, plane, n_ctx, need_col):
    rows, width = kv_local.shape
    return pl.pallas_call(
        functools.partial(window_kernel, depth, plane, n_ctx, need_col),
        out_shape=jax.ShapeDtypeStruct((plane, depth + 1, rows, width), kv_local.dtype),
        in_specs=[pl.BlockSpec(memory_space=pl.ANY)],
        out_specs=pl.BlockSpec(memory_space=pl.ANY),
        scratch_shapes=[
            pltpu.SemaphoreType.DMA((depth,)),
            pltpu.SemaphoreType.DMA((depth,)),
            pltpu.SemaphoreType.DMA((3, depth + 1)),
            pltpu.SemaphoreType.DMA((3, depth + 1)),
            pltpu.SemaphoreType.DMA(()),
        ],
        compiler_params=pltpu.CompilerParams(collective_id=0, has_side_effects=True),
    )(kv_local)


def project_kernel(n_head, att_ref, w_hbm, o_ref, w_buf, w_sem, send_buf, got, send_sem, recv_sem):
    me = lax.axis_index("head")
    row = lax.axis_index("ctx")
    cols = o_ref.shape[1]
    for d in list(range(1, n_head)) + [0]:
        pltpu.make_async_copy(
            w_hbm.at[:, pl.ds(pl.multiple_of(lax.rem(me + d, n_head) * cols, cols), cols)],
            w_buf.at[d], w_sem.at[d],
        ).start()
    barrier = pltpu.get_barrier_semaphore()
    for d in range(1, n_head):
        pl.semaphore_signal(
            barrier, 1, device_id=(row, lax.rem(me + d, n_head)), device_id_type=MESH_ID
        )
    pl.semaphore_wait(barrier, n_head - 1)

    def fetch(d):
        c0 = pl.multiple_of(lax.rem(me + d, n_head) * cols, cols)
        return pltpu.make_async_copy(w_hbm.at[:, pl.ds(c0, cols)], w_buf.at[d], w_sem.at[d])

    def part(d):
        fetch(d).wait()
        return jnp.dot(
            att_ref[...], w_buf[d], preferred_element_type=jnp.float32
        ).astype(jnp.bfloat16)

    def send(d):
        dst = lax.rem(me + d, n_head)
        return pltpu.make_async_remote_copy(
            src_ref=send_buf.at[d - 1],
            dst_ref=got.at[me],
            send_sem=send_sem.at[d - 1],
            recv_sem=recv_sem.at[d - 1],
            device_id=(row, dst),
            device_id_type=MESH_ID,
        )

    def arrival(d):
        src = lax.rem(me + n_head - d, n_head)
        return pltpu.make_async_remote_copy(
            src_ref=send_buf.at[d - 1],
            dst_ref=got.at[src],
            send_sem=send_sem.at[d - 1],
            recv_sem=recv_sem.at[d - 1],
            device_id=(row, src),
            device_id_type=MESH_ID,
        )

    send_buf[0] = part(1)
    for d in range(1, n_head):
        if d + 1 < n_head:
            send_buf[d] = part(d + 1)
        send(d).start()
    total = part(0).astype(jnp.float32)
    for d in range(1, n_head):
        send(d).wait_send()
        arrival(d).wait_recv()
        total = total + got[lax.rem(me + n_head - d, n_head)].astype(jnp.float32)
    o_ref[...] = total.astype(o_ref.dtype)


def project(att, out_weight, n_head):
    rows = att.shape[0]
    cols = out_weight.shape[1] // n_head
    vmem = pltpu.MemorySpace.VMEM if hasattr(pltpu, "MemorySpace") else pltpu.VMEM
    return pl.pallas_call(
        functools.partial(project_kernel, n_head),
        out_shape=jax.ShapeDtypeStruct((rows, cols), jnp.bfloat16),
        in_specs=[pl.BlockSpec(memory_space=vmem), pl.BlockSpec(memory_space=pl.ANY)],
        out_specs=pl.BlockSpec(memory_space=vmem),
        scratch_shapes=[
            pltpu.VMEM((n_head, out_weight.shape[0], cols), out_weight.dtype),
            pltpu.SemaphoreType.DMA((n_head,)),
            pltpu.VMEM((n_head - 1, rows, cols), jnp.bfloat16),
            pltpu.VMEM((n_head, rows, cols), jnp.bfloat16),
            pltpu.SemaphoreType.DMA((n_head - 1,)),
            pltpu.SemaphoreType.DMA((n_head - 1,)),
        ],
        compiler_params=pltpu.CompilerParams(collective_id=1, has_side_effects=True),
    )(att, out_weight)


def on_device(queries, key_rows, values, lengths, block_plan, inverse, mask_lo, out_weight):
    row_count, query_width = queries.shape
    group_size = query_width // HD
    here = lax.axis_index("ctx")
    first = here * row_count
    pos = first + jnp.arange(row_count, dtype=jnp.int32)
    doc_ends = jnp.cumsum(lengths).astype(jnp.int32)
    doc_start = jnp.max(jnp.where(doc_ends[None, :] <= pos[:, None], doc_ends[None, :], 0), axis=1)
    block_lo = lax.dynamic_slice_in_dim(mask_lo, here * (row_count // BLK), row_count // BLK)
    lo_tok = jnp.maximum(jnp.repeat(block_lo, BLK) * BLK, doc_start)
    qpos_rows = jnp.tile(pos, group_size)[None, :]
    lo_rows = jnp.tile(lo_tok, group_size)[None, :]
    n_q = row_count * group_size // TQ
    tile_lo = jnp.full((n_q,), jnp.min(lo_tok))
    tile_hi = jnp.full((n_q,), pos[-1])
    tile_lo_max = jnp.full((n_q,), jnp.max(lo_tok))
    tile_hi_min = jnp.full((n_q,), pos[0])

    kv_local = jnp.concatenate([key_rows, values], axis=1)
    n_ctx = lax.axis_size("ctx")
    plane = PLANE
    depth = min(n_ctx // plane - 1, -(-(LONGEST - 1) // (plane * row_count)))
    need_col = max(0, -(-(plane * row_count * depth - (LONGEST - 1) - (row_count - 1)) // row_count))
    need_col = need_col // (TK // SHARD) * (TK // SHARD)
    kv_win = gather_window(kv_local, depth, plane, n_ctx, need_col)
    kv_win = kv_win.reshape(-1, kv_win.shape[-1])
    base = (here // plane - depth) * plane * row_count
    span = kv_win.shape[0]
    t0 = (tile_lo - base) // TK
    t3 = jnp.minimum((tile_hi - base) // TK + 1, span // TK)
    t1 = jnp.clip((tile_lo_max - base + TK - 1) // TK, t0, t3)
    t2 = jnp.clip((tile_hi_min - base + 1) // TK, t1, t3)
    tiles = jnp.stack([t0, t1, t2, t3], axis=1).astype(jnp.int32)
    att = attend(queries, kv_win, qpos_rows - base, lo_rows - base, tiles, plane, depth + 1)

    return project(att, out_weight, lax.axis_size("head"))


def solution(mesh):
    in_specs = (
        P("ctx", "head"),
        P("ctx", "head"),
        P("ctx", "head"),
        P(),
        P("ctx"),
        P(),
        P(),
        P("head", None),
    )
    out_specs = P("ctx", "head")
    return jax.shard_map(
        on_device, mesh=mesh, in_specs=in_specs, out_specs=out_specs, check_vma=False
    )
```

```python
import functools

import jax
import jax.numpy as jnp
from jax import lax
from jax.experimental import pallas as pl
from jax.experimental.pallas import tpu as pltpu
from jax.sharding import PartitionSpec as P

HD = 128
BLK = 8
TQ = 1024
TK = 512
SHARD = 256
NEG_FILL = -1e30
LONGEST = 4352
PLANE = 4


def attn_kernel(plane, slots, tiles_ref, q_ref, kv_ref, qpos_ref, lo_ref, o_ref, m_sc, l_sc, acc_sc):
    n_q = q_ref.shape[0] * q_ref.shape[1] // (HD * TQ)
    scale = HD ** (-0.5)

    def q_body(qi, carry):
        r0 = pl.multiple_of(qi * TQ, TQ)
        heads = TQ // q_ref.shape[0]
        q = jnp.concatenate([
            q_ref[:, pl.ds(pl.multiple_of((qi * heads + g) * HD, HD), HD)] for g in range(heads)
        ], axis=0)
        qpos = qpos_ref[:, pl.ds(r0, TQ)]
        lo = lo_ref[:, pl.ds(r0, TQ)]
        m_sc[...] = jnp.full(m_sc.shape, NEG_FILL, jnp.float32)
        l_sc[...] = jnp.zeros(l_sc.shape, jnp.float32)
        acc_sc[...] = jnp.zeros(acc_sc.shape, jnp.float32)

        def k_step(kj, masked):
            c0 = pl.multiple_of(kj * TK, TK)
            at = []
            for piece in range(TK // SHARD):
                i = kj * (TK // SHARD) + piece
                at.append(pl.multiple_of((lax.rem(i, plane) * slots + i // plane) * 2 * SHARD, SHARD))
            s = jnp.concatenate([
                lax.dot_general(
                    kv_ref[pl.ds(a, SHARD), :], q, (((1,), (1,)), ((), ())),
                    preferred_element_type=jnp.float32,
                )
                for a in at
            ], axis=0) * scale
            if masked:
                kpos = c0 + lax.broadcasted_iota(jnp.int32, (TK, TQ), 0)
                ok = (kpos >= lo) & (kpos <= qpos)
                s = jnp.where(ok, s, NEG_FILL)
            m_prev = m_sc[...]
            m_new = jnp.maximum(m_prev, jnp.max(s, axis=0, keepdims=True))
            p = jnp.exp(s - m_new)
            if masked:
                p = jnp.where(ok, p, 0.0)
            fade = jnp.exp(m_prev - m_new)
            l_sc[...] = l_sc[...] * fade + jnp.sum(p, axis=0, keepdims=True)
            pb = p.astype(jnp.bfloat16)
            update = acc_sc[...] * fade
            for piece, a in enumerate(at):
                update = update + lax.dot_general(
                    kv_ref[pl.ds(a + SHARD, SHARD), :], pb[piece * SHARD:(piece + 1) * SHARD],
                    (((0,), (0,)), ((), ())), preferred_element_type=jnp.float32,
                )
            acc_sc[...] = update
            m_sc[...] = m_new

        def masked_body(kj, c):
            k_step(kj, True)
            return c

        def open_body(kj, c):
            k_step(kj, False)
            return c

        lax.fori_loop(tiles_ref[qi, 0], tiles_ref[qi, 1], masked_body, 0)
        lax.fori_loop(tiles_ref[qi, 1], tiles_ref[qi, 2], open_body, 0)
        lax.fori_loop(tiles_ref[qi, 2], tiles_ref[qi, 3], masked_body, 0)
        out = (acc_sc[...] / l_sc[...]).T.astype(o_ref.dtype)
        tokens = q_ref.shape[0]
        for g in range(heads):
            o_ref[:, pl.ds(pl.multiple_of((qi * heads + g) * HD, HD), HD)] = out[g * tokens:(g + 1) * tokens]
        return carry

    lax.fori_loop(0, n_q, q_body, 0)


def attend(q_rows, kv_all, qpos_rows, lo_rows, tiles, plane, slots):
    vmem = pltpu.MemorySpace.VMEM if hasattr(pltpu, "MemorySpace") else pltpu.VMEM
    return pl.pallas_call(
        functools.partial(attn_kernel, plane, slots),
        out_shape=jax.ShapeDtypeStruct(q_rows.shape, jnp.bfloat16),
        in_specs=[
            pl.BlockSpec(memory_space=pltpu.SMEM),
            pl.BlockSpec(memory_space=vmem),
            pl.BlockSpec(memory_space=vmem),
            pl.BlockSpec(memory_space=vmem),
            pl.BlockSpec(memory_space=vmem),
        ],
        out_specs=pl.BlockSpec(memory_space=vmem),
        scratch_shapes=[
            pltpu.VMEM((1, TQ), jnp.float32),
            pltpu.VMEM((1, TQ), jnp.float32),
            pltpu.VMEM((HD, TQ), jnp.float32),
        ],
    )(tiles, q_rows, kv_all, qpos_rows, lo_rows)


MESH_ID = pl.DeviceIdType.MESH


def window_kernel(depth, plane, n_ctx, need_col, k_ref, v_ref, win_ref, send1, recv1, send2, recv2, local_sem):
    me = lax.axis_index("ctx")
    h = lax.axis_index("head")
    z = me // plane
    r = me % plane
    n_z = n_ctx // plane
    mate = r + 1 - 2 * (r % 2)
    across = (r + 2) % plane
    far = across + 1 - 2 * (across % 2)
    barrier = pltpu.get_barrier_semaphore()

    @pl.when(z + 1 < n_z)
    def _():
        pl.semaphore_signal(barrier, 1, device_id=(me + plane, h), device_id_type=MESH_ID)

    @pl.when(z - 1 >= 0)
    def _():
        pl.semaphore_signal(barrier, 1, device_id=(me - plane, h), device_id_type=MESH_ID)

    for peer in (mate, across):
        pl.semaphore_signal(barrier, 1, device_id=(z * plane + peer, h), device_id_type=MESH_ID)
    pl.semaphore_wait(barrier, jnp.minimum(1, n_z - 1 - z) + jnp.minimum(1, z) + 2)
    local = [
        pltpu.make_async_copy(src, win_ref.at[r, depth, part], local_sem.at[part])
        for part, src in enumerate((k_ref, v_ref))
    ]
    for c in local:
        c.start()

    def wanted(d):
        return (d < depth) | (r >= need_col)

    def up(k):
        if k == 1:
            return [
                pltpu.make_async_remote_copy(
                    src_ref=src,
                    dst_ref=win_ref.at[r, depth - 1, part],
                    send_sem=send1.at[part * depth],
                    recv_sem=recv1.at[part * depth],
                    device_id=(me + plane, h),
                    device_id_type=MESH_ID,
                )
                for part, src in enumerate((k_ref, v_ref))
            ]
        return [pltpu.make_async_remote_copy(
            src_ref=win_ref.at[r, depth - k + 1],
            dst_ref=win_ref.at[r, depth - k],
            send_sem=send1.at[k - 1],
            recv_sem=recv1.at[k - 1],
            device_id=(me + plane, h),
            device_id_type=MESH_ID,
        )]

    def sends(k):
        return (z + 1 < n_z) & (z - (k - 1) >= 0) & wanted(k)

    def gets(k):
        return (z - k >= 0) & wanted(k)

    @pl.when(sends(1))
    def _():
        for c in up(1):
            c.start()

    def has(slot, col):
        return (z - (depth - slot) >= 0) & ((slot > 0) | (col >= need_col))

    def hop(idx, col, slot, to):
        return pltpu.make_async_remote_copy(
            src_ref=win_ref.at[col, slot],
            dst_ref=win_ref.at[col, slot],
            send_sem=send2.at[idx, slot],
            recv_sem=recv2.at[idx, slot],
            device_id=(z * plane + to, h),
            device_id_type=MESH_ID,
        )

    for c in local:
        c.wait()
    hop(0, r, depth, mate).start()
    hop(1, r, depth, across).start()
    for k in range(1, depth + 1):
        @pl.when(gets(k))
        def _():
            for c in up(k):
                c.wait_recv()
            hop(0, r, depth - k, mate).start()
            hop(1, r, depth - k, across).start()

        if k < depth:
            @pl.when(sends(k + 1))
            def _():
                for c in up(k + 1):
                    c.start()

    for k in range(1, depth + 1):
        @pl.when(sends(k))
        def _():
            for c in up(k):
                c.wait_send()

    for slot in range(depth, -1, -1):
        @pl.when(has(slot, across))
        def _():
            hop(1, across, slot, across).wait_recv()
            hop(2, across, slot, mate).start()

    for slot in range(depth + 1):
        @pl.when(has(slot, r))
        def _():
            hop(0, r, slot, mate).wait_send()
            hop(1, r, slot, across).wait_send()

        @pl.when(has(slot, across))
        def _():
            hop(2, across, slot, mate).wait_send()

        @pl.when(has(slot, mate))
        def _():
            hop(0, mate, slot, mate).wait_recv()

        @pl.when(has(slot, far))
        def _():
            hop(2, far, slot, mate).wait_recv()


def gather_window(key_rows, values, depth, plane, n_ctx, need_col):
    rows, width = key_rows.shape
    return pl.pallas_call(
        functools.partial(window_kernel, depth, plane, n_ctx, need_col),
        out_shape=jax.ShapeDtypeStruct((plane, depth + 1, 2, rows, width), key_rows.dtype),
        in_specs=[pl.BlockSpec(memory_space=pl.ANY)] * 2,
        out_specs=pl.BlockSpec(memory_space=pl.ANY),
        scratch_shapes=[
            pltpu.SemaphoreType.DMA((depth + 1,)),
            pltpu.SemaphoreType.DMA((depth + 1,)),
            pltpu.SemaphoreType.DMA((3, depth + 1)),
            pltpu.SemaphoreType.DMA((3, depth + 1)),
            pltpu.SemaphoreType.DMA((2,)),
        ],
        compiler_params=pltpu.CompilerParams(collective_id=0, has_side_effects=True),
    )(key_rows, values)


def project_kernel(n_head, att_ref, w_hbm, o_ref, w_buf, w_sem, send_buf, got, send_sem, recv_sem):
    me = lax.axis_index("head")
    row = lax.axis_index("ctx")
    cols = o_ref.shape[1]
    for d in list(range(1, n_head)) + [0]:
        pltpu.make_async_copy(
            w_hbm.at[:, pl.ds(pl.multiple_of(lax.rem(me + d, n_head) * cols, cols), cols)],
            w_buf.at[d], w_sem.at[d],
        ).start()
    barrier = pltpu.get_barrier_semaphore()
    for d in range(1, n_head):
        pl.semaphore_signal(
            barrier, 1, device_id=(row, lax.rem(me + d, n_head)), device_id_type=MESH_ID
        )
    pl.semaphore_wait(barrier, n_head - 1)

    def fetch(d):
        c0 = pl.multiple_of(lax.rem(me + d, n_head) * cols, cols)
        return pltpu.make_async_copy(w_hbm.at[:, pl.ds(c0, cols)], w_buf.at[d], w_sem.at[d])

    def part(d):
        fetch(d).wait()
        return jnp.dot(
            att_ref[...], w_buf[d], preferred_element_type=jnp.float32
        ).astype(jnp.bfloat16)

    def send(d):
        dst = lax.rem(me + d, n_head)
        return pltpu.make_async_remote_copy(
            src_ref=send_buf.at[d - 1],
            dst_ref=got.at[me],
            send_sem=send_sem.at[d - 1],
            recv_sem=recv_sem.at[d - 1],
            device_id=(row, dst),
            device_id_type=MESH_ID,
        )

    def arrival(d):
        src = lax.rem(me + n_head - d, n_head)
        return pltpu.make_async_remote_copy(
            src_ref=send_buf.at[d - 1],
            dst_ref=got.at[src],
            send_sem=send_sem.at[d - 1],
            recv_sem=recv_sem.at[d - 1],
            device_id=(row, src),
            device_id_type=MESH_ID,
        )

    send_buf[0] = part(1)
    for d in range(1, n_head):
        if d + 1 < n_head:
            send_buf[d] = part(d + 1)
        send(d).start()
    total = part(0).astype(jnp.float32)
    for d in range(1, n_head):
        send(d).wait_send()
        arrival(d).wait_recv()
        total = total + got[lax.rem(me + n_head - d, n_head)].astype(jnp.float32)
    o_ref[...] = total.astype(o_ref.dtype)


def project(att, out_weight, n_head):
    rows = att.shape[0]
    cols = out_weight.shape[1] // n_head
    vmem = pltpu.MemorySpace.VMEM if hasattr(pltpu, "MemorySpace") else pltpu.VMEM
    return pl.pallas_call(
        functools.partial(project_kernel, n_head),
        out_shape=jax.ShapeDtypeStruct((rows, cols), jnp.bfloat16),
        in_specs=[pl.BlockSpec(memory_space=vmem), pl.BlockSpec(memory_space=pl.ANY)],
        out_specs=pl.BlockSpec(memory_space=vmem),
        scratch_shapes=[
            pltpu.VMEM((n_head, out_weight.shape[0], cols), out_weight.dtype),
            pltpu.SemaphoreType.DMA((n_head,)),
            pltpu.VMEM((n_head - 1, rows, cols), jnp.bfloat16),
            pltpu.VMEM((n_head, rows, cols), jnp.bfloat16),
            pltpu.SemaphoreType.DMA((n_head - 1,)),
            pltpu.SemaphoreType.DMA((n_head - 1,)),
        ],
        compiler_params=pltpu.CompilerParams(collective_id=1, has_side_effects=True),
    )(att, out_weight)


def on_device(queries, key_rows, values, lengths, block_plan, inverse, mask_lo, out_weight):
    row_count, query_width = queries.shape
    group_size = query_width // HD
    here = lax.axis_index("ctx")
    first = here * row_count
    pos = first + jnp.arange(row_count, dtype=jnp.int32)
    doc_ends = jnp.cumsum(lengths).astype(jnp.int32)
    doc_start = jnp.max(jnp.where(doc_ends[None, :] <= pos[:, None], doc_ends[None, :], 0), axis=1)
    block_lo = lax.dynamic_slice_in_dim(mask_lo, here * (row_count // BLK), row_count // BLK)
    lo_tok = jnp.maximum(jnp.repeat(block_lo, BLK) * BLK, doc_start)
    qpos_rows = jnp.tile(pos, group_size)[None, :]
    lo_rows = jnp.tile(lo_tok, group_size)[None, :]
    n_q = row_count * group_size // TQ
    tile_lo = jnp.full((n_q,), jnp.min(lo_tok))
    tile_hi = jnp.full((n_q,), pos[-1])
    tile_lo_max = jnp.full((n_q,), jnp.max(lo_tok))
    tile_hi_min = jnp.full((n_q,), pos[0])

    n_ctx = lax.axis_size("ctx")
    plane = PLANE
    depth = min(n_ctx // plane - 1, -(-(LONGEST - 1) // (plane * row_count)))
    need_col = max(0, -(-(plane * row_count * depth - (LONGEST - 1) - (row_count - 1)) // row_count))
    need_col = need_col // (TK // SHARD) * (TK // SHARD)
    kv_win = gather_window(key_rows, values, depth, plane, n_ctx, need_col)
    kv_win = kv_win.reshape(-1, kv_win.shape[-1])
    base = (here // plane - depth) * plane * row_count
    span = kv_win.shape[0] // 2
    t0 = (tile_lo - base) // TK
    t3 = jnp.minimum((tile_hi - base) // TK + 1, span // TK)
    t1 = jnp.clip((tile_lo_max - base + TK - 1) // TK, t0, t3)
    t2 = jnp.clip((tile_hi_min - base + 1) // TK, t1, t3)
    tiles = jnp.stack([t0, t1, t2, t3], axis=1).astype(jnp.int32)
    att = attend(queries, kv_win, qpos_rows - base, lo_rows - base, tiles, plane, depth + 1)

    return project(att, out_weight, lax.axis_size("head"))


def solution(mesh):
    in_specs = (
        P("ctx", "head"),
        P("ctx", "head"),
        P("ctx", "head"),
        P(),
        P("ctx"),
        P(),
        P(),
        P("head", None),
    )
    out_specs = P("ctx", "head")
    return jax.shard_map(
        on_device, mesh=mesh, in_specs=in_specs, out_specs=out_specs, check_vma=False
    )
```

```python
import functools

import jax
import jax.numpy as jnp
from jax import lax
from jax.experimental import pallas as pl
from jax.experimental.pallas import tpu as pltpu
from jax.sharding import PartitionSpec as P

HD = 128
BLK = 8
TQ = 1024
TK = 512
SHARD = 256
NEG_FILL = -1e30
LONGEST = 4352
PLANE = 4


def attn_kernel(plane, slots, tiles_ref, q_ref, kv_ref, qpos_ref, lo_ref, o_ref, m_sc, l_sc, acc_sc):
    n_q = q_ref.shape[0] * q_ref.shape[1] // (HD * TQ)
    scale = HD ** (-0.5)

    def q_body(qi, carry):
        r0 = pl.multiple_of(qi * TQ, TQ)
        heads = TQ // q_ref.shape[0]
        q = jnp.concatenate([
            q_ref[:, pl.ds(pl.multiple_of((qi * heads + g) * HD, HD), HD)] for g in range(heads)
        ], axis=0)
        qpos = qpos_ref[:, pl.ds(r0, TQ)]
        lo = lo_ref[:, pl.ds(r0, TQ)]
        m_sc[...] = jnp.full(m_sc.shape, NEG_FILL, jnp.float32)
        l_sc[...] = jnp.zeros(l_sc.shape, jnp.float32)
        acc_sc[...] = jnp.zeros(acc_sc.shape, jnp.float32)

        def k_step(kj, masked):
            c0 = pl.multiple_of(kj * TK, TK)
            at = []
            for piece in range(TK // SHARD):
                i = kj * (TK // SHARD) + piece
                at.append(pl.multiple_of((lax.rem(i, plane) * slots + i // plane) * SHARD, SHARD))
            s = jnp.concatenate([
                lax.dot_general(
                    kv_ref[pl.ds(a, SHARD), pl.ds(0, HD)], q, (((1,), (1,)), ((), ())),
                    preferred_element_type=jnp.float32,
                )
                for a in at
            ], axis=0) * scale
            if masked:
                kpos = c0 + lax.broadcasted_iota(jnp.int32, (TK, TQ), 0)
                ok = (kpos >= lo) & (kpos <= qpos)
                s = jnp.where(ok, s, NEG_FILL)
            m_prev = m_sc[...]
            m_new = jnp.maximum(m_prev, jnp.max(s, axis=0, keepdims=True))
            p = jnp.exp(s - m_new)
            if masked:
                p = jnp.where(ok, p, 0.0)
            fade = jnp.exp(m_prev - m_new)
            l_sc[...] = l_sc[...] * fade + jnp.sum(p, axis=0, keepdims=True)
            pb = p.astype(jnp.bfloat16)
            update = acc_sc[...] * fade
            for piece, a in enumerate(at):
                update = update + lax.dot_general(
                    kv_ref[pl.ds(a, SHARD), pl.ds(HD, HD)], pb[piece * SHARD:(piece + 1) * SHARD],
                    (((0,), (0,)), ((), ())), preferred_element_type=jnp.float32,
                )
            acc_sc[...] = update
            m_sc[...] = m_new

        def masked_body(kj, c):
            k_step(kj, True)
            return c

        def open_body(kj, c):
            k_step(kj, False)
            return c

        lax.fori_loop(tiles_ref[qi, 0], tiles_ref[qi, 1], masked_body, 0)
        lax.fori_loop(tiles_ref[qi, 1], tiles_ref[qi, 2], open_body, 0)
        lax.fori_loop(tiles_ref[qi, 2], tiles_ref[qi, 3], masked_body, 0)
        out = (acc_sc[...] / l_sc[...]).T.astype(o_ref.dtype)
        tokens = q_ref.shape[0]
        for g in range(heads):
            o_ref[:, pl.ds(pl.multiple_of((qi * heads + g) * HD, HD), HD)] = out[g * tokens:(g + 1) * tokens]
        return carry

    lax.fori_loop(0, n_q, q_body, 0)


def attend(q_rows, kv_all, qpos_rows, lo_rows, tiles, plane, slots):
    vmem = pltpu.MemorySpace.VMEM if hasattr(pltpu, "MemorySpace") else pltpu.VMEM
    return pl.pallas_call(
        functools.partial(attn_kernel, plane, slots),
        out_shape=jax.ShapeDtypeStruct(q_rows.shape, jnp.bfloat16),
        in_specs=[
            pl.BlockSpec(memory_space=pltpu.SMEM),
            pl.BlockSpec(memory_space=vmem),
            pl.BlockSpec(memory_space=vmem),
            pl.BlockSpec(memory_space=vmem),
            pl.BlockSpec(memory_space=vmem),
        ],
        out_specs=pl.BlockSpec(memory_space=vmem),
        scratch_shapes=[
            pltpu.VMEM((1, TQ), jnp.float32),
            pltpu.VMEM((1, TQ), jnp.float32),
            pltpu.VMEM((HD, TQ), jnp.float32),
        ],
    )(tiles, q_rows, kv_all, qpos_rows, lo_rows)


MESH_ID = pl.DeviceIdType.MESH


def window_kernel(depth, plane, n_ctx, need_col, kv_ref, win_ref, send1, recv1, send2, recv2, local_sem):
    me = lax.axis_index("ctx")
    h = lax.axis_index("head")
    z = me // plane
    r = me % plane
    n_z = n_ctx // plane
    mate = r + 1 - 2 * (r % 2)
    across = (r + 2) % plane
    far = across + 1 - 2 * (across % 2)
    barrier = pltpu.get_barrier_semaphore()

    @pl.when(z + 1 < n_z)
    def _():
        pl.semaphore_signal(barrier, 1, device_id=(me + plane, h), device_id_type=MESH_ID)

    @pl.when(z - 1 >= 0)
    def _():
        pl.semaphore_signal(barrier, 1, device_id=(me - plane, h), device_id_type=MESH_ID)

    for peer in (mate, across):
        pl.semaphore_signal(barrier, 1, device_id=(z * plane + peer, h), device_id_type=MESH_ID)
    pl.semaphore_wait(barrier, jnp.minimum(1, n_z - 1 - z) + jnp.minimum(1, z) + 2)
    local = pltpu.make_async_copy(kv_ref, win_ref.at[r, depth], local_sem)
    local.start()

    def wanted(d):
        return (d < depth) | (r >= need_col)

    def up(k):
        return pltpu.make_async_remote_copy(
            src_ref=kv_ref if k == 1 else win_ref.at[r, depth - k + 1],
            dst_ref=win_ref.at[r, depth - k],
            send_sem=send1.at[k - 1],
            recv_sem=recv1.at[k - 1],
            device_id=(me + plane, h),
            device_id_type=MESH_ID,
        )

    def sends(k):
        return (z + 1 < n_z) & (z - (k - 1) >= 0) & wanted(k)

    def gets(k):
        return (z - k >= 0) & wanted(k)

    @pl.when(sends(1))
    def _():
        up(1).start()

    def has(slot, col):
        return (z - (depth - slot) >= 0) & ((slot > 0) | (col >= need_col))

    def hop(idx, col, slot, to):
        return pltpu.make_async_remote_copy(
            src_ref=win_ref.at[col, slot],
            dst_ref=win_ref.at[col, slot],
            send_sem=send2.at[idx, slot],
            recv_sem=recv2.at[idx, slot],
            device_id=(z * plane + to, h),
            device_id_type=MESH_ID,
        )

    local.wait()
    hop(0, r, depth, mate).start()
    hop(1, r, depth, across).start()
    for k in range(1, depth + 1):
        @pl.when(gets(k))
        def _():
            up(k).wait_recv()
            hop(0, r, depth - k, mate).start()
            hop(1, r, depth - k, across).start()

        if k < depth:
            @pl.when(sends(k + 1))
            def _():
                up(k + 1).start()

    for k in range(1, depth + 1):
        @pl.when(sends(k))
        def _():
            up(k).wait_send()

    for slot in range(depth, -1, -1):
        @pl.when(has(slot, across))
        def _():
            hop(1, across, slot, across).wait_recv()
            hop(2, across, slot, mate).start()

    for slot in range(depth + 1):
        @pl.when(has(slot, r))
        def _():
            hop(0, r, slot, mate).wait_send()
            hop(1, r, slot, across).wait_send()

        @pl.when(has(slot, across))
        def _():
            hop(2, across, slot, mate).wait_send()

        @pl.when(has(slot, mate))
        def _():
            hop(0, mate, slot, mate).wait_recv()

        @pl.when(has(slot, far))
        def _():
            hop(2, far, slot, mate).wait_recv()


def gather_window(kv_local, depth, plane, n_ctx, need_col):
    rows, width = kv_local.shape
    return pl.pallas_call(
        functools.partial(window_kernel, depth, plane, n_ctx, need_col),
        out_shape=jax.ShapeDtypeStruct((plane, depth + 1, rows, width), kv_local.dtype),
        in_specs=[pl.BlockSpec(memory_space=pl.ANY)],
        out_specs=pl.BlockSpec(memory_space=pl.ANY),
        scratch_shapes=[
            pltpu.SemaphoreType.DMA((depth,)),
            pltpu.SemaphoreType.DMA((depth,)),
            pltpu.SemaphoreType.DMA((3, depth + 1)),
            pltpu.SemaphoreType.DMA((3, depth + 1)),
            pltpu.SemaphoreType.DMA(()),
        ],
        compiler_params=pltpu.CompilerParams(collective_id=0, has_side_effects=True),
    )(kv_local)


def project_kernel(n_head, att_ref, w_hbm, o_ref, w_buf, w_sem, send_buf, got, send_sem, recv_sem):
    me = lax.axis_index("head")
    row = lax.axis_index("ctx")
    cols = o_ref.shape[1]
    for d in list(range(1, n_head)) + [0]:
        pltpu.make_async_copy(
            w_hbm.at[:, pl.ds(pl.multiple_of(lax.rem(me + d, n_head) * cols, cols), cols)],
            w_buf.at[d], w_sem.at[d],
        ).start()
    barrier = pltpu.get_barrier_semaphore()
    for d in range(1, n_head):
        pl.semaphore_signal(
            barrier, 1, device_id=(row, lax.rem(me + d, n_head)), device_id_type=MESH_ID
        )
    pl.semaphore_wait(barrier, n_head - 1)

    def fetch(d):
        c0 = pl.multiple_of(lax.rem(me + d, n_head) * cols, cols)
        return pltpu.make_async_copy(w_hbm.at[:, pl.ds(c0, cols)], w_buf.at[d], w_sem.at[d])

    def part(d):
        fetch(d).wait()
        return jnp.dot(
            att_ref[...], w_buf[d], preferred_element_type=jnp.float32
        ).astype(jnp.bfloat16)

    def send(d):
        dst = lax.rem(me + d, n_head)
        return pltpu.make_async_remote_copy(
            src_ref=send_buf.at[d - 1],
            dst_ref=got.at[me],
            send_sem=send_sem.at[d - 1],
            recv_sem=recv_sem.at[d - 1],
            device_id=(row, dst),
            device_id_type=MESH_ID,
        )

    def arrival(d):
        src = lax.rem(me + n_head - d, n_head)
        return pltpu.make_async_remote_copy(
            src_ref=send_buf.at[d - 1],
            dst_ref=got.at[src],
            send_sem=send_sem.at[d - 1],
            recv_sem=recv_sem.at[d - 1],
            device_id=(row, src),
            device_id_type=MESH_ID,
        )

    send_buf[0] = part(1)
    for d in range(1, n_head):
        if d + 1 < n_head:
            send_buf[d] = part(d + 1)
        send(d).start()
    total = part(0).astype(jnp.float32)
    for d in range(1, n_head):
        send(d).wait_send()
        arrival(d).wait_recv()
        total = total + got[lax.rem(me + n_head - d, n_head)].astype(jnp.float32)
    o_ref[...] = total


def project(att, out_weight, n_head):
    rows = att.shape[0]
    cols = out_weight.shape[1] // n_head
    vmem = pltpu.MemorySpace.VMEM if hasattr(pltpu, "MemorySpace") else pltpu.VMEM
    return pl.pallas_call(
        functools.partial(project_kernel, n_head),
        out_shape=jax.ShapeDtypeStruct((rows, cols), jnp.float32),
        in_specs=[pl.BlockSpec(memory_space=vmem), pl.BlockSpec(memory_space=pl.ANY)],
        out_specs=pl.BlockSpec(memory_space=vmem),
        scratch_shapes=[
            pltpu.VMEM((n_head, out_weight.shape[0], cols), out_weight.dtype),
            pltpu.SemaphoreType.DMA((n_head,)),
            pltpu.VMEM((n_head - 1, rows, cols), jnp.bfloat16),
            pltpu.VMEM((n_head, rows, cols), jnp.bfloat16),
            pltpu.SemaphoreType.DMA((n_head - 1,)),
            pltpu.SemaphoreType.DMA((n_head - 1,)),
        ],
        compiler_params=pltpu.CompilerParams(collective_id=1, has_side_effects=True),
    )(att, out_weight)


def on_device(queries, key_rows, values, lengths, block_plan, inverse, mask_lo, out_weight):
    row_count, query_width = queries.shape
    group_size = query_width // HD
    here = lax.axis_index("ctx")
    first = here * row_count
    pos = first + jnp.arange(row_count, dtype=jnp.int32)
    doc_ends = jnp.cumsum(lengths).astype(jnp.int32)
    doc_start = jnp.max(jnp.where(doc_ends[None, :] <= pos[:, None], doc_ends[None, :], 0), axis=1)
    block_lo = lax.dynamic_slice_in_dim(mask_lo, here * (row_count // BLK), row_count // BLK)
    lo_tok = jnp.maximum(jnp.repeat(block_lo, BLK) * BLK, doc_start)
    qpos_rows = jnp.tile(pos, group_size)[None, :]
    lo_rows = jnp.tile(lo_tok, group_size)[None, :]
    n_q = row_count * group_size // TQ
    tile_lo = jnp.full((n_q,), jnp.min(lo_tok))
    tile_hi = jnp.full((n_q,), pos[-1])
    tile_lo_max = jnp.full((n_q,), jnp.max(lo_tok))
    tile_hi_min = jnp.full((n_q,), pos[0])

    kv_local = jnp.concatenate([key_rows, values], axis=1)
    n_ctx = lax.axis_size("ctx")
    plane = PLANE
    depth = min(n_ctx // plane - 1, -(-(LONGEST - 1) // (plane * row_count)))
    need_col = max(0, -(-(plane * row_count * depth - (LONGEST - 1) - (row_count - 1)) // row_count))
    need_col = need_col // (TK // SHARD) * (TK // SHARD)
    kv_win = gather_window(kv_local, depth, plane, n_ctx, need_col)
    kv_win = kv_win.reshape(-1, kv_win.shape[-1])
    base = (here // plane - depth) * plane * row_count
    span = kv_win.shape[0]
    t0 = (tile_lo - base) // TK
    t3 = jnp.minimum((tile_hi - base) // TK + 1, span // TK)
    t1 = jnp.clip((tile_lo_max - base + TK - 1) // TK, t0, t3)
    t2 = jnp.clip((tile_hi_min - base + 1) // TK, t1, t3)
    tiles = jnp.stack([t0, t1, t2, t3], axis=1).astype(jnp.int32)
    att = attend(queries, kv_win, qpos_rows - base, lo_rows - base, tiles, plane, depth + 1)

    return project(att, out_weight, lax.axis_size("head")).astype(jnp.bfloat16)


def solution(mesh):
    in_specs = (
        P("ctx", "head"),
        P("ctx", "head"),
        P("ctx", "head"),
        P(),
        P("ctx"),
        P(),
        P(),
        P("head", None),
    )
    out_specs = P("ctx", "head")
    return jax.shard_map(
        on_device, mesh=mesh, in_specs=in_specs, out_specs=out_specs, check_vma=False
    )
```

```python
import functools

import jax
import jax.numpy as jnp
from jax import lax
from jax.experimental import pallas as pl
from jax.experimental.pallas import tpu as pltpu
from jax.sharding import PartitionSpec as P

HD = 128
BLK = 8
TQ = 1024
TK = 512
SHARD = 256
NEG_FILL = -1e30
LONGEST = 4352
PLANE = 4


def attn_kernel(plane, slots, tiles_ref, q_ref, kv_ref, qpos_ref, lo_ref, o_ref, m_sc, l_sc, acc_sc):
    n_q = q_ref.shape[0] * q_ref.shape[1] // (HD * TQ)
    scale = HD ** (-0.5)

    def q_body(qi, carry):
        r0 = pl.multiple_of(qi * TQ, TQ)
        heads = TQ // q_ref.shape[0]
        q = jnp.concatenate([
            q_ref[:, pl.ds(pl.multiple_of((qi * heads + g) * HD, HD), HD)] for g in range(heads)
        ], axis=0)
        qpos = jnp.concatenate([qpos_ref[...]] * heads, axis=1)
        lo = jnp.concatenate([lo_ref[...]] * heads, axis=1)
        m_sc[...] = jnp.full(m_sc.shape, NEG_FILL, jnp.float32)
        l_sc[...] = jnp.zeros(l_sc.shape, jnp.float32)
        acc_sc[...] = jnp.zeros(acc_sc.shape, jnp.float32)

        def k_step(kj, masked):
            c0 = pl.multiple_of(kj * TK, TK)
            at = []
            for piece in range(TK // SHARD):
                i = kj * (TK // SHARD) + piece
                at.append(pl.multiple_of((lax.rem(i, plane) * slots + i // plane) * SHARD, SHARD))
            s = jnp.concatenate([
                lax.dot_general(
                    kv_ref[pl.ds(a, SHARD), pl.ds(0, HD)], q, (((1,), (1,)), ((), ())),
                    preferred_element_type=jnp.float32,
                )
                for a in at
            ], axis=0) * scale
            if masked:
                kpos = c0 + lax.broadcasted_iota(jnp.int32, (TK, TQ), 0)
                ok = (kpos >= lo) & (kpos <= qpos)
                s = jnp.where(ok, s, NEG_FILL)
            m_prev = m_sc[...]
            m_new = jnp.maximum(m_prev, jnp.max(s, axis=0, keepdims=True))
            p = jnp.exp(s - m_new)
            if masked:
                p = jnp.where(ok, p, 0.0)
            fade = jnp.exp(m_prev - m_new)
            l_sc[...] = l_sc[...] * fade + jnp.sum(p, axis=0, keepdims=True)
            pb = p.astype(jnp.bfloat16)
            update = acc_sc[...] * fade
            for piece, a in enumerate(at):
                update = update + lax.dot_general(
                    kv_ref[pl.ds(a, SHARD), pl.ds(HD, HD)], pb[piece * SHARD:(piece + 1) * SHARD],
                    (((0,), (0,)), ((), ())), preferred_element_type=jnp.float32,
                )
            acc_sc[...] = update
            m_sc[...] = m_new

        def masked_body(kj, c):
            k_step(kj, True)
            return c

        def open_body(kj, c):
            k_step(kj, False)
            return c

        lax.fori_loop(tiles_ref[qi, 0], tiles_ref[qi, 1], masked_body, 0)
        lax.fori_loop(tiles_ref[qi, 1], tiles_ref[qi, 2], open_body, 0)
        lax.fori_loop(tiles_ref[qi, 2], tiles_ref[qi, 3], masked_body, 0)
        out = (acc_sc[...] / l_sc[...]).T.astype(o_ref.dtype)
        tokens = q_ref.shape[0]
        for g in range(heads):
            o_ref[:, pl.ds(pl.multiple_of((qi * heads + g) * HD, HD), HD)] = out[g * tokens:(g + 1) * tokens]
        return carry

    lax.fori_loop(0, n_q, q_body, 0)


def attend(q_rows, kv_all, qpos_rows, lo_rows, tiles, plane, slots):
    vmem = pltpu.MemorySpace.VMEM if hasattr(pltpu, "MemorySpace") else pltpu.VMEM
    return pl.pallas_call(
        functools.partial(attn_kernel, plane, slots),
        out_shape=jax.ShapeDtypeStruct(q_rows.shape, jnp.bfloat16),
        in_specs=[
            pl.BlockSpec(memory_space=pltpu.SMEM),
            pl.BlockSpec(memory_space=vmem),
            pl.BlockSpec(memory_space=vmem),
            pl.BlockSpec(memory_space=vmem),
            pl.BlockSpec(memory_space=vmem),
        ],
        out_specs=pl.BlockSpec(memory_space=vmem),
        scratch_shapes=[
            pltpu.VMEM((1, TQ), jnp.float32),
            pltpu.VMEM((1, TQ), jnp.float32),
            pltpu.VMEM((HD, TQ), jnp.float32),
        ],
    )(tiles, q_rows, kv_all, qpos_rows, lo_rows)


MESH_ID = pl.DeviceIdType.MESH


def window_kernel(depth, plane, n_ctx, need_col, kv_ref, win_ref, send1, recv1, send2, recv2, local_sem):
    me = lax.axis_index("ctx")
    h = lax.axis_index("head")
    z = me // plane
    r = me % plane
    n_z = n_ctx // plane
    mate = r + 1 - 2 * (r % 2)
    across = (r + 2) % plane
    far = across + 1 - 2 * (across % 2)
    barrier = pltpu.get_barrier_semaphore()

    @pl.when(z + 1 < n_z)
    def _():
        pl.semaphore_signal(barrier, 1, device_id=(me + plane, h), device_id_type=MESH_ID)

    @pl.when(z - 1 >= 0)
    def _():
        pl.semaphore_signal(barrier, 1, device_id=(me - plane, h), device_id_type=MESH_ID)

    for peer in (mate, across):
        pl.semaphore_signal(barrier, 1, device_id=(z * plane + peer, h), device_id_type=MESH_ID)
    pl.semaphore_wait(barrier, jnp.minimum(1, n_z - 1 - z) + jnp.minimum(1, z) + 2)
    local = pltpu.make_async_copy(kv_ref, win_ref.at[r, depth], local_sem)
    local.start()

    def wanted(d):
        return (d < depth) | (r >= need_col)

    def up(k):
        return pltpu.make_async_remote_copy(
            src_ref=kv_ref if k == 1 else win_ref.at[r, depth - k + 1],
            dst_ref=win_ref.at[r, depth - k],
            send_sem=send1.at[k - 1],
            recv_sem=recv1.at[k - 1],
            device_id=(me + plane, h),
            device_id_type=MESH_ID,
        )

    def sends(k):
        return (z + 1 < n_z) & (z - (k - 1) >= 0) & wanted(k)

    def gets(k):
        return (z - k >= 0) & wanted(k)

    @pl.when(sends(1))
    def _():
        up(1).start()

    def has(slot, col):
        return (z - (depth - slot) >= 0) & ((slot > 0) | (col >= need_col))

    def hop(idx, col, slot, to):
        return pltpu.make_async_remote_copy(
            src_ref=win_ref.at[col, slot],
            dst_ref=win_ref.at[col, slot],
            send_sem=send2.at[idx, slot],
            recv_sem=recv2.at[idx, slot],
            device_id=(z * plane + to, h),
            device_id_type=MESH_ID,
        )

    local.wait()
    hop(0, r, depth, mate).start()
    hop(1, r, depth, across).start()
    for k in range(1, depth + 1):
        @pl.when(gets(k))
        def _():
            up(k).wait_recv()
            hop(0, r, depth - k, mate).start()
            hop(1, r, depth - k, across).start()

        if k < depth:
            @pl.when(sends(k + 1))
            def _():
                up(k + 1).start()

    for k in range(1, depth + 1):
        @pl.when(sends(k))
        def _():
            up(k).wait_send()

    for slot in range(depth, -1, -1):
        @pl.when(has(slot, across))
        def _():
            hop(1, across, slot, across).wait_recv()
            hop(2, across, slot, mate).start()

    for slot in range(depth + 1):
        @pl.when(has(slot, r))
        def _():
            hop(0, r, slot, mate).wait_send()
            hop(1, r, slot, across).wait_send()

        @pl.when(has(slot, across))
        def _():
            hop(2, across, slot, mate).wait_send()

        @pl.when(has(slot, mate))
        def _():
            hop(0, mate, slot, mate).wait_recv()

        @pl.when(has(slot, far))
        def _():
            hop(2, far, slot, mate).wait_recv()


def gather_window(kv_local, depth, plane, n_ctx, need_col):
    rows, width = kv_local.shape
    return pl.pallas_call(
        functools.partial(window_kernel, depth, plane, n_ctx, need_col),
        out_shape=jax.ShapeDtypeStruct((plane, depth + 1, rows, width), kv_local.dtype),
        in_specs=[pl.BlockSpec(memory_space=pl.ANY)],
        out_specs=pl.BlockSpec(memory_space=pl.ANY),
        scratch_shapes=[
            pltpu.SemaphoreType.DMA((depth,)),
            pltpu.SemaphoreType.DMA((depth,)),
            pltpu.SemaphoreType.DMA((3, depth + 1)),
            pltpu.SemaphoreType.DMA((3, depth + 1)),
            pltpu.SemaphoreType.DMA(()),
        ],
        compiler_params=pltpu.CompilerParams(collective_id=0, has_side_effects=True),
    )(kv_local)


def project_kernel(n_head, att_ref, w_hbm, o_ref, w_buf, w_sem, send_buf, got, send_sem, recv_sem):
    me = lax.axis_index("head")
    row = lax.axis_index("ctx")
    cols = o_ref.shape[1]
    for d in list(range(1, n_head)) + [0]:
        pltpu.make_async_copy(
            w_hbm.at[:, pl.ds(pl.multiple_of(lax.rem(me + d, n_head) * cols, cols), cols)],
            w_buf.at[d], w_sem.at[d],
        ).start()
    barrier = pltpu.get_barrier_semaphore()
    for d in range(1, n_head):
        pl.semaphore_signal(
            barrier, 1, device_id=(row, lax.rem(me + d, n_head)), device_id_type=MESH_ID
        )
    pl.semaphore_wait(barrier, n_head - 1)

    def fetch(d):
        c0 = pl.multiple_of(lax.rem(me + d, n_head) * cols, cols)
        return pltpu.make_async_copy(w_hbm.at[:, pl.ds(c0, cols)], w_buf.at[d], w_sem.at[d])

    def part(d):
        fetch(d).wait()
        return jnp.dot(
            att_ref[...], w_buf[d], preferred_element_type=jnp.float32
        ).astype(jnp.bfloat16)

    def send(d):
        dst = lax.rem(me + d, n_head)
        return pltpu.make_async_remote_copy(
            src_ref=send_buf.at[d - 1],
            dst_ref=got.at[me],
            send_sem=send_sem.at[d - 1],
            recv_sem=recv_sem.at[d - 1],
            device_id=(row, dst),
            device_id_type=MESH_ID,
        )

    def arrival(d):
        src = lax.rem(me + n_head - d, n_head)
        return pltpu.make_async_remote_copy(
            src_ref=send_buf.at[d - 1],
            dst_ref=got.at[src],
            send_sem=send_sem.at[d - 1],
            recv_sem=recv_sem.at[d - 1],
            device_id=(row, src),
            device_id_type=MESH_ID,
        )

    send_buf[0] = part(1)
    for d in range(1, n_head):
        if d + 1 < n_head:
            send_buf[d] = part(d + 1)
        send(d).start()
    total = part(0).astype(jnp.float32)
    for d in range(1, n_head):
        send(d).wait_send()
        arrival(d).wait_recv()
        total = total + got[lax.rem(me + n_head - d, n_head)].astype(jnp.float32)
    o_ref[...] = total.astype(o_ref.dtype)


def project(att, out_weight, n_head):
    rows = att.shape[0]
    cols = out_weight.shape[1] // n_head
    vmem = pltpu.MemorySpace.VMEM if hasattr(pltpu, "MemorySpace") else pltpu.VMEM
    return pl.pallas_call(
        functools.partial(project_kernel, n_head),
        out_shape=jax.ShapeDtypeStruct((rows, cols), jnp.bfloat16),
        in_specs=[pl.BlockSpec(memory_space=vmem), pl.BlockSpec(memory_space=pl.ANY)],
        out_specs=pl.BlockSpec(memory_space=vmem),
        scratch_shapes=[
            pltpu.VMEM((n_head, out_weight.shape[0], cols), out_weight.dtype),
            pltpu.SemaphoreType.DMA((n_head,)),
            pltpu.VMEM((n_head - 1, rows, cols), jnp.bfloat16),
            pltpu.VMEM((n_head, rows, cols), jnp.bfloat16),
            pltpu.SemaphoreType.DMA((n_head - 1,)),
            pltpu.SemaphoreType.DMA((n_head - 1,)),
        ],
        compiler_params=pltpu.CompilerParams(collective_id=1, has_side_effects=True),
    )(att, out_weight)


def on_device(queries, key_rows, values, lengths, block_plan, inverse, mask_lo, out_weight):
    row_count, query_width = queries.shape
    group_size = query_width // HD
    here = lax.axis_index("ctx")
    first = here * row_count
    pos = first + jnp.arange(row_count, dtype=jnp.int32)
    doc_ends = jnp.cumsum(lengths).astype(jnp.int32)
    doc_start = jnp.max(jnp.where(doc_ends[None, :] <= pos[:, None], doc_ends[None, :], 0), axis=1)
    block_lo = lax.dynamic_slice_in_dim(mask_lo, here * (row_count // BLK), row_count // BLK)
    lo_tok = jnp.maximum(jnp.repeat(block_lo, BLK) * BLK, doc_start)
    qpos_rows = pos[None, :]
    lo_rows = lo_tok[None, :]
    n_q = row_count * group_size // TQ
    tile_lo = jnp.full((n_q,), jnp.min(lo_tok))
    tile_hi = jnp.full((n_q,), pos[-1])
    tile_lo_max = jnp.full((n_q,), jnp.max(lo_tok))
    tile_hi_min = jnp.full((n_q,), pos[0])

    kv_local = jnp.concatenate([key_rows, values], axis=1)
    n_ctx = lax.axis_size("ctx")
    plane = PLANE
    depth = min(n_ctx // plane - 1, -(-(LONGEST - 1) // (plane * row_count)))
    need_col = max(0, -(-(plane * row_count * depth - (LONGEST - 1) - (row_count - 1)) // row_count))
    need_col = need_col // (TK // SHARD) * (TK // SHARD)
    kv_win = gather_window(kv_local, depth, plane, n_ctx, need_col)
    kv_win = kv_win.reshape(-1, kv_win.shape[-1])
    base = (here // plane - depth) * plane * row_count
    span = kv_win.shape[0]
    t0 = (tile_lo - base) // TK
    t3 = jnp.minimum((tile_hi - base) // TK + 1, span // TK)
    t1 = jnp.clip((tile_lo_max - base + TK - 1) // TK, t0, t3)
    t2 = jnp.clip((tile_hi_min - base + 1) // TK, t1, t3)
    tiles = jnp.stack([t0, t1, t2, t3], axis=1).astype(jnp.int32)
    att = attend(queries, kv_win, qpos_rows - base, lo_rows - base, tiles, plane, depth + 1)

    return project(att, out_weight, lax.axis_size("head"))


def solution(mesh):
    in_specs = (
        P("ctx", "head"),
        P("ctx", "head"),
        P("ctx", "head"),
        P(),
        P("ctx"),
        P(),
        P(),
        P("head", None),
    )
    out_specs = P("ctx", "head")
    return jax.shard_map(
        on_device, mesh=mesh, in_specs=in_specs, out_specs=out_specs, check_vma=False
    )
```

```python
import functools

import jax
import jax.numpy as jnp
from jax import lax
from jax.experimental import pallas as pl
from jax.experimental.pallas import tpu as pltpu
from jax.sharding import PartitionSpec as P

HD = 128
BLK = 8
TQ = 1024
TK = 512
SHARD = 256
NEG_FILL = -1e30
LONGEST = 4352
PLANE = 4


def attn_kernel(plane, slots, tiles_ref, q_ref, kv_ref, qpos_ref, lo_ref, o_ref, m_sc, l_sc, acc_sc):
    n_q = q_ref.shape[0] * q_ref.shape[1] // (HD * TQ)
    scale = HD ** (-0.5)

    def q_body(qi, carry):
        r0 = pl.multiple_of(qi * TQ, TQ)
        heads = TQ // q_ref.shape[0]
        q = jnp.concatenate([
            q_ref[:, pl.ds(pl.multiple_of((qi * heads + g) * HD, HD), HD)] for g in range(heads)
        ], axis=0)
        qpos = jnp.concatenate([qpos_ref[...]] * heads, axis=1)
        lo = jnp.concatenate([lo_ref[...]] * heads, axis=1)
        m_sc[...] = jnp.full(m_sc.shape, NEG_FILL, jnp.float32)
        l_sc[...] = jnp.zeros(l_sc.shape, jnp.float32)
        acc_sc[...] = jnp.zeros(acc_sc.shape, jnp.float32)

        def k_step(kj, masked):
            c0 = pl.multiple_of(kj * TK, TK)
            at = []
            for piece in range(TK // SHARD):
                i = kj * (TK // SHARD) + piece
                at.append(pl.multiple_of((lax.rem(i, plane) * slots + i // plane) * 2 * SHARD, SHARD))
            s = jnp.concatenate([
                lax.dot_general(
                    kv_ref[pl.ds(a, SHARD), :], q, (((1,), (1,)), ((), ())),
                    preferred_element_type=jnp.float32,
                )
                for a in at
            ], axis=0) * scale
            if masked:
                kpos = c0 + lax.broadcasted_iota(jnp.int32, (TK, TQ), 0)
                ok = (kpos >= lo) & (kpos <= qpos)
                s = jnp.where(ok, s, NEG_FILL)
            m_prev = m_sc[...]
            m_new = jnp.maximum(m_prev, jnp.max(s, axis=0, keepdims=True))
            p = jnp.exp(s - m_new)
            if masked:
                p = jnp.where(ok, p, 0.0)
            fade = jnp.exp(m_prev - m_new)
            l_sc[...] = l_sc[...] * fade + jnp.sum(p, axis=0, keepdims=True)
            pb = p.astype(jnp.bfloat16)
            update = acc_sc[...] * fade
            for piece, a in enumerate(at):
                update = update + lax.dot_general(
                    kv_ref[pl.ds(a + SHARD, SHARD), :], pb[piece * SHARD:(piece + 1) * SHARD],
                    (((0,), (0,)), ((), ())), preferred_element_type=jnp.float32,
                )
            acc_sc[...] = update
            m_sc[...] = m_new

        def masked_body(kj, c):
            k_step(kj, True)
            return c

        def open_body(kj, c):
            k_step(kj, False)
            return c

        lax.fori_loop(tiles_ref[qi, 0], tiles_ref[qi, 1], masked_body, 0)
        lax.fori_loop(tiles_ref[qi, 1], tiles_ref[qi, 2], open_body, 0)
        lax.fori_loop(tiles_ref[qi, 2], tiles_ref[qi, 3], masked_body, 0)
        out = (acc_sc[...] / l_sc[...]).T.astype(o_ref.dtype)
        tokens = q_ref.shape[0]
        for g in range(heads):
            o_ref[:, pl.ds(pl.multiple_of((qi * heads + g) * HD, HD), HD)] = out[g * tokens:(g + 1) * tokens]
        return carry

    lax.fori_loop(0, n_q, q_body, 0)


def attend(q_rows, kv_all, qpos_rows, lo_rows, tiles, plane, slots):
    vmem = pltpu.MemorySpace.VMEM if hasattr(pltpu, "MemorySpace") else pltpu.VMEM
    return pl.pallas_call(
        functools.partial(attn_kernel, plane, slots),
        out_shape=jax.ShapeDtypeStruct(q_rows.shape, jnp.bfloat16),
        in_specs=[
            pl.BlockSpec(memory_space=pltpu.SMEM),
            pl.BlockSpec(memory_space=vmem),
            pl.BlockSpec(memory_space=vmem),
            pl.BlockSpec(memory_space=vmem),
            pl.BlockSpec(memory_space=vmem),
        ],
        out_specs=pl.BlockSpec(memory_space=vmem),
        scratch_shapes=[
            pltpu.VMEM((1, TQ), jnp.float32),
            pltpu.VMEM((1, TQ), jnp.float32),
            pltpu.VMEM((HD, TQ), jnp.float32),
        ],
    )(tiles, q_rows, kv_all, qpos_rows, lo_rows)


MESH_ID = pl.DeviceIdType.MESH


def window_kernel(depth, plane, n_ctx, need_col, k_ref, v_ref, win_ref, send1, recv1, send2, recv2, local_sem):
    me = lax.axis_index("ctx")
    h = lax.axis_index("head")
    z = me // plane
    r = me % plane
    n_z = n_ctx // plane
    mate = r + 1 - 2 * (r % 2)
    across = (r + 2) % plane
    far = across + 1 - 2 * (across % 2)
    barrier = pltpu.get_barrier_semaphore()

    @pl.when(z + 1 < n_z)
    def _():
        pl.semaphore_signal(barrier, 1, device_id=(me + plane, h), device_id_type=MESH_ID)

    @pl.when(z - 1 >= 0)
    def _():
        pl.semaphore_signal(barrier, 1, device_id=(me - plane, h), device_id_type=MESH_ID)

    for peer in (mate, across):
        pl.semaphore_signal(barrier, 1, device_id=(z * plane + peer, h), device_id_type=MESH_ID)
    pl.semaphore_wait(barrier, jnp.minimum(1, n_z - 1 - z) + jnp.minimum(1, z) + 2)
    local = [
        pltpu.make_async_copy(src, win_ref.at[r, depth, part], local_sem.at[part])
        for part, src in enumerate((k_ref, v_ref))
    ]
    for c in local:
        c.start()

    def wanted(d):
        return (d < depth) | (r >= need_col)

    def up(k):
        if k == 1:
            return [
                pltpu.make_async_remote_copy(
                    src_ref=src,
                    dst_ref=win_ref.at[r, depth - 1, part],
                    send_sem=send1.at[part * depth],
                    recv_sem=recv1.at[part * depth],
                    device_id=(me + plane, h),
                    device_id_type=MESH_ID,
                )
                for part, src in enumerate((k_ref, v_ref))
            ]
        return [pltpu.make_async_remote_copy(
            src_ref=win_ref.at[r, depth - k + 1],
            dst_ref=win_ref.at[r, depth - k],
            send_sem=send1.at[k - 1],
            recv_sem=recv1.at[k - 1],
            device_id=(me + plane, h),
            device_id_type=MESH_ID,
        )]

    def sends(k):
        return (z + 1 < n_z) & (z - (k - 1) >= 0) & wanted(k)

    def gets(k):
        return (z - k >= 0) & wanted(k)

    @pl.when(sends(1))
    def _():
        for c in up(1):
            c.start()

    def has(slot, col):
        return (z - (depth - slot) >= 0) & ((slot > 0) | (col >= need_col))

    def hop(idx, col, slot, to):
        return pltpu.make_async_remote_copy(
            src_ref=win_ref.at[col, slot],
            dst_ref=win_ref.at[col, slot],
            send_sem=send2.at[idx, slot],
            recv_sem=recv2.at[idx, slot],
            device_id=(z * plane + to, h),
            device_id_type=MESH_ID,
        )

    for c in local:
        c.wait()
    hop(0, r, depth, mate).start()
    hop(1, r, depth, across).start()
    for k in range(1, depth + 1):
        @pl.when(gets(k))
        def _():
            for c in up(k):
                c.wait_recv()
            hop(0, r, depth - k, mate).start()
            hop(1, r, depth - k, across).start()

        if k < depth:
            @pl.when(sends(k + 1))
            def _():
                for c in up(k + 1):
                    c.start()

    for k in range(1, depth + 1):
        @pl.when(sends(k))
        def _():
            for c in up(k):
                c.wait_send()

    for slot in range(depth, -1, -1):
        @pl.when(has(slot, across))
        def _():
            hop(1, across, slot, across).wait_recv()
            hop(2, across, slot, mate).start()

    for slot in range(depth + 1):
        @pl.when(has(slot, r))
        def _():
            hop(0, r, slot, mate).wait_send()
            hop(1, r, slot, across).wait_send()

        @pl.when(has(slot, across))
        def _():
            hop(2, across, slot, mate).wait_send()

        @pl.when(has(slot, mate))
        def _():
            hop(0, mate, slot, mate).wait_recv()

        @pl.when(has(slot, far))
        def _():
            hop(2, far, slot, mate).wait_recv()


def gather_window(key_rows, values, depth, plane, n_ctx, need_col):
    rows, width = key_rows.shape
    return pl.pallas_call(
        functools.partial(window_kernel, depth, plane, n_ctx, need_col),
        out_shape=jax.ShapeDtypeStruct((plane, depth + 1, 2, rows, width), key_rows.dtype),
        in_specs=[pl.BlockSpec(memory_space=pl.ANY)] * 2,
        out_specs=pl.BlockSpec(memory_space=pl.ANY),
        scratch_shapes=[
            pltpu.SemaphoreType.DMA((depth + 1,)),
            pltpu.SemaphoreType.DMA((depth + 1,)),
            pltpu.SemaphoreType.DMA((3, depth + 1)),
            pltpu.SemaphoreType.DMA((3, depth + 1)),
            pltpu.SemaphoreType.DMA((2,)),
        ],
        compiler_params=pltpu.CompilerParams(collective_id=0, has_side_effects=True),
    )(key_rows, values)


def project_kernel(n_head, att_ref, w_hbm, o_ref, w_buf, w_sem, send_buf, got, send_sem, recv_sem):
    me = lax.axis_index("head")
    row = lax.axis_index("ctx")
    cols = o_ref.shape[1]
    for d in list(range(1, n_head)) + [0]:
        pltpu.make_async_copy(
            w_hbm.at[:, pl.ds(pl.multiple_of(lax.rem(me + d, n_head) * cols, cols), cols)],
            w_buf.at[d], w_sem.at[d],
        ).start()
    barrier = pltpu.get_barrier_semaphore()
    for d in range(1, n_head):
        pl.semaphore_signal(
            barrier, 1, device_id=(row, lax.rem(me + d, n_head)), device_id_type=MESH_ID
        )
    pl.semaphore_wait(barrier, n_head - 1)

    def fetch(d):
        c0 = pl.multiple_of(lax.rem(me + d, n_head) * cols, cols)
        return pltpu.make_async_copy(w_hbm.at[:, pl.ds(c0, cols)], w_buf.at[d], w_sem.at[d])

    def part(d):
        fetch(d).wait()
        return jnp.dot(
            att_ref[...], w_buf[d], preferred_element_type=jnp.float32
        ).astype(jnp.bfloat16)

    def send(d):
        dst = lax.rem(me + d, n_head)
        return pltpu.make_async_remote_copy(
            src_ref=send_buf.at[d - 1],
            dst_ref=got.at[me],
            send_sem=send_sem.at[d - 1],
            recv_sem=recv_sem.at[d - 1],
            device_id=(row, dst),
            device_id_type=MESH_ID,
        )

    def arrival(d):
        src = lax.rem(me + n_head - d, n_head)
        return pltpu.make_async_remote_copy(
            src_ref=send_buf.at[d - 1],
            dst_ref=got.at[src],
            send_sem=send_sem.at[d - 1],
            recv_sem=recv_sem.at[d - 1],
            device_id=(row, src),
            device_id_type=MESH_ID,
        )

    send_buf[0] = part(1)
    for d in range(1, n_head):
        if d + 1 < n_head:
            send_buf[d] = part(d + 1)
        send(d).start()
    total = part(0).astype(jnp.float32)
    for d in range(1, n_head):
        send(d).wait_send()
        arrival(d).wait_recv()
        total = total + got[lax.rem(me + n_head - d, n_head)].astype(jnp.float32)
    o_ref[...] = total.astype(o_ref.dtype)


def project(att, out_weight, n_head):
    rows = att.shape[0]
    cols = out_weight.shape[1] // n_head
    vmem = pltpu.MemorySpace.VMEM if hasattr(pltpu, "MemorySpace") else pltpu.VMEM
    return pl.pallas_call(
        functools.partial(project_kernel, n_head),
        out_shape=jax.ShapeDtypeStruct((rows, cols), jnp.bfloat16),
        in_specs=[pl.BlockSpec(memory_space=vmem), pl.BlockSpec(memory_space=pl.ANY)],
        out_specs=pl.BlockSpec(memory_space=vmem),
        scratch_shapes=[
            pltpu.VMEM((n_head, out_weight.shape[0], cols), out_weight.dtype),
            pltpu.SemaphoreType.DMA((n_head,)),
            pltpu.VMEM((n_head - 1, rows, cols), jnp.bfloat16),
            pltpu.VMEM((n_head, rows, cols), jnp.bfloat16),
            pltpu.SemaphoreType.DMA((n_head - 1,)),
            pltpu.SemaphoreType.DMA((n_head - 1,)),
        ],
        compiler_params=pltpu.CompilerParams(collective_id=1, has_side_effects=True),
    )(att, out_weight)


def on_device(queries, key_rows, values, lengths, block_plan, inverse, mask_lo, out_weight):
    row_count, query_width = queries.shape
    group_size = query_width // HD
    here = lax.axis_index("ctx")
    first = here * row_count
    pos = first + jnp.arange(row_count, dtype=jnp.int32)
    doc_ends = jnp.cumsum(lengths).astype(jnp.int32)
    doc_start = jnp.max(jnp.where(doc_ends[None, :] <= pos[:, None], doc_ends[None, :], 0), axis=1)
    block_lo = lax.dynamic_slice_in_dim(mask_lo, here * (row_count // BLK), row_count // BLK)
    lo_tok = jnp.maximum(jnp.repeat(block_lo, BLK) * BLK, doc_start)
    qpos_rows = pos[None, :]
    lo_rows = lo_tok[None, :]
    n_q = row_count * group_size // TQ
    tile_lo = jnp.full((n_q,), jnp.min(lo_tok))
    tile_hi = jnp.full((n_q,), pos[-1])
    tile_lo_max = jnp.full((n_q,), jnp.max(lo_tok))
    tile_hi_min = jnp.full((n_q,), pos[0])

    n_ctx = lax.axis_size("ctx")
    plane = PLANE
    depth = min(n_ctx // plane - 1, -(-(LONGEST - 1) // (plane * row_count)))
    need_col = max(0, -(-(plane * row_count * depth - (LONGEST - 1) - (row_count - 1)) // row_count))
    need_col = need_col // (TK // SHARD) * (TK // SHARD)
    kv_win = gather_window(key_rows, values, depth, plane, n_ctx, need_col)
    kv_win = kv_win.reshape(-1, kv_win.shape[-1])
    base = (here // plane - depth) * plane * row_count
    span = kv_win.shape[0] // 2
    t0 = (tile_lo - base) // TK
    t3 = jnp.minimum((tile_hi - base) // TK + 1, span // TK)
    t1 = jnp.clip((tile_lo_max - base + TK - 1) // TK, t0, t3)
    t2 = jnp.clip((tile_hi_min - base + 1) // TK, t1, t3)
    tiles = jnp.stack([t0, t1, t2, t3], axis=1).astype(jnp.int32)
    att = attend(queries, kv_win, qpos_rows - base, lo_rows - base, tiles, plane, depth + 1)

    return project(att, out_weight, lax.axis_size("head"))


def solution(mesh):
    in_specs = (
        P("ctx", "head"),
        P("ctx", "head"),
        P("ctx", "head"),
        P(),
        P("ctx"),
        P(),
        P(),
        P("head", None),
    )
    out_specs = P("ctx", "head")
    return jax.shard_map(
        on_device, mesh=mesh, in_specs=in_specs, out_specs=out_specs, check_vma=False
    )
```

```python
import functools

import jax
import jax.numpy as jnp
from jax import lax
from jax.experimental import pallas as pl
from jax.experimental.pallas import tpu as pltpu
from jax.sharding import PartitionSpec as P

HD = 128
BLK = 8
TQ = 1024
TK = 512
SHARD = 256
NEG_FILL = -1e30
LONGEST = 4352
PLANE = 4


def attn_kernel(plane, slots, tiles_ref, q_ref, kv_ref, qpos_ref, lo_ref, o_ref, m_sc, l_sc, acc_sc):
    n_q = q_ref.shape[0] * q_ref.shape[1] // (HD * TQ)
    scale = HD ** (-0.5)

    def q_body(qi, carry):
        r0 = pl.multiple_of(qi * TQ, TQ)
        heads = TQ // q_ref.shape[0]
        q = jnp.concatenate([
            q_ref[:, pl.ds(pl.multiple_of((qi * heads + g) * HD, HD), HD)] for g in range(heads)
        ], axis=0)
        qpos = qpos_ref[:, pl.ds(r0, TQ)]
        lo = lo_ref[:, pl.ds(r0, TQ)]
        m_sc[...] = jnp.full(m_sc.shape, NEG_FILL, jnp.float32)
        l_sc[...] = jnp.zeros(l_sc.shape, jnp.float32)
        acc_sc[...] = jnp.zeros(acc_sc.shape, jnp.float32)

        def k_step(kj, masked):
            c0 = pl.multiple_of(kj * TK, TK)
            at = []
            for piece in range(TK // SHARD):
                i = kj * (TK // SHARD) + piece
                at.append(pl.multiple_of((lax.rem(i, plane) * slots + i // plane) * SHARD, SHARD))
            s = jnp.concatenate([
                lax.dot_general(
                    kv_ref[pl.ds(a, SHARD), pl.ds(0, HD)], q, (((1,), (1,)), ((), ())),
                    preferred_element_type=jnp.float32,
                )
                for a in at
            ], axis=0) * scale
            if masked:
                kpos = c0 + lax.broadcasted_iota(jnp.int32, (TK, TQ), 0)
                ok = (kpos >= lo) & (kpos <= qpos)
                s = jnp.where(ok, s, NEG_FILL)
            m_prev = m_sc[...]
            m_new = jnp.maximum(m_prev, jnp.max(s, axis=0, keepdims=True))
            p = jnp.exp(s - m_new)
            if masked:
                p = jnp.where(ok, p, 0.0)
            fade = jnp.exp(m_prev - m_new)
            l_sc[...] = l_sc[...] * fade + jnp.sum(p, axis=0, keepdims=True)
            pb = p.astype(jnp.bfloat16)
            update = acc_sc[...] * fade
            for piece, a in enumerate(at):
                update = update + lax.dot_general(
                    kv_ref[pl.ds(a, SHARD), pl.ds(HD, HD)], pb[piece * SHARD:(piece + 1) * SHARD],
                    (((0,), (0,)), ((), ())), preferred_element_type=jnp.float32,
                )
            acc_sc[...] = update
            m_sc[...] = m_new

        def masked_body(kj, c):
            k_step(kj, True)
            return c

        def open_body(kj, c):
            k_step(kj, False)
            return c

        lax.fori_loop(tiles_ref[qi, 0], tiles_ref[qi, 1], masked_body, 0)
        lax.fori_loop(tiles_ref[qi, 1], tiles_ref[qi, 2], open_body, 0)
        lax.fori_loop(tiles_ref[qi, 2], tiles_ref[qi, 3], masked_body, 0)
        out = (acc_sc[...] / l_sc[...]).T.astype(o_ref.dtype)
        tokens = q_ref.shape[0]
        for g in range(heads):
            o_ref[:, pl.ds(pl.multiple_of((qi * heads + g) * HD, HD), HD)] = out[g * tokens:(g + 1) * tokens]
        return carry

    lax.fori_loop(0, n_q, q_body, 0)


def attend(q_rows, kv_all, qpos_rows, lo_rows, tiles, plane, slots):
    vmem = pltpu.MemorySpace.VMEM if hasattr(pltpu, "MemorySpace") else pltpu.VMEM
    return pl.pallas_call(
        functools.partial(attn_kernel, plane, slots),
        out_shape=jax.ShapeDtypeStruct(q_rows.shape, jnp.bfloat16),
        in_specs=[
            pl.BlockSpec(memory_space=pltpu.SMEM),
            pl.BlockSpec(memory_space=vmem),
            pl.BlockSpec(memory_space=vmem),
            pl.BlockSpec(memory_space=vmem),
            pl.BlockSpec(memory_space=vmem),
        ],
        out_specs=pl.BlockSpec(memory_space=vmem),
        scratch_shapes=[
            pltpu.VMEM((1, TQ), jnp.float32),
            pltpu.VMEM((1, TQ), jnp.float32),
            pltpu.VMEM((HD, TQ), jnp.float32),
        ],
    )(tiles, q_rows, kv_all, qpos_rows, lo_rows)


MESH_ID = pl.DeviceIdType.MESH


def window_kernel(depth, plane, n_ctx, need_col, kv_ref, win_ref, send1, recv1, send2, recv2, local_sem):
    me = lax.axis_index("ctx")
    h = lax.axis_index("head")
    z = me // plane
    r = me % plane
    n_z = n_ctx // plane
    mate = r + 1 - 2 * (r % 2)
    across = (r + 2) % plane
    far = across + 1 - 2 * (across % 2)
    barrier = pltpu.get_barrier_semaphore()

    @pl.when(z + 1 < n_z)
    def _():
        pl.semaphore_signal(barrier, 1, device_id=(me + plane, h), device_id_type=MESH_ID)

    @pl.when(z - 1 >= 0)
    def _():
        pl.semaphore_signal(barrier, 1, device_id=(me - plane, h), device_id_type=MESH_ID)

    for peer in (mate, across):
        pl.semaphore_signal(barrier, 1, device_id=(z * plane + peer, h), device_id_type=MESH_ID)
    pl.semaphore_wait(barrier, jnp.minimum(1, n_z - 1 - z) + jnp.minimum(1, z) + 2)
    local = pltpu.make_async_copy(kv_ref, win_ref.at[r, depth], local_sem)
    local.start()

    def wanted(d):
        return (d < depth) | (r >= need_col)

    def up(k):
        return pltpu.make_async_remote_copy(
            src_ref=kv_ref if k == 1 else win_ref.at[r, depth - k + 1],
            dst_ref=win_ref.at[r, depth - k],
            send_sem=send1.at[k - 1],
            recv_sem=recv1.at[k - 1],
            device_id=(me + plane, h),
            device_id_type=MESH_ID,
        )

    def sends(k):
        return (z + 1 < n_z) & (z - (k - 1) >= 0) & wanted(k)

    def gets(k):
        return (z - k >= 0) & wanted(k)

    @pl.when(sends(1))
    def _():
        up(1).start()

    def has(slot, col):
        return (z - (depth - slot) >= 0) & ((slot > 0) | (col >= need_col))

    def hop(idx, col, slot, to):
        return pltpu.make_async_remote_copy(
            src_ref=win_ref.at[col, slot],
            dst_ref=win_ref.at[col, slot],
            send_sem=send2.at[idx, slot],
            recv_sem=recv2.at[idx, slot],
            device_id=(z * plane + to, h),
            device_id_type=MESH_ID,
        )

    local.wait()
    hop(0, r, depth, mate).start()
    hop(1, r, depth, across).start()
    for k in range(1, depth + 1):
        @pl.when(gets(k))
        def _():
            up(k).wait_recv()
            hop(0, r, depth - k, mate).start()
            hop(1, r, depth - k, across).start()

        if k < depth:
            @pl.when(sends(k + 1))
            def _():
                up(k + 1).start()

    for k in range(1, depth + 1):
        @pl.when(sends(k))
        def _():
            up(k).wait_send()

    for slot in range(depth, -1, -1):
        @pl.when(has(slot, across))
        def _():
            hop(1, across, slot, across).wait_recv()
            hop(2, across, slot, mate).start()

    for slot in range(depth + 1):
        @pl.when(has(slot, r))
        def _():
            hop(0, r, slot, mate).wait_send()
            hop(1, r, slot, across).wait_send()

        @pl.when(has(slot, across))
        def _():
            hop(2, across, slot, mate).wait_send()

        @pl.when(has(slot, mate))
        def _():
            hop(0, mate, slot, mate).wait_recv()

        @pl.when(has(slot, far))
        def _():
            hop(2, far, slot, mate).wait_recv()


def gather_window(kv_local, depth, plane, n_ctx, need_col):
    rows, width = kv_local.shape
    return pl.pallas_call(
        functools.partial(window_kernel, depth, plane, n_ctx, need_col),
        out_shape=jax.ShapeDtypeStruct((plane, depth + 1, rows, width), kv_local.dtype),
        in_specs=[pl.BlockSpec(memory_space=pl.ANY)],
        out_specs=pl.BlockSpec(memory_space=pl.ANY),
        scratch_shapes=[
            pltpu.SemaphoreType.DMA((depth,)),
            pltpu.SemaphoreType.DMA((depth,)),
            pltpu.SemaphoreType.DMA((3, depth + 1)),
            pltpu.SemaphoreType.DMA((3, depth + 1)),
            pltpu.SemaphoreType.DMA(()),
        ],
        compiler_params=pltpu.CompilerParams(collective_id=0, has_side_effects=True),
    )(kv_local)


def project_kernel(n_head, att_ref, w_hbm, o_ref, w_buf, w_sem, send_buf, got, send_sem, recv_sem):
    me = lax.axis_index("head")
    row = lax.axis_index("ctx")
    cols = o_ref.shape[1]
    for d in list(range(1, n_head, 2)) + list(range(2, n_head, 2)) + [0]:
        pltpu.make_async_copy(
            w_hbm.at[:, pl.ds(pl.multiple_of(lax.rem(me + d, n_head) * cols, cols), cols)],
            w_buf.at[d], w_sem.at[d],
        ).start()
    barrier = pltpu.get_barrier_semaphore()
    for d in range(1, n_head):
        pl.semaphore_signal(
            barrier, 1, device_id=(row, lax.rem(me + d, n_head)), device_id_type=MESH_ID
        )
    pl.semaphore_wait(barrier, n_head - 1)

    def fetch(d):
        c0 = pl.multiple_of(lax.rem(me + d, n_head) * cols, cols)
        return pltpu.make_async_copy(w_hbm.at[:, pl.ds(c0, cols)], w_buf.at[d], w_sem.at[d])

    def part(d):
        fetch(d).wait()
        return jnp.dot(
            att_ref[...], w_buf[d], preferred_element_type=jnp.float32
        ).astype(jnp.bfloat16)

    def send(d):
        dst = lax.rem(me + d, n_head)
        return pltpu.make_async_remote_copy(
            src_ref=send_buf.at[d - 1],
            dst_ref=got.at[me],
            send_sem=send_sem.at[d - 1],
            recv_sem=recv_sem.at[d - 1],
            device_id=(row, dst),
            device_id_type=MESH_ID,
        )

    def arrival(d):
        src = lax.rem(me + n_head - d, n_head)
        return pltpu.make_async_remote_copy(
            src_ref=send_buf.at[d - 1],
            dst_ref=got.at[src],
            send_sem=send_sem.at[d - 1],
            recv_sem=recv_sem.at[d - 1],
            device_id=(row, src),
            device_id_type=MESH_ID,
        )

    order = list(range(1, n_head, 2)) + list(range(2, n_head, 2))
    send_buf[order[0] - 1] = part(order[0])
    for i, d in enumerate(order):
        if i + 1 < len(order):
            send_buf[order[i + 1] - 1] = part(order[i + 1])
        send(d).start()
    total = part(0).astype(jnp.float32)
    for d in range(1, n_head):
        send(d).wait_send()
        arrival(d).wait_recv()
        total = total + got[lax.rem(me + n_head - d, n_head)].astype(jnp.float32)
    o_ref[...] = total.astype(o_ref.dtype)


def project(att, out_weight, n_head):
    rows = att.shape[0]
    cols = out_weight.shape[1] // n_head
    vmem = pltpu.MemorySpace.VMEM if hasattr(pltpu, "MemorySpace") else pltpu.VMEM
    return pl.pallas_call(
        functools.partial(project_kernel, n_head),
        out_shape=jax.ShapeDtypeStruct((rows, cols), jnp.bfloat16),
        in_specs=[pl.BlockSpec(memory_space=vmem), pl.BlockSpec(memory_space=pl.ANY)],
        out_specs=pl.BlockSpec(memory_space=vmem),
        scratch_shapes=[
            pltpu.VMEM((n_head, out_weight.shape[0], cols), out_weight.dtype),
            pltpu.SemaphoreType.DMA((n_head,)),
            pltpu.VMEM((n_head - 1, rows, cols), jnp.bfloat16),
            pltpu.VMEM((n_head, rows, cols), jnp.bfloat16),
            pltpu.SemaphoreType.DMA((n_head - 1,)),
            pltpu.SemaphoreType.DMA((n_head - 1,)),
        ],
        compiler_params=pltpu.CompilerParams(collective_id=1, has_side_effects=True),
    )(att, out_weight)


def on_device(queries, key_rows, values, lengths, block_plan, inverse, mask_lo, out_weight):
    row_count, query_width = queries.shape
    group_size = query_width // HD
    here = lax.axis_index("ctx")
    first = here * row_count
    pos = first + jnp.arange(row_count, dtype=jnp.int32)
    doc_ends = jnp.cumsum(lengths).astype(jnp.int32)
    doc_start = jnp.max(jnp.where(doc_ends[None, :] <= pos[:, None], doc_ends[None, :], 0), axis=1)
    block_lo = lax.dynamic_slice_in_dim(mask_lo, here * (row_count // BLK), row_count // BLK)
    lo_tok = jnp.maximum(jnp.repeat(block_lo, BLK) * BLK, doc_start)
    qpos_rows = jnp.tile(pos, group_size)[None, :]
    lo_rows = jnp.tile(lo_tok, group_size)[None, :]
    n_q = row_count * group_size // TQ
    tile_lo = jnp.full((n_q,), jnp.min(lo_tok))
    tile_hi = jnp.full((n_q,), pos[-1])
    tile_lo_max = jnp.full((n_q,), jnp.max(lo_tok))
    tile_hi_min = jnp.full((n_q,), pos[0])

    kv_local = jnp.concatenate([key_rows, values], axis=1)
    n_ctx = lax.axis_size("ctx")
    plane = PLANE
    depth = min(n_ctx // plane - 1, -(-(LONGEST - 1) // (plane * row_count)))
    need_col = max(0, -(-(plane * row_count * depth - (LONGEST - 1) - (row_count - 1)) // row_count))
    need_col = need_col // (TK // SHARD) * (TK // SHARD)
    kv_win = gather_window(kv_local, depth, plane, n_ctx, need_col)
    kv_win = kv_win.reshape(-1, kv_win.shape[-1])
    base = (here // plane - depth) * plane * row_count
    span = kv_win.shape[0]
    t0 = (tile_lo - base) // TK
    t3 = jnp.minimum((tile_hi - base) // TK + 1, span // TK)
    t1 = jnp.clip((tile_lo_max - base + TK - 1) // TK, t0, t3)
    t2 = jnp.clip((tile_hi_min - base + 1) // TK, t1, t3)
    tiles = jnp.stack([t0, t1, t2, t3], axis=1).astype(jnp.int32)
    att = attend(queries, kv_win, qpos_rows - base, lo_rows - base, tiles, plane, depth + 1)

    return project(att, out_weight, lax.axis_size("head"))


def solution(mesh):
    in_specs = (
        P("ctx", "head"),
        P("ctx", "head"),
        P("ctx", "head"),
        P(),
        P("ctx"),
        P(),
        P(),
        P("head", None),
    )
    out_specs = P("ctx", "head")
    return jax.shard_map(
        on_device, mesh=mesh, in_specs=in_specs, out_specs=out_specs, check_vma=False
    )
```

```python
import functools

import jax
import jax.numpy as jnp
from jax import lax
from jax.experimental import pallas as pl
from jax.experimental.pallas import tpu as pltpu
from jax.sharding import PartitionSpec as P

HD = 128
BLK = 8
TQ = 1024
TK = 512
SHARD = 256
NEG_FILL = -1e30
LONGEST = 4352
PLANE = 4


def attn_kernel(plane, slots, tiles_ref, q_ref, kv_ref, qpos_ref, lo_ref, o_ref, m_sc, l_sc, acc_sc):
    n_q = q_ref.shape[0] * q_ref.shape[1] // (HD * TQ)
    scale = HD ** (-0.5)

    def q_body(qi, carry):
        r0 = pl.multiple_of(qi * TQ, TQ)
        heads = TQ // q_ref.shape[0]
        q = jnp.concatenate([
            q_ref[:, pl.ds(pl.multiple_of((qi * heads + g) * HD, HD), HD)] for g in range(heads)
        ], axis=0)
        qpos = qpos_ref[:, pl.ds(r0, TQ)]
        lo = lo_ref[:, pl.ds(r0, TQ)]
        m_sc[...] = jnp.full(m_sc.shape, NEG_FILL, jnp.float32)
        l_sc[...] = jnp.zeros(l_sc.shape, jnp.float32)
        acc_sc[...] = jnp.zeros(acc_sc.shape, jnp.float32)

        def k_step(kj, masked):
            c0 = pl.multiple_of(kj * TK, TK)
            at = []
            for piece in range(TK // SHARD):
                i = kj * (TK // SHARD) + piece
                at.append(pl.multiple_of((lax.rem(i, plane) * slots + i // plane) * SHARD, SHARD))
            s = jnp.concatenate([
                lax.dot_general(
                    kv_ref[pl.ds(a, SHARD), pl.ds(0, HD)], q, (((1,), (1,)), ((), ())),
                    preferred_element_type=jnp.float32,
                )
                for a in at
            ], axis=0) * scale
            if masked:
                kpos = c0 + lax.broadcasted_iota(jnp.int32, (TK, TQ), 0)
                ok = (kpos >= lo) & (kpos <= qpos)
                s = jnp.where(ok, s, NEG_FILL)
            m_prev = m_sc[...]
            m_new = jnp.maximum(m_prev, jnp.max(s, axis=0, keepdims=True))
            p = jnp.exp(s - m_new)
            fade = jnp.exp(m_prev - m_new)
            l_sc[...] = l_sc[...] * fade + jnp.sum(p, axis=0, keepdims=True)
            pb = p.astype(jnp.bfloat16)
            update = acc_sc[...] * fade
            for piece, a in enumerate(at):
                update = update + lax.dot_general(
                    kv_ref[pl.ds(a, SHARD), pl.ds(HD, HD)], pb[piece * SHARD:(piece + 1) * SHARD],
                    (((0,), (0,)), ((), ())), preferred_element_type=jnp.float32,
                )
            acc_sc[...] = update
            m_sc[...] = m_new

        def masked_body(kj, c):
            k_step(kj, True)
            return c

        def open_body(kj, c):
            k_step(kj, False)
            return c

        lax.fori_loop(tiles_ref[qi, 0], tiles_ref[qi, 1], masked_body, 0)
        lax.fori_loop(tiles_ref[qi, 1], tiles_ref[qi, 2], open_body, 0)
        lax.fori_loop(tiles_ref[qi, 2], tiles_ref[qi, 3], masked_body, 0)
        out = (acc_sc[...] / l_sc[...]).T.astype(o_ref.dtype)
        tokens = q_ref.shape[0]
        for g in range(heads):
            o_ref[:, pl.ds(pl.multiple_of((qi * heads + g) * HD, HD), HD)] = out[g * tokens:(g + 1) * tokens]
        return carry

    lax.fori_loop(0, n_q, q_body, 0)


def attend(q_rows, kv_all, qpos_rows, lo_rows, tiles, plane, slots):
    vmem = pltpu.MemorySpace.VMEM if hasattr(pltpu, "MemorySpace") else pltpu.VMEM
    return pl.pallas_call(
        functools.partial(attn_kernel, plane, slots),
        out_shape=jax.ShapeDtypeStruct(q_rows.shape, jnp.bfloat16),
        in_specs=[
            pl.BlockSpec(memory_space=pltpu.SMEM),
            pl.BlockSpec(memory_space=vmem),
            pl.BlockSpec(memory_space=vmem),
            pl.BlockSpec(memory_space=vmem),
            pl.BlockSpec(memory_space=vmem),
        ],
        out_specs=pl.BlockSpec(memory_space=vmem),
        scratch_shapes=[
            pltpu.VMEM((1, TQ), jnp.float32),
            pltpu.VMEM((1, TQ), jnp.float32),
            pltpu.VMEM((HD, TQ), jnp.float32),
        ],
    )(tiles, q_rows, kv_all, qpos_rows, lo_rows)


MESH_ID = pl.DeviceIdType.MESH


def window_kernel(depth, plane, n_ctx, need_col, kv_ref, win_ref, send1, recv1, send2, recv2, local_sem):
    me = lax.axis_index("ctx")
    h = lax.axis_index("head")
    z = me // plane
    r = me % plane
    n_z = n_ctx // plane
    mate = r + 1 - 2 * (r % 2)
    across = (r + 2) % plane
    far = across + 1 - 2 * (across % 2)
    barrier = pltpu.get_barrier_semaphore()

    @pl.when(z + 1 < n_z)
    def _():
        pl.semaphore_signal(barrier, 1, device_id=(me + plane, h), device_id_type=MESH_ID)

    @pl.when(z - 1 >= 0)
    def _():
        pl.semaphore_signal(barrier, 1, device_id=(me - plane, h), device_id_type=MESH_ID)

    for peer in (mate, across):
        pl.semaphore_signal(barrier, 1, device_id=(z * plane + peer, h), device_id_type=MESH_ID)
    pl.semaphore_wait(barrier, jnp.minimum(1, n_z - 1 - z) + jnp.minimum(1, z) + 2)
    local = pltpu.make_async_copy(kv_ref, win_ref.at[r, depth], local_sem)
    local.start()

    def wanted(d):
        return (d < depth) | (r >= need_col)

    def up(k):
        return pltpu.make_async_remote_copy(
            src_ref=kv_ref if k == 1 else win_ref.at[r, depth - k + 1],
            dst_ref=win_ref.at[r, depth - k],
            send_sem=send1.at[k - 1],
            recv_sem=recv1.at[k - 1],
            device_id=(me + plane, h),
            device_id_type=MESH_ID,
        )

    def sends(k):
        return (z + 1 < n_z) & (z - (k - 1) >= 0) & wanted(k)

    def gets(k):
        return (z - k >= 0) & wanted(k)

    @pl.when(sends(1))
    def _():
        up(1).start()

    def has(slot, col):
        return (z - (depth - slot) >= 0) & ((slot > 0) | (col >= need_col))

    def hop(idx, col, slot, to):
        return pltpu.make_async_remote_copy(
            src_ref=win_ref.at[col, slot],
            dst_ref=win_ref.at[col, slot],
            send_sem=send2.at[idx, slot],
            recv_sem=recv2.at[idx, slot],
            device_id=(z * plane + to, h),
            device_id_type=MESH_ID,
        )

    local.wait()
    hop(0, r, depth, mate).start()
    hop(1, r, depth, across).start()
    for k in range(1, depth + 1):
        @pl.when(gets(k))
        def _():
            up(k).wait_recv()
            hop(0, r, depth - k, mate).start()
            hop(1, r, depth - k, across).start()

        if k < depth:
            @pl.when(sends(k + 1))
            def _():
                up(k + 1).start()

    for k in range(1, depth + 1):
        @pl.when(sends(k))
        def _():
            up(k).wait_send()

    for slot in range(depth, -1, -1):
        @pl.when(has(slot, across))
        def _():
            hop(1, across, slot, across).wait_recv()
            hop(2, across, slot, mate).start()

    for slot in range(depth + 1):
        @pl.when(has(slot, r))
        def _():
            hop(0, r, slot, mate).wait_send()
            hop(1, r, slot, across).wait_send()

        @pl.when(has(slot, across))
        def _():
            hop(2, across, slot, mate).wait_send()

        @pl.when(has(slot, mate))
        def _():
            hop(0, mate, slot, mate).wait_recv()

        @pl.when(has(slot, far))
        def _():
            hop(2, far, slot, mate).wait_recv()


def gather_window(kv_local, depth, plane, n_ctx, need_col):
    rows, width = kv_local.shape
    return pl.pallas_call(
        functools.partial(window_kernel, depth, plane, n_ctx, need_col),
        out_shape=jax.ShapeDtypeStruct((plane, depth + 1, rows, width), kv_local.dtype),
        in_specs=[pl.BlockSpec(memory_space=pl.ANY)],
        out_specs=pl.BlockSpec(memory_space=pl.ANY),
        scratch_shapes=[
            pltpu.SemaphoreType.DMA((depth,)),
            pltpu.SemaphoreType.DMA((depth,)),
            pltpu.SemaphoreType.DMA((3, depth + 1)),
            pltpu.SemaphoreType.DMA((3, depth + 1)),
            pltpu.SemaphoreType.DMA(()),
        ],
        compiler_params=pltpu.CompilerParams(collective_id=0, has_side_effects=True),
    )(kv_local)


def project_kernel(n_head, att_ref, w_hbm, o_ref, w_buf, w_sem, send_buf, got, send_sem, recv_sem):
    me = lax.axis_index("head")
    row = lax.axis_index("ctx")
    cols = o_ref.shape[1]
    for d in list(range(1, n_head)) + [0]:
        pltpu.make_async_copy(
            w_hbm.at[:, pl.ds(pl.multiple_of(lax.rem(me + d, n_head) * cols, cols), cols)],
            w_buf.at[d], w_sem.at[d],
        ).start()
    barrier = pltpu.get_barrier_semaphore()
    for d in range(1, n_head):
        pl.semaphore_signal(
            barrier, 1, device_id=(row, lax.rem(me + d, n_head)), device_id_type=MESH_ID
        )
    pl.semaphore_wait(barrier, n_head - 1)

    def fetch(d):
        c0 = pl.multiple_of(lax.rem(me + d, n_head) * cols, cols)
        return pltpu.make_async_copy(w_hbm.at[:, pl.ds(c0, cols)], w_buf.at[d], w_sem.at[d])

    def part(d):
        fetch(d).wait()
        return jnp.dot(
            att_ref[...], w_buf[d], preferred_element_type=jnp.float32
        ).astype(jnp.bfloat16)

    def send(d):
        dst = lax.rem(me + d, n_head)
        return pltpu.make_async_remote_copy(
            src_ref=send_buf.at[d - 1],
            dst_ref=got.at[me],
            send_sem=send_sem.at[d - 1],
            recv_sem=recv_sem.at[d - 1],
            device_id=(row, dst),
            device_id_type=MESH_ID,
        )

    def arrival(d):
        src = lax.rem(me + n_head - d, n_head)
        return pltpu.make_async_remote_copy(
            src_ref=send_buf.at[d - 1],
            dst_ref=got.at[src],
            send_sem=send_sem.at[d - 1],
            recv_sem=recv_sem.at[d - 1],
            device_id=(row, src),
            device_id_type=MESH_ID,
        )

    send_buf[0] = part(1)
    for d in range(1, n_head):
        if d + 1 < n_head:
            send_buf[d] = part(d + 1)
        send(d).start()
    total = part(0).astype(jnp.float32)
    for d in range(1, n_head):
        send(d).wait_send()
        arrival(d).wait_recv()
        total = total + got[lax.rem(me + n_head - d, n_head)].astype(jnp.float32)
    o_ref[...] = total.astype(o_ref.dtype)


def project(att, out_weight, n_head):
    rows = att.shape[0]
    cols = out_weight.shape[1] // n_head
    vmem = pltpu.MemorySpace.VMEM if hasattr(pltpu, "MemorySpace") else pltpu.VMEM
    return pl.pallas_call(
        functools.partial(project_kernel, n_head),
        out_shape=jax.ShapeDtypeStruct((rows, cols), jnp.bfloat16),
        in_specs=[pl.BlockSpec(memory_space=vmem), pl.BlockSpec(memory_space=pl.ANY)],
        out_specs=pl.BlockSpec(memory_space=vmem),
        scratch_shapes=[
            pltpu.VMEM((n_head, out_weight.shape[0], cols), out_weight.dtype),
            pltpu.SemaphoreType.DMA((n_head,)),
            pltpu.VMEM((n_head - 1, rows, cols), jnp.bfloat16),
            pltpu.VMEM((n_head, rows, cols), jnp.bfloat16),
            pltpu.SemaphoreType.DMA((n_head - 1,)),
            pltpu.SemaphoreType.DMA((n_head - 1,)),
        ],
        compiler_params=pltpu.CompilerParams(collective_id=1, has_side_effects=True),
    )(att, out_weight)


def on_device(queries, key_rows, values, lengths, block_plan, inverse, mask_lo, out_weight):
    row_count, query_width = queries.shape
    group_size = query_width // HD
    here = lax.axis_index("ctx")
    first = here * row_count
    pos = first + jnp.arange(row_count, dtype=jnp.int32)
    doc_ends = jnp.cumsum(lengths).astype(jnp.int32)
    doc_start = jnp.max(jnp.where(doc_ends[None, :] <= pos[:, None], doc_ends[None, :], 0), axis=1)
    block_lo = lax.dynamic_slice_in_dim(mask_lo, here * (row_count // BLK), row_count // BLK)
    lo_tok = jnp.maximum(jnp.repeat(block_lo, BLK) * BLK, doc_start)
    qpos_rows = jnp.tile(pos, group_size)[None, :]
    lo_rows = jnp.tile(lo_tok, group_size)[None, :]
    n_q = row_count * group_size // TQ
    tile_lo = jnp.full((n_q,), jnp.min(lo_tok))
    tile_hi = jnp.full((n_q,), pos[-1])
    tile_lo_max = jnp.full((n_q,), jnp.max(lo_tok))
    tile_hi_min = jnp.full((n_q,), pos[0])

    kv_local = jnp.concatenate([key_rows, values], axis=1)
    n_ctx = lax.axis_size("ctx")
    plane = PLANE
    depth = min(n_ctx // plane - 1, -(-(LONGEST - 1) // (plane * row_count)))
    need_col = max(0, -(-(plane * row_count * depth - (LONGEST - 1) - (row_count - 1)) // row_count))
    need_col = need_col // (TK // SHARD) * (TK // SHARD)
    kv_win = gather_window(kv_local, depth, plane, n_ctx, need_col)
    kv_win = kv_win.reshape(-1, kv_win.shape[-1])
    base = (here // plane - depth) * plane * row_count
    span = kv_win.shape[0]
    t0 = (tile_lo - base) // TK
    t3 = jnp.minimum((tile_hi - base) // TK + 1, span // TK)
    t1 = jnp.clip((tile_lo_max - base + TK - 1) // TK, t0, t3)
    t2 = jnp.clip((tile_hi_min - base + 1) // TK, t1, t3)
    tiles = jnp.stack([t0, t1, t2, t3], axis=1).astype(jnp.int32)
    att = attend(queries, kv_win, qpos_rows - base, lo_rows - base, tiles, plane, depth + 1)

    return project(att, out_weight, lax.axis_size("head"))


def solution(mesh):
    in_specs = (
        P("ctx", "head"),
        P("ctx", "head"),
        P("ctx", "head"),
        P(),
        P("ctx"),
        P(),
        P(),
        P("head", None),
    )
    out_specs = P("ctx", "head")
    return jax.shard_map(
        on_device, mesh=mesh, in_specs=in_specs, out_specs=out_specs, check_vma=False
    )
```
